32 devices in a mesh: dp: 8 (over y, x, core), tensor: 4 (over z).
Axes of the slice: x: 2, y: 2, z: 4, core: 2. Of those that a mesh axis runs over, the one named last changes fastest.
Arguments:
- hidden_in: bfloat16 [8, 1024, 2048], P('dp', 'tensor'), may hold values from -6 to 6
- cotangent: bfloat16 [8, 1024, 2048], P('dp', 'tensor'), may hold values from -6 to 6
- lengths: int32 [8], replicated, may hold values from 1 to 1024, 5632 in all
- slot_of_seq: int32 [8], replicated, may hold values from 0 to 7, as said below
- seq_of_slot: int32 [8], replicated, may hold values from 0 to 7, as said below
- qkv_weight: bfloat16 [2048, 3, 2048], P('dp', None, 'tensor'), may hold values from -0.125 to 0.125
- out_weight: bfloat16 [2048, 2048], P('dp', 'tensor'), may hold values from -0.75 to 0.75
- fc1_weight: bfloat16 [2048, 8192], P('dp', 'tensor'), may hold values from -0.125 to 0.125
- fc2_weight: bfloat16 [2048, 8192], P('dp', 'tensor'), may hold values from -0.0625 to 0.0625
- ln_gain: bfloat16 [2048], P(('dp', 'tensor')), may hold values from 0.5 to 1.5
- ln_bias: bfloat16 [2048], P(('dp', 'tensor')), may hold values from -3 to 3
- qkv_bias: bfloat16 [6144], P(('dp', 'tensor')), may hold values from -3 to 3
- out_bias: bfloat16 [2048], P(('dp', 'tensor')), may hold values from -3 to 3
- fc1_bias: bfloat16 [8192], P(('dp', 'tensor')), may hold values from -3 to 3
- fc2_bias: bfloat16 [2048], P(('dp', 'tensor')), may hold values from -3 to 3
Outputs:
- block_out: bfloat16 [8, 1024, 2048], P('dp', 'tensor')
- grad_input: bfloat16 [8, 1024, 2048], P('dp', 'tensor')
- grad_qkv_weight: float32 [2048, 3, 2048], P('dp', None, 'tensor')
- grad_out_weight: float32 [2048, 2048], P('dp', 'tensor')
- grad_fc1_weight: float32 [2048, 8192], P('dp', 'tensor')
- grad_fc2_weight: float32 [2048, 8192], P('dp', 'tensor')
- grad_ln_gain: float32 [2048], P(('dp', 'tensor'))
- grad_ln_bias: float32 [2048], P(('dp', 'tensor'))
- grad_qkv_bias: float32 [6144], P(('dp', 'tensor'))
- grad_out_bias: float32 [2048], P(('dp', 'tensor'))
- grad_fc1_bias: float32 [8192], P(('dp', 'tensor'))
- grad_fc2_bias: float32 [2048], P(('dp', 'tensor'))
The draws below stay inside these ranges and needn't reach their ends.
Inputs may be any that keep to these rules, and one draw needn't show every extreme that they name: 8 lengths that sum to 5632, the longest exactly 1024; sequence s fills positions 0 to lengths[s] - 1. A permutation: sequence s is computed in slot slot_of_seq[s]; slot p lies on index p // 1 of dp. `seq_of_slot`: the inverse permutation of slot_of_seq.
All inputs are finite; a program needn't handle non-finite values.
Results may differ from the reference program's by a relative error of at most 0.0086.
Values may be sent and summed in bfloat16 or wider, within the bound.
No kernel may reach another device: no remote copies, remote signals or barrier semaphores. Data moves between devices by JAX's collectives and lax.ppermute only.
A program may use at most 256 MiB of HBM per device.

```python
import math
import jax
import jax.numpy as jnp
import numpy as np
from jax import lax

D = 2048
HEADS = 32
HEAD_DIM = 64
ROT = 32
FF = 8192
LMAX = 1024
NSEQ = 8
TOTAL = 5632


def deal_order(key):
    return jax.random.permutation(jax.random.fold_in(key, 11), NSEQ).astype(jnp.int32)


def draw_slot_of_seq(key, part):
    return deal_order(key)


def draw_seq_of_slot(key, part):
    return jnp.argsort(deal_order(key)).astype(jnp.int32)


def block_levels(rng, shape, cuts, smallest, largest):
    level, own = 1.0, jax.random.fold_in(rng, 6)
    for dim, parts in cuts:
        steps = jnp.exp(jax.random.uniform(jax.random.fold_in(own, dim), (parts,), jnp.float32, smallest / len(cuts), largest / len(cuts)))
        level = level * jnp.repeat(steps, shape[dim] // parts).reshape([-1 if axis == dim else 1 for axis in range(len(shape))])
    return level


def profile(amount, total, reach, lean):
    portions = [(1 << 20) // math.isqrt(standing ** lean) + 1 for standing in range(2, amount + 1)]
    surplus, given = total - reach - (amount - 1), [1] * (amount - 1)
    while surplus > 0:
        movable = [i for i in range(amount - 1) if given[i] < reach]
        mass, budget = sum([portions[i] for i in movable]), surplus
        for i in movable:
            addition = min(reach - given[i], max(1, budget * portions[i] // mass), surplus)
            given[i] = given[i] + addition
            surplus = surplus - addition
    return np.array([reach] + given)


def uneven_parts(own_key, number_of, total, bound, lean):
    if number_of == 2:
        one = jax.random.randint(own_key, (), max(1, total - bound), min(bound, total - 1) + 1)
        return jnp.stack([one, total - one])
    sizes = jnp.asarray(profile(number_of, total, bound, lean), jnp.int32)
    pairs = (number_of - 1) // 2
    giver, receiver = sizes[1:1 + 2 * pairs:2], sizes[2:2 + 2 * pairs:2]
    margin = jnp.minimum(giver - 1, bound - receiver)
    moved = jax.random.randint(jax.random.fold_in(own_key, 1), (pairs,), 0, 1 << 20) % (margin + 1)
    sizes = sizes.at[1:1 + 2 * pairs:2].set(giver - moved).at[2:2 + 2 * pairs:2].set(receiver + moved)
    return sizes[jax.random.permutation(jax.random.fold_in(own_key, 2), number_of)]


def normal_values(stream_key, extent, width, bound, split=(), dtype=jnp.bfloat16):
    entries = width * jax.random.normal(stream_key, extent, jnp.float32)
    if split:
        entries = entries * block_levels(stream_key, extent, split, -0.22, 0.18)
    return jnp.clip(entries, -bound, bound).astype(dtype)


def setup_inputs(seed: int = 0) -> dict:
    key_list = jax.random.split(jax.random.key(seed), 16)
    hidden_in = normal_values(key_list[0], (NSEQ, LMAX, D), 1.0, 6.0, ((0, 8), (1, 4)))
    cotangent = normal_values(key_list[1], (NSEQ, LMAX, D), 1.0, 6.0, ((0, 8), (1, 4)))
    lengths = uneven_parts(key_list[2], NSEQ, TOTAL, LMAX, 1).astype(jnp.int32)
    slot_of_seq = draw_slot_of_seq(jax.random.fold_in(key_list[15], 71), 0)
    seq_of_slot = draw_seq_of_slot(jax.random.fold_in(key_list[15], 71), 0)
    qkv_weight = normal_values(key_list[5], (D, 3, D), D ** -0.5, 0.125, ((0, 8), (2, 4)))
    out_weight = normal_values(key_list[6], (D, D), 64 ** -0.5, 0.75, ((0, 8), (1, 4)))
    fc1_weight = normal_values(key_list[7], (D, FF), D ** -0.5, 0.125, ((0, 8), (1, 4)))
    fc2_weight = normal_values(key_list[8], (D, FF), FF ** -0.5, 0.0625, ((0, 8), (1, 4)))
    ln_gain = jnp.clip(1.0 + 0.1 * jax.random.normal(key_list[9], (D,), jnp.float32), 0.5, 1.5).astype(jnp.bfloat16)
    ln_bias = normal_values(key_list[10], (D,), 0.3, 3.0, ((0, 32),))
    qkv_bias = normal_values(key_list[11], (3 * D,), 0.3, 3.0, ((0, 32),))
    out_bias = normal_values(key_list[12], (D,), 0.3, 3.0, ((0, 32),))
    fc1_bias = normal_values(key_list[13], (FF,), 0.3, 3.0, ((0, 32),))
    fc2_bias = normal_values(key_list[14], (D,), 0.3, 3.0, ((0, 32),))
    return dict(hidden_in=hidden_in, cotangent=cotangent, lengths=lengths, slot_of_seq=slot_of_seq, seq_of_slot=seq_of_slot, qkv_weight=qkv_weight, out_weight=out_weight, fc1_weight=fc1_weight, fc2_weight=fc2_weight, ln_gain=ln_gain, ln_bias=ln_bias, qkv_bias=qkv_bias, out_bias=out_bias, fc1_bias=fc1_bias, fc2_bias=fc2_bias)


@jax.custom_vjp
def low(v):
    return lax.optimization_barrier(v.astype(jnp.bfloat16)).astype(jnp.float32)

@jax.custom_vjp
def low_back(v):
    return v

def low_keep(v):
    return (low(v), None)

def low_pass(kept, grad):
    return (grad,)

def back_keep(v):
    return (v, None)

def back_low(kept, grad):
    return (low(grad),)
low.defvjp(low_keep, low_pass)
low_back.defvjp(back_keep, back_low)
eps = 1e-05
masked_score = -1e+30
highest = lax.Precision.HIGHEST

def rotary_tables(row_count, col_count):
    half_rot = ROT // 2
    column = jnp.arange(col_count) % HEAD_DIM
    exponent = (2 * (column % half_rot)).astype(jnp.float32) / ROT
    frequency = jnp.exp(-math.log(10000.0) * exponent)
    angles = jnp.arange(row_count).astype(jnp.float32)[:, None] * frequency[None, :]
    inside = column < ROT
    cosine = jnp.where(inside, jnp.cos(angles), 1.0)
    sine_part = jnp.sin(angles)
    ahead_sin = jnp.where(column < half_rot, -sine_part, 0.0)
    behind_sin = jnp.where(inside & (column >= half_rot), sine_part, 0.0)
    return (cosine, ahead_sin, behind_sin)

def rotate(field, tables):
    cosine, ahead_sin, behind_sin = tables
    half_rot = ROT // 2
    return field * cosine + jnp.roll(field, -half_rot, axis=-1) * ahead_sin + jnp.roll(field, half_rot, axis=-1) * behind_sin

def attend(queries, key_rows, values, length):
    block_rows = min(512, LMAX)
    score_scale = 1.0 / math.sqrt(HEAD_DIM)
    query_blocks = queries.reshape(LMAX // block_rows, block_rows, HEADS, HEAD_DIM)
    key_heads = key_rows.reshape(LMAX, HEADS, HEAD_DIM)
    value_heads = values.reshape(LMAX, HEADS, HEAD_DIM)
    col_ids = jnp.arange(LMAX).astype(jnp.int32)

    def one_block(inputs):
        query_block, first_row = inputs
        row_ids = first_row + jnp.arange(block_rows).astype(jnp.int32)
        scores = jnp.einsum('qhd,khd->hqk', query_block, key_heads, precision=highest) * score_scale
        allowed = (col_ids[None, :] <= row_ids[:, None]) & (col_ids[None, :] < length)
        scores = low_back(jnp.where(allowed[None], scores, masked_score))
        attn_probs = low(jax.nn.softmax(scores, axis=-1))
        attention_mixture = jnp.einsum('hqk,khd->qhd', attn_probs, value_heads, precision=highest)
        return attention_mixture.reshape(block_rows, HEADS * HEAD_DIM)
    first_rows = (jnp.arange(LMAX // block_rows) * block_rows).astype(jnp.int32)
    attention_mixture = lax.map(jax.checkpoint(one_block), (query_blocks, first_rows))
    return attention_mixture.reshape(LMAX, HEADS * HEAD_DIM)

def block_forward(seq_rows, params, length):
    qkv_weight, out_weight, fc1_weight, fc2_weight, ln_gain, ln_bias, qkv_bias, out_bias, fc1_bias, fc2_bias = params
    row_mean = lax.optimization_barrier(jnp.mean(seq_rows, -1, keepdims=True))
    centred = seq_rows - row_mean
    variance = lax.optimization_barrier(jnp.mean(centred * centred, -1, keepdims=True))
    normed = centred * lax.rsqrt(variance + eps)
    layernorm_rows = low(normed * ln_gain + ln_bias)
    qkv_raw = jnp.einsum('ld,dcf->lcf', layernorm_rows, qkv_weight, precision=highest) + qkv_bias.reshape(3, D)
    tables = rotary_tables(LMAX, D)
    queries = low(rotate(low_back(qkv_raw[:, 0]), tables))
    key_rows = low(rotate(low_back(qkv_raw[:, 1]), tables))
    values = low_back(low(qkv_raw[:, 2]))
    attention_mixture = low_back(low(attend(queries, key_rows, values, length)))
    pre_act = low_back(jnp.einsum('ld,df->lf', layernorm_rows, fc1_weight, precision=highest) + fc1_bias)
    hidden = low(jax.nn.gelu(pre_act, approximate=True))
    branch = jnp.einsum('ld,ed->le', attention_mixture, out_weight, precision=highest) + jnp.einsum('lf,ef->le', hidden, fc2_weight, precision=highest) + out_bias + fc2_bias
    valid = (jnp.arange(LMAX).astype(jnp.int32) < length)[:, None]
    return seq_rows + jnp.where(valid, branch, 0.0)

def reference(hidden_in, cotangent, lengths, slot_of_seq, seq_of_slot, qkv_weight, out_weight, fc1_weight, fc2_weight, ln_gain, ln_bias, qkv_bias, out_bias, fc1_bias, fc2_bias):
    params = tuple((weight.astype(jnp.float32) for weight in (qkv_weight, out_weight, fc1_weight, fc2_weight, ln_gain, ln_bias, qkv_bias, out_bias, fc1_bias, fc2_bias)))
    slot_x = jnp.take(hidden_in, seq_of_slot, axis=0).astype(jnp.float32)
    slot_len = jnp.take(lengths, seq_of_slot).astype(jnp.int32)
    slot_cot = cotangent.astype(jnp.float32)

    def one_sequence(grad_sums, inputs):
        seq_rows, seq_cot, length = inputs
        seq_out, pull_back = jax.vjp(lambda rows_in, weights_in: block_forward(rows_in, weights_in, length), seq_rows, params)
        grad_seq, grad_weights = pull_back(seq_cot)
        grad_sums = jax.tree.map(jnp.add, grad_sums, grad_weights)
        return (grad_sums, (seq_out.astype(jnp.bfloat16), grad_seq.astype(jnp.bfloat16)))
    zero_grads = jax.tree.map(jnp.zeros_like, params)
    grad_sums, (block_out, grad_slot) = lax.scan(one_sequence, zero_grads, (slot_x, slot_cot, slot_len))
    grad_input = jnp.take(grad_slot, slot_of_seq, axis=0)
    return (block_out, grad_input, grad_sums[0], grad_sums[1], grad_sums[2], grad_sums[3], grad_sums[4], grad_sums[5], grad_sums[6], grad_sums[7], grad_sums[8], grad_sums[9])
```

```python
import math

import jax
import jax.numpy as jnp
from jax import lax
from jax.sharding import PartitionSpec as P

HEAD_DIM = 64
ROT = 32


eps = 1e-05
masked_score = -1e30
f32 = jnp.float32
bf16 = jnp.bfloat16


def rotary_tables(row_count, col_count):
    half_rot = ROT // 2
    column = jnp.arange(col_count) % HEAD_DIM
    exponent = (2 * (column % half_rot)).astype(jnp.float32) / ROT
    frequency = jnp.exp(-math.log(10000.0) * exponent)
    angles = jnp.arange(row_count).astype(jnp.float32)[:, None] * frequency[None, :]
    inside = column < ROT
    cosine = jnp.where(inside, jnp.cos(angles), 1.0)
    sine_part = jnp.sin(angles)
    ahead_sin = jnp.where(column < half_rot, -sine_part, 0.0)
    behind_sin = jnp.where(inside & (column >= half_rot), sine_part, 0.0)
    return (cosine, ahead_sin, behind_sin)


def rotate(field, tables):
    cosine, ahead_sin, behind_sin = tables
    half_rot = ROT // 2
    return (
        field * cosine
        + jnp.roll(field, -half_rot, axis=-1) * ahead_sin
        + jnp.roll(field, half_rot, axis=-1) * behind_sin
    )


def normalize(rows_in):
    row_mean = jnp.mean(rows_in, -1, keepdims=True)
    centred = rows_in - row_mean
    variance = jnp.mean(centred * centred, -1, keepdims=True)
    inv_scale = lax.rsqrt(variance + eps)
    return (centred * inv_scale, inv_scale)


def block_scores(queries, key_heads, first_row, block_rows, length):
    head_count = key_heads.shape[1]
    query_block = queries[first_row : first_row + block_rows].reshape(
        block_rows, head_count, HEAD_DIM
    )
    scores = jnp.einsum(
        "qhd,khd->hqk", query_block, key_heads, preferred_element_type=jnp.float32
    ) * (1.0 / math.sqrt(HEAD_DIM))
    row_ids = first_row + jnp.arange(block_rows, dtype=jnp.int32)
    col_ids = jnp.arange(key_heads.shape[0], dtype=jnp.int32)
    allowed = (col_ids[None, :] <= row_ids[:, None]) & (col_ids[None, :] < length)
    return (jnp.where(allowed[None], scores, masked_score), query_block)


def attend_forward(queries, key_rows, values, length):
    seq_len = queries.shape[0]
    head_count = queries.shape[1] // HEAD_DIM
    key_heads = key_rows.reshape(seq_len, head_count, HEAD_DIM)
    value_heads = values.reshape(seq_len, head_count, HEAD_DIM)
    block_rows = min(512, seq_len)
    mixed_parts = []
    total_parts = []
    for first_row in range(0, seq_len, block_rows):
        scores, query_block = block_scores(queries, key_heads, first_row, block_rows, length)
        row_max = jnp.max(scores, -1, keepdims=True)
        exped = jnp.exp(scores - row_max)
        row_total = jnp.sum(exped, -1, keepdims=True)
        attn_probs = (exped / row_total).astype(jnp.bfloat16)
        attention_mixture = jnp.einsum(
            "hqk,khd->qhd", attn_probs, value_heads, preferred_element_type=jnp.float32
        )
        mixed_parts.append(attention_mixture.reshape(block_rows, head_count * HEAD_DIM))
        total_parts.append(row_max[..., 0] + jnp.log(row_total[..., 0]))
    return (jnp.concatenate(mixed_parts, 0).astype(jnp.bfloat16), jnp.concatenate(total_parts, 1))


def attend_backward(queries, key_rows, values, log_total, grad_mixed, length):
    seq_len = queries.shape[0]
    head_count = queries.shape[1] // HEAD_DIM
    key_heads = key_rows.reshape(seq_len, head_count, HEAD_DIM)
    value_heads = values.reshape(seq_len, head_count, HEAD_DIM)
    block_rows = min(512, seq_len)
    score_scale = 1.0 / math.sqrt(HEAD_DIM)
    grad_query_parts = []
    grad_keys = jnp.zeros((seq_len, head_count, HEAD_DIM), jnp.float32)
    grad_values = jnp.zeros((seq_len, head_count, HEAD_DIM), jnp.float32)
    for first_row in range(0, seq_len, block_rows):
        scores, query_block = block_scores(queries, key_heads, first_row, block_rows, length)
        attn_probs = jnp.exp(scores - log_total[:, first_row : first_row + block_rows, None])
        grad_block = grad_mixed[first_row : first_row + block_rows].reshape(
            block_rows, head_count, HEAD_DIM
        )
        grad_probs = jnp.einsum(
            "qhd,khd->hqk", grad_block, value_heads, preferred_element_type=jnp.float32
        )
        grad_scores = (
            attn_probs * (grad_probs - jnp.sum(attn_probs * grad_probs, -1, keepdims=True))
        ).astype(jnp.bfloat16)
        grad_query = (
            jnp.einsum("hqk,khd->qhd", grad_scores, key_heads, preferred_element_type=jnp.float32)
            * score_scale
        )
        grad_query_parts.append(grad_query.reshape(block_rows, head_count * HEAD_DIM))
        grad_keys = (
            grad_keys
            + jnp.einsum(
                "hqk,qhd->khd", grad_scores, query_block, preferred_element_type=jnp.float32
            )
            * score_scale
        )
        grad_values = grad_values + jnp.einsum(
            "hqk,qhd->khd",
            attn_probs.astype(jnp.bfloat16),
            grad_block,
            preferred_element_type=jnp.float32,
        )
    return (
        jnp.concatenate(grad_query_parts, 0),
        grad_keys.reshape(seq_len, head_count * HEAD_DIM),
        grad_values.reshape(seq_len, head_count * HEAD_DIM),
    )


def flip(array, axis_name, bit):
    size = lax.axis_size(axis_name)
    return lax.ppermute(array, axis_name, [(i, i ^ (1 << bit)) for i in range(size)])


def bits_of(size):
    return size.bit_length() - 1


def swap_blocks(array, index, axis, blocks):
    for bit in range(bits_of(blocks)):
        shape = array.shape
        parts = shape[:axis] + (blocks >> (bit + 1), 2, 1 << bit, shape[axis] // blocks)
        view = array.reshape(parts + shape[axis + 1 :])
        turned = jnp.flip(view, axis=axis + 1)
        array = jnp.where((index >> bit) & 1 == 1, turned, view).reshape(shape)
    return array


def reversed_bits(value, bits):
    return sum(((value >> k) & 1) << (bits - 1 - k) for k in range(bits))


def xor_columns(array, index, blocks):
    width = array.shape[-1] // blocks
    bits = bits_of(blocks)
    pieces = [
        lax.dynamic_slice_in_dim(
            array, (index ^ reversed_bits(p, bits)) * width, width, array.ndim - 1
        )
        for p in range(blocks)
    ]
    return jnp.concatenate(pieces, -1)


def plain_columns(array, index, blocks):
    width = array.shape[-1] // blocks
    bits = bits_of(blocks)
    pieces = []
    for q in range(blocks):
        mask = index ^ q
        place = sum(((mask >> k) & 1) << (bits - 1 - k) for k in range(bits))
        pieces.append(lax.dynamic_slice_in_dim(array, place * width, width, array.ndim - 1))
    return jnp.concatenate(pieces, -1)


def gather_blocks(shard, order):
    bits = len(order)
    stack = shard[None]
    masks = [0]
    for bit in order:
        stack = jnp.concatenate([stack, flip(stack, "dp", bit)], 0)
        masks = masks + [m | (1 << bit) for m in masks]
    pieces = [stack[masks.index(reversed_bits(p, bits))] for p in range(1 << bits)]
    return jnp.concatenate(pieces, 0)


def scatter_blocks(kept, order, rows):
    bits = len(order) + 1
    count = 1 << (bits - 1)
    blocks = {reversed_bits(p, bits): kept[p * rows : (p + 1) * rows] for p in range(count)}
    for step, bit in enumerate(order):
        sent = [m for m in blocks if (m >> bit) & 1]
        arrived = flip(jnp.concatenate([blocks[m] for m in sent], 0), "dp", bit)
        last = step == len(order) - 1
        fresh = {}
        for i, m in enumerate(sent):
            target = m ^ (1 << bit)
            total = blocks[target].astype(f32) + arrived[i * rows : (i + 1) * rows].astype(f32)
            fresh[target] = total if last else total.astype(bf16)
        blocks = fresh
    return blocks[0]


def weight_gradient(rows_by_feature, other, order, rows):
    half = rows_by_feature.shape[1] // 2
    sent = jnp.einsum(
        "rd,rc->dc", rows_by_feature[:, half:], other, preferred_element_type=f32
    ).astype(bf16)
    arrived = flip(sent, "dp", 0)
    kept = jnp.einsum("rd,rc->dc", rows_by_feature[:, :half], other, preferred_element_type=f32)
    kept = (kept + arrived.astype(f32)).astype(bf16)
    return scatter_blocks(kept, order, rows)


def route(block, wanted, index, last):
    bits = bits_of(lax.axis_size("dp"))
    order = [b for b in range(bits - 1, -1, -1) if b != last]
    stack = block[None]
    for bit in order:
        stack = jnp.concatenate([stack, flip(stack, "dp", bit)], 0)

    def place(mask):
        return sum(((mask >> bit) & 1) << k for k, bit in enumerate(order))

    mine = wanted[index]
    theirs = wanted[index ^ (1 << last)]
    given = lax.dynamic_index_in_dim(stack, place(index ^ theirs), 0, keepdims=False)
    held = lax.dynamic_index_in_dim(stack, place(index ^ mine), 0, keepdims=False)
    arrived = flip(given, "dp", last)
    return jnp.where(((index ^ mine) >> last) & 1 == 1, arrived, held)


def route_rows(rows, wanted, index):
    bits = bits_of(lax.axis_size("dp"))
    half = rows.shape[0] // 2
    return jnp.concatenate(
        [
            route(rows[:half], wanted, index, bits - 1),
            route(rows[half:], wanted, index, max(bits - 2, 0)),
        ],
        0,
    )


def gather_small(vector, data_index, tensor_index):
    data_count, tensor_count = lax.axis_size("dp"), lax.axis_size("tensor")
    stack = vector[None]
    for bit in range(bits_of(tensor_count)):
        stack = jnp.concatenate([stack, flip(stack, "tensor", bit)], 0)
    for bit in range(bits_of(data_count)):
        stack = jnp.concatenate([stack, flip(stack, "dp", bit)], 0)
    stack = swap_blocks(stack, data_index * tensor_count + tensor_index, 0, stack.shape[0])
    return stack.reshape(data_count, tensor_count, vector.shape[0])


def scatter_small(blocks, data_index, tensor_index):
    data_count, tensor_count = lax.axis_size("dp"), lax.axis_size("tensor")
    stack = swap_blocks(blocks, data_index * tensor_count + tensor_index, 0, blocks.shape[0])
    for bit in range(bits_of(data_count) - 1, -1, -1):
        half = stack.shape[0] // 2
        stack = stack[:half] + flip(stack[half:], "dp", bit)
    for bit in range(bits_of(tensor_count) - 1, -1, -1):
        half = stack.shape[0] // 2
        stack = stack[:half] + flip(stack[half:], "tensor", bit)
    return stack[0]


def shards(
    hidden_in,
    cotangent,
    lengths,
    slot_of_seq,
    seq_of_slot,
    qkv_weight,
    out_weight,
    fc1_weight,
    fc2_weight,
    ln_gain,
    ln_bias,
    qkv_bias,
    out_bias,
    fc1_bias,
    fc2_bias,
):
    rows_here = hidden_in.shape[1]
    width = hidden_in.shape[2]
    tensor_count = lax.axis_size("tensor")
    data_count = lax.axis_size("dp")
    tensor_index = lax.axis_index("tensor")
    data_index = lax.axis_index("dp")
    seq_len = rows_here * tensor_count
    heads_local = qkv_weight.shape[2]
    hidden_local = fc1_weight.shape[1]
    block = width // data_count
    length = lengths[seq_of_slot[data_index]]
    bits = bits_of(data_count)
    upper = list(range(1, bits))
    x_first = upper + [0]
    y_first = upper[::-1] + [0]

    positions = tensor_index * rows_here + jnp.arange(rows_here, dtype=jnp.int32)
    valid = (positions < length)[:, None]
    cot_rows = xor_columns(cotangent[0], data_index, data_count)
    grad_low = jnp.where(valid, cot_rows, jnp.zeros_like(cot_rows))
    halfway = width // 2
    grads_left = lax.all_gather(grad_low[:, :halfway], "tensor", axis=0, tiled=True)

    routed = route_rows(hidden_in[0], seq_of_slot, data_index)
    slot_rows = xor_columns(routed, data_index, data_count)
    rows_full = lax.all_gather(slot_rows, "tensor", axis=0, tiled=True)
    grads_right = lax.all_gather(grad_low[:, halfway:], "tensor", axis=0, tiled=True)
    grads = jnp.concatenate([grads_left, grads_right], 1)

    small = jnp.concatenate([ln_gain, ln_bias, out_bias, fc2_bias, qkv_bias, fc1_bias])
    gathered = gather_small(small, data_index, tensor_index)
    s = ln_gain.shape[0]
    vectors = [
        xor_columns(gathered[:, :, i * s : (i + 1) * s].reshape(width), data_index, data_count)
        for i in range(4)
    ]
    gain, shift, bias_a, bias_b = [v.astype(f32) for v in vectors]
    q = qkv_bias.shape[0]
    bias_qkv = lax.dynamic_slice_in_dim(
        gathered[:, :, 4 * s : 4 * s + q].reshape(3, width), tensor_index * heads_local, heads_local, 1
    ).astype(f32)
    bias_fc1 = lax.dynamic_slice_in_dim(
        gathered[:, :, 4 * s + q :].reshape(hidden_local * tensor_count),
        tensor_index * hidden_local,
        hidden_local,
        0,
    ).astype(f32)

    w_qk = gather_blocks(
        qkv_weight[:, :2].reshape(block, 2 * heads_local), x_first
    )
    w_vo = gather_blocks(jnp.concatenate([qkv_weight[:, 2], out_weight], 1), y_first)
    w_fc1 = gather_blocks(fc1_weight, x_first)
    w_fc2 = gather_blocks(fc2_weight, y_first)
    w_v, w_out = w_vo[:, :heads_local], w_vo[:, heads_local:]

    full_normed, _ = normalize(rows_full.astype(f32))
    ln = (full_normed * gain + shift).astype(bf16)
    tables = rotary_tables(seq_len, heads_local)
    qk_raw = jnp.einsum("rd,dc->rc", ln, w_qk, preferred_element_type=f32)
    v_raw = jnp.einsum("rd,dc->rc", ln, w_v, preferred_element_type=f32)
    queries = rotate(qk_raw[:, :heads_local] + bias_qkv[0], tables).astype(bf16)
    key_rows = rotate(qk_raw[:, heads_local:] + bias_qkv[1], tables).astype(bf16)
    values = (v_raw + bias_qkv[2]).astype(bf16)
    mixed, log_total = attend_forward(queries, key_rows, values, length)
    pre_act = jnp.einsum("rd,dc->rc", ln, w_fc1, preferred_element_type=f32) + bias_fc1
    hidden = jax.nn.gelu(pre_act, approximate=True).astype(bf16)
    branch_part = (
        jnp.einsum("rd,ed->re", mixed, w_out, preferred_element_type=f32)
        + jnp.einsum("rf,ef->re", hidden, w_fc2, preferred_element_type=f32)
    ).astype(bf16)
    branch_sum = lax.psum_scatter(branch_part, "tensor", scatter_dimension=0, tiled=True)
    slot_f32 = slot_rows.astype(f32)
    branch = branch_sum.astype(f32) + bias_a + bias_b
    block_out = (slot_f32 + jnp.where(valid, branch, 0.0)).astype(bf16)
    block_out = plain_columns(block_out, data_index, data_count)[None]

    grad_bias = jnp.sum(grad_low.astype(f32), axis=0)
    grad_mixed = jnp.einsum("re,ed->rd", grads, w_out, preferred_element_type=f32).astype(bf16)
    grad_hidden = jnp.einsum("re,ef->rf", grads, w_fc2, preferred_element_type=f32)
    _, gelu_pull = jax.vjp(lambda inputs: jax.nn.gelu(inputs, approximate=True), pre_act)
    grad_pre = gelu_pull(grad_hidden)[0].astype(bf16)
    grad_fc1_b = jnp.sum(grad_pre, axis=0, dtype=f32)
    grad_query, grad_keys, grad_values = attend_backward(
        queries, key_rows, values, log_total, grad_mixed, length
    )
    _, rotate_pull = jax.vjp(lambda field: rotate(field, tables), grad_query)
    grad_qk = jnp.concatenate(
        [rotate_pull(grad_query)[0].astype(bf16), rotate_pull(grad_keys)[0].astype(bf16)], 1
    )
    grad_v = grad_values.astype(bf16)
    grad_qkv_b = jnp.concatenate(
        [jnp.sum(grad_qk, 0, dtype=f32), jnp.sum(grad_v, 0, dtype=f32)]
    ).reshape(3, heads_local)
    ln_part = (
        jnp.einsum("rf,df->rd", grad_pre, w_fc1, preferred_element_type=f32)
        + jnp.einsum("rc,dc->rd", grad_qk, w_qk, preferred_element_type=f32)
        + jnp.einsum("rc,dc->rd", grad_v, w_v, preferred_element_type=f32)
    ).astype(bf16)
    grad_ln = lax.psum_scatter(ln_part, "tensor", scatter_dimension=0, tiled=True).astype(f32)

    grad_fc2_w = weight_gradient(grads, hidden, y_first[:-1], block)
    grad_out_w = weight_gradient(grads, mixed, y_first[:-1], block)
    grad_fc1_w = weight_gradient(ln, grad_pre, x_first[:-1], block)
    grad_qk_w = weight_gradient(ln, grad_qk, x_first[:-1], block)
    grad_v_w = weight_gradient(ln, grad_v, y_first[:-1], block)
    grad_qkv_w = jnp.stack(
        [grad_qk_w[:, :heads_local], grad_qk_w[:, heads_local:], grad_v_w], 1
    )

    normed, inv_scale = normalize(slot_f32)
    grad_gain = jnp.sum(grad_ln * normed, axis=0)
    grad_shift = jnp.sum(grad_ln, axis=0)
    grad_norm = grad_ln * gain
    grad_from_norm = inv_scale * (
        grad_norm
        - jnp.mean(grad_norm, -1, keepdims=True)
        - normed * jnp.mean(grad_norm * normed, -1, keepdims=True)
    )
    grad_slot = (cot_rows.astype(f32) + grad_from_norm).astype(bf16)
    grad_slot = plain_columns(grad_slot, data_index, data_count)
    grad_input = route_rows(grad_slot, slot_of_seq, data_index)[None]

    devices = data_count * tensor_count
    full_qkv_b = lax.dynamic_update_slice_in_dim(
        jnp.zeros((3, width), f32), grad_qkv_b, tensor_index * heads_local, 1
    )
    full_fc1_b = lax.dynamic_update_slice_in_dim(
        jnp.zeros((hidden_local * tensor_count,), f32), grad_fc1_b, tensor_index * hidden_local, 0
    )
    sums = jnp.concatenate(
        [plain_columns(v, data_index, data_count).reshape(devices, s) for v in (grad_gain, grad_shift, grad_bias)]
        + [full_qkv_b.reshape(devices, q), full_fc1_b.reshape(devices, -1)],
        1,
    )
    total = scatter_small(sums, data_index, tensor_index)
    return (
        block_out,
        grad_input,
        grad_qkv_w,
        grad_out_w,
        grad_fc1_w,
        grad_fc2_w,
        total[:s],
        total[s : 2 * s],
        total[3 * s : 3 * s + q],
        total[2 * s : 3 * s],
        total[3 * s + q :],
        total[2 * s : 3 * s],
    )


def solution(mesh):
    in_specs = (
        P("dp", "tensor", None),
        P("dp", "tensor", None),
        P(),
        P(),
        P(),
        P("dp", None, "tensor"),
        P("dp", "tensor"),
        P("dp", "tensor"),
        P("dp", "tensor"),
        P(("dp", "tensor")),
        P(("dp", "tensor")),
        P(("dp", "tensor")),
        P(("dp", "tensor")),
        P(("dp", "tensor")),
        P(("dp", "tensor")),
    )
    out_specs = (
        P("dp", "tensor", None),
        P("dp", "tensor", None),
        P("dp", None, "tensor"),
        P("dp", "tensor"),
        P("dp", "tensor"),
        P("dp", "tensor"),
        P(("dp", "tensor")),
        P(("dp", "tensor")),
        P(("dp", "tensor")),
        P(("dp", "tensor")),
        P(("dp", "tensor")),
        P(("dp", "tensor")),
    )
    return jax.shard_map(shards, mesh=mesh, in_specs=in_specs, out_specs=out_specs, check_vma=False)
```

```python
import functools
import math

import jax
import jax.numpy as jnp
from jax import lax
from jax.experimental import pallas as pl
from jax.experimental.pallas import tpu as pltpu
from jax.sharding import PartitionSpec as P

HEAD_DIM = 64
ROT = 32
PAIR = 2 * HEAD_DIM


eps = 1e-05
masked_score = -1e30
f32 = jnp.float32
bf16 = jnp.bfloat16
NN = (((1,), (0,)), ((), ()))
NT = (((1,), (1,)), ((), ()))
TN = (((0,), (0,)), ((), ()))
once = pl.Buffered(1)


def dot(a, b, dims):
    return lax.dot_general(a, b, dims, preferred_element_type=f32)


def params(mib):
    return pltpu.CompilerParams(vmem_limit_bytes=mib * 1024 * 1024)


def cost(flops, nbytes, exps=0):
    return pl.CostEstimate(flops=int(flops), bytes_accessed=int(nbytes), transcendentals=int(exps))


def shape(dims, dtype):
    return jax.ShapeDtypeStruct(dims, dtype)


def turned(field, tables):
    cosine, ahead, behind = tables
    half = ROT // 2
    wide = field.shape[1]
    return (
        field * cosine
        + pltpu.roll(field, wide - half, 1) * ahead
        + pltpu.roll(field, half, 1) * behind
    )


def turned_back(grad, tables):
    cosine, ahead, behind = tables
    half = ROT // 2
    wide = grad.shape[1]
    return (
        grad * cosine
        + pltpu.roll(grad * ahead, half, 1)
        + pltpu.roll(grad * behind, wide - half, 1)
    )


def qkv_kernel(ln_ref, qka_ref, qkb_ref, va_ref, vb_ref, bias_ref, c_ref, a_ref, b_ref, out_ref):
    kind = pl.program_id(0)
    half = ln_ref.shape[1] // 2
    rows = ln_ref.shape[0]
    tile = min(512, rows)
    tables_of = lambda r: (c_ref[r, :], a_ref[r, :], b_ref[r, :])
    for start in range(0, rows, tile):
        r = slice(start, start + tile)

        @pl.when(kind < 2)
        def _():
            raw = dot(ln_ref[r, :half], qka_ref[...], NN) + dot(ln_ref[r, half:], qkb_ref[...], NN)
            raw = raw + bias_ref[0]
            for pair in range(raw.shape[1] // PAIR):
                cols = slice(pair * PAIR, (pair + 1) * PAIR)
                out_ref[0, r, cols] = turned(raw[:, cols], tables_of(r)).astype(bf16)

        @pl.when(kind == 2)
        def _():
            raw = dot(ln_ref[r, :half], va_ref[...], NN) + dot(ln_ref[r, half:], vb_ref[...], NN)
            out_ref[0, r, :] = (raw + bias_ref[0]).astype(bf16)


def project(ln, qk, vo, bias, tables):
    rows, width = ln.shape
    heads = bias.shape[1]
    half = width // 2
    qk_spec = pl.BlockSpec((half, heads), lambda i: (0, jnp.minimum(i, 1)))
    v_spec = pl.BlockSpec((half, heads), lambda i: (0, 0), pipeline_mode=once)
    table_spec = pl.BlockSpec((rows, PAIR), lambda i: (0, 0), pipeline_mode=once)
    return pl.pallas_call(
        qkv_kernel,
        grid=(3,),
        in_specs=[
            pl.BlockSpec((rows, width), lambda i: (0, 0), pipeline_mode=once),
            qk_spec,
            qk_spec,
            v_spec,
            v_spec,
            pl.BlockSpec((1, 1, heads), lambda i: (i, 0, 0)),
            table_spec,
            table_spec,
            table_spec,
        ],
        out_specs=pl.BlockSpec((1, rows, heads), lambda i: (i, 0, 0)),
        out_shape=shape((3, rows, heads), bf16),
        compiler_params=params(48),
        cost_estimate=cost(6 * rows * width * heads, 12 << 20),
        name="project",
    )(ln, qk[0], qk[1], vo[0], vo[1], bias[:, None, :], *tables)


def head_lanes(head):
    lane = lax.broadcasted_iota(jnp.int32, (1, PAIR), 1)
    return (lane // HEAD_DIM) == (head % 2)


def masked_scores(keys, queries, first, length):
    scores = dot(keys, queries, NT)
    key = lax.broadcasted_iota(jnp.int32, scores.shape, 0)
    row = first + lax.broadcasted_iota(jnp.int32, (1, scores.shape[1]), 1)
    return jnp.where(key <= jnp.minimum(row, length - 1), scores, masked_score)


def attend_kernel(block, len_ref, q_ref, k_ref, v_ref, out_ref, total_ref, q_mine, v_turned):
    head = pl.program_id(0)
    lanes = head_lanes(head)
    rows = q_ref.shape[1]
    zero = jnp.zeros((rows, PAIR), bf16)
    scale = jnp.asarray(1.0 / math.sqrt(HEAD_DIM), bf16)
    q_mine[...] = jnp.where(lanes, q_ref[0] * scale, zero)
    v_turned[...] = jnp.where(lanes, v_ref[0], zero).T
    length = len_ref[0]
    for first in range(0, rows, block):
        n = first + block
        r = slice(first, n)
        scores = masked_scores(k_ref[0, :n, :], q_mine[r, :], first, length)
        top = jnp.max(scores, 0, keepdims=True)
        exped = jnp.exp(scores - top)
        total = jnp.sum(exped, 0, keepdims=True)
        probs = (exped * (1.0 / total)).astype(bf16)
        mixed = dot(v_turned[:, :n], probs, NN).T.astype(bf16)
        total_ref[0, :, r] = top + jnp.log(total)

        @pl.when(head % 2 == 0)
        def _():
            out_ref[r, :] = mixed

        @pl.when(head % 2 == 1)
        def _():
            out_ref[r, :] = out_ref[r, :] + mixed


def attend(qkv, length):
    _, rows, width = qkv.shape
    heads = width // HEAD_DIM
    kind = lambda c: pl.BlockSpec((1, rows, PAIR), lambda h, n: (c, 0, h // 2))
    return pl.pallas_call(
        functools.partial(attend_kernel, min(512, rows)),
        grid_spec=pltpu.PrefetchScalarGridSpec(
            num_scalar_prefetch=1,
            grid=(heads,),
            in_specs=[kind(0), kind(1), kind(2)],
            out_specs=[
                pl.BlockSpec((rows, PAIR), lambda h, n: (0, h // 2)),
                pl.BlockSpec((1, 1, rows), lambda h, n: (h, 0, 0)),
            ],
            scratch_shapes=[pltpu.VMEM((rows, PAIR), bf16), pltpu.VMEM((PAIR, rows), bf16)],
        ),
        out_shape=[shape((rows, width), bf16), shape((heads, 1, rows), f32)],
        compiler_params=params(48),
        cost_estimate=cost(16 * rows * rows * width, 4 << 20, rows * rows * heads),
        name="attend",
    )(length, qkv, qkv, qkv)


def attend_back_kernel(
    block, len_ref, q_ref, k_ref, v_ref, do_ref, total_ref, c_ref, a_ref, b_ref,
    grad_ref, q_mine, do_mine, k_turned, key_sum, value_sum,
):
    head = pl.program_id(0)
    lanes = head_lanes(head)
    rows = q_ref.shape[1]
    zero = jnp.zeros((rows, PAIR), bf16)
    scale = 1.0 / math.sqrt(HEAD_DIM)
    q_mine[...] = jnp.where(lanes, q_ref[0] * jnp.asarray(scale, bf16), zero)
    do_mine[...] = jnp.where(lanes, do_ref[...], zero)
    k_turned[...] = jnp.where(lanes, k_ref[0], zero).T
    length = len_ref[0]

    def put(kind, r, value):
        value = value.astype(bf16)

        @pl.when(head % 2 == 0)
        def _():
            grad_ref[kind, r, :] = value

        @pl.when(head % 2 == 1)
        def _():
            grad_ref[kind, r, :] = grad_ref[kind, r, :] + value

    tables_of = lambda r: (c_ref[r, :], a_ref[r, :], b_ref[r, :])
    for first in range(rows - block, -1, -block):
        n = first + block
        r = slice(first, n)
        scores = masked_scores(k_ref[0, :n, :], q_mine[r, :], first, length)
        probs = jnp.exp(scores - total_ref[0, :, r])
        grad_probs = dot(v_ref[0, :n, :], do_mine[r, :], NT)
        product = probs * grad_probs
        delta = jnp.sum(product, 0, keepdims=True)
        grad_scores = (product - probs * delta).astype(bf16)
        keys = dot(grad_scores, q_mine[r, :], NN)
        vals = dot(probs.astype(bf16), do_mine[r, :], NN)
        if n == rows:
            key_sum[...] = keys
            value_sum[...] = vals
        else:
            key_sum[:n, :] += keys
            value_sum[:n, :] += vals
        grad_query = dot(k_turned[:, :n], grad_scores, NN).T * scale
        put(0, r, turned_back(grad_query, tables_of(r)))
    for first in range(0, rows, block):
        r = slice(first, first + block)
        put(1, r, turned_back(key_sum[r, :], tables_of(r)))
        put(2, r, value_sum[r, :])


def attend_back(qkv, grad_mixed, totals, length, tables):
    _, rows, width = qkv.shape
    heads = width // HEAD_DIM
    kind = lambda c: pl.BlockSpec((1, rows, PAIR), lambda h, n: (c, 0, h // 2))
    table_spec = pl.BlockSpec((rows, PAIR), lambda h, n: (0, 0))
    return pl.pallas_call(
        functools.partial(attend_back_kernel, min(512, rows)),
        grid_spec=pltpu.PrefetchScalarGridSpec(
            num_scalar_prefetch=1,
            grid=(heads,),
            in_specs=[
                kind(0),
                kind(1),
                kind(2),
                pl.BlockSpec((rows, PAIR), lambda h, n: (0, h // 2)),
                pl.BlockSpec((1, 1, rows), lambda h, n: (h, 0, 0)),
                table_spec,
                table_spec,
                table_spec,
            ],
            out_specs=pl.BlockSpec((3, rows, PAIR), lambda h, n: (0, 0, h // 2)),
            scratch_shapes=[
                pltpu.VMEM((rows, PAIR), bf16),
                pltpu.VMEM((rows, PAIR), bf16),
                pltpu.VMEM((PAIR, rows), bf16),
                pltpu.VMEM((rows, PAIR), f32),
                pltpu.VMEM((rows, PAIR), f32),
            ],
        ),
        out_shape=shape((3, rows, width), bf16),
        compiler_params=params(48),
        cost_estimate=cost(40 * rows * rows * width, 8 << 20, rows * rows * heads),
        name="attend_back",
    )(length, qkv, qkv, qkv, grad_mixed, totals, *tables)


def feed_kernel(
    tile, steps, ln_ref, mixed_ref, oa_ref, ob_ref, w1a_ref, w1b_ref, w2a_ref, w2b_ref, bias_ref,
    branch_ref, hidden_ref, slope_ref, acc,
):
    step = pl.program_id(0)
    rows = ln_ref.shape[0]
    half = ln_ref.shape[1] // 2
    c0 = math.sqrt(2.0 / math.pi)
    c1 = 0.044715

    @pl.loop(0, rows // tile)
    def _(m):
        r = pl.ds(pl.multiple_of(m * tile, tile), tile)
        pre = dot(ln_ref[r, :half], w1a_ref[...], NN) + dot(ln_ref[r, half:], w1b_ref[...], NN)
        pre = pre + bias_ref[...]
        square = pre * pre
        bent = jnp.tanh(c0 * (pre + c1 * (square * pre)))
        half_pre = 0.5 * pre
        hidden = (half_pre * (1.0 + bent)).astype(bf16)
        hidden_ref[r, :] = hidden
        slope_ref[r, :] = 0.5 * (1.0 + bent) + half_pre * (1.0 - bent * bent) * (
            c0 * (1.0 + (3.0 * c1) * square)
        )
        parts = (dot(hidden, w2a_ref[...], NT), dot(hidden, w2b_ref[...], NT))
        for side, part in enumerate(parts):
            cols = slice(side * half, (side + 1) * half)

            @pl.when(step == 0)
            def _():
                out_ref = (oa_ref, ob_ref)[side]
                acc[r, cols] = part + dot(mixed_ref[r, :], out_ref[...], NT)

            @pl.when((step > 0) & (step < steps - 1))
            def _():
                acc[r, cols] += part

            @pl.when(step == steps - 1)
            def _():
                branch_ref[r, cols] = (acc[r, cols] + part).astype(bf16)


def feed(ln, mixed, vo, w1, w2, bias, tile_f):
    rows, width = ln.shape
    half = width // 2
    hidden = bias.shape[1]
    heads = mixed.shape[1]
    steps = hidden // tile_f
    whole = lambda dims: pl.BlockSpec(dims, lambda i: (0, 0), pipeline_mode=once)
    out_spec = pl.BlockSpec((half, heads), lambda i: (0, 1), pipeline_mode=once)
    weight = pl.BlockSpec((half, tile_f), lambda i: (0, i))
    by_row = pl.BlockSpec((rows, tile_f), lambda i: (0, i))
    return pl.pallas_call(
        functools.partial(feed_kernel, min(512, rows), steps),
        grid=(steps,),
        in_specs=[whole((rows, width)), whole((rows, heads)), out_spec, out_spec]
        + [weight] * 4
        + [pl.BlockSpec((1, tile_f), lambda i: (0, i))],
        out_specs=[whole((rows, width)), by_row, by_row],
        out_shape=[
            shape((rows, width), bf16),
            shape((rows, hidden), bf16),
            shape((rows, hidden), f32),
        ],
        scratch_shapes=[pltpu.VMEM((rows, width), f32)],
        compiler_params=params(58),
        cost_estimate=cost(4 * rows * width * hidden, 40 << 20, rows * hidden),
        name="feed",
    )(ln, mixed, vo[0], vo[1], w1[0], w1[1], w2[0], w2[1], bias)


def feed_back_kernel(
    tile, tile_d, ln_ref, g_ref, w1a_ref, w1b_ref, w2a_ref, w2b_ref, hidden_ref, slope_ref,
    sum_ref, k1_ref, s1_ref, k2_ref, s2_ref, bias_ref, grad_pre,
):
    step = pl.program_id(0)
    rows, width = ln_ref.shape
    half = width // 2

    @pl.loop(0, rows // tile)
    def _(m):
        r = pl.ds(pl.multiple_of(m * tile, tile), tile)
        grad = dot(g_ref[r, :half], w2a_ref[...], NN) + dot(g_ref[r, half:], w2b_ref[...], NN)
        grad = (grad * slope_ref[r, :]).astype(bf16)
        grad_pre[r, :] = grad
        for side, weight_ref in enumerate((w1a_ref, w1b_ref)):
            cols = slice(side * half, (side + 1) * half)
            part = dot(grad, weight_ref[...], NT)

            @pl.when(step == 0)
            def _():
                sum_ref[r, cols] = part

            @pl.when(step > 0)
            def _():
                sum_ref[r, cols] += part

    bias_ref[...] = jnp.sum(grad_pre[...].astype(f32), axis=0, keepdims=True)

    @pl.loop(0, half // tile_d)
    def _(k):
        c = pl.ds(pl.multiple_of(k * tile_d, tile_d), tile_d)
        far = pl.ds(pl.multiple_of(half + k * tile_d, tile_d), tile_d)
        k2_ref[c, :] = dot(g_ref[:, c], hidden_ref[...], TN).astype(bf16)
        s2_ref[c, :] = dot(g_ref[:, far], hidden_ref[...], TN).astype(bf16)
        k1_ref[c, :] = dot(ln_ref[:, c], grad_pre[...], TN).astype(bf16)
        s1_ref[c, :] = dot(ln_ref[:, far], grad_pre[...], TN).astype(bf16)


def feed_back(ln, grads, w1, w2, hidden, slope, tile_f):
    rows, width = ln.shape
    half = width // 2
    units = hidden.shape[1]
    steps = units // tile_f
    whole = pl.BlockSpec((rows, width), lambda i: (0, 0), pipeline_mode=once)
    weight = pl.BlockSpec((half, tile_f), lambda i: (0, i))
    by_row = pl.BlockSpec((rows, tile_f), lambda i: (0, i))
    return pl.pallas_call(
        functools.partial(feed_back_kernel, min(512, rows), min(512, half)),
        grid=(steps,),
        in_specs=[whole, whole] + [weight] * 4 + [by_row, by_row],
        out_specs=[whole] + [weight] * 4 + [pl.BlockSpec((1, tile_f), lambda i: (0, i))],
        out_shape=[shape((rows, width), f32)]
        + [shape((half, units), bf16)] * 4
        + [shape((1, units), f32)],
        scratch_shapes=[pltpu.VMEM((rows, tile_f), bf16)],
        compiler_params=params(60),
        cost_estimate=cost(8 * rows * width * units, 60 << 20),
        name="feed_back",
    )(ln, grads, w1[0], w1[1], w2[0], w2[1], hidden, slope)


def mixed_grad_kernel(g_ref, oa_ref, ob_ref, out_ref):
    half = g_ref.shape[1] // 2
    out_ref[...] = (
        dot(g_ref[:, :half], oa_ref[...], NN) + dot(g_ref[:, half:], ob_ref[...], NN)
    ).astype(bf16)


def mixed_grad(grads, vo, heads):
    rows, width = grads.shape
    half = width // 2
    tile = min(512, rows)
    out_spec = pl.BlockSpec((half, heads), lambda i: (0, 1), pipeline_mode=once)
    return pl.pallas_call(
        mixed_grad_kernel,
        grid=(rows // tile,),
        in_specs=[pl.BlockSpec((tile, width), lambda i: (i, 0)), out_spec, out_spec],
        out_specs=pl.BlockSpec((tile, heads), lambda i: (i, 0)),
        out_shape=shape((rows, heads), bf16),
        compiler_params=params(40),
        cost_estimate=cost(2 * rows * width * heads, 7 << 20),
        name="mixed_grad",
    )(grads, vo[0], vo[1])


def ln_grad_kernel(grad_ref, qka_ref, qkb_ref, va_ref, vb_ref, sum_ref, out_ref):
    half = sum_ref.shape[1] // 2
    heads = grad_ref.shape[2]
    sides = ((qka_ref, va_ref), (qkb_ref, vb_ref))
    for side, (qk_ref, v_ref) in enumerate(sides):
        cols = slice(side * half, (side + 1) * half)
        total = sum_ref[:, cols]
        total += dot(grad_ref[0], qk_ref[:, :heads], NT)
        total += dot(grad_ref[1], qk_ref[:, heads:], NT)
        total += dot(grad_ref[2], v_ref[...], NT)
        out_ref[:, cols] = total.astype(bf16)


def ln_grad(grad_qkv, qk, vo, partial_sum):
    _, rows, heads = grad_qkv.shape
    width = partial_sum.shape[1]
    half = width // 2
    tile = min(512, rows)
    qk_spec = pl.BlockSpec((half, 2 * heads), lambda i: (0, 0), pipeline_mode=once)
    v_spec = pl.BlockSpec((half, heads), lambda i: (0, 0), pipeline_mode=once)
    return pl.pallas_call(
        ln_grad_kernel,
        grid=(rows // tile,),
        in_specs=[
            pl.BlockSpec((3, tile, heads), lambda i: (0, i, 0)),
            qk_spec,
            qk_spec,
            v_spec,
            v_spec,
            pl.BlockSpec((tile, width), lambda i: (i, 0)),
        ],
        out_specs=pl.BlockSpec((tile, width), lambda i: (i, 0)),
        out_shape=shape((rows, width), bf16),
        compiler_params=params(48),
        cost_estimate=cost(6 * rows * width * heads, 22 << 20),
        name="ln_grad",
    )(grad_qkv, qk[0], qk[1], vo[0], vo[1], partial_sum)


def weight_grad_kernel(ln_ref, g_ref, grad_ref, mixed_ref, kqk_ref, kvo_ref, sqk_ref, svo_ref, bias_ref):
    heads = mixed_ref.shape[1]
    step = pl.program_id(0)
    steps = pl.num_programs(0)
    for kind in range(3):
        @pl.when(step == 0)
        def _():
            bias_ref[kind] = jnp.sum(grad_ref[kind].astype(f32), axis=0, keepdims=True)

    for qk_ref, vo_ref, here in ((kqk_ref, kvo_ref, step < steps // 2), (sqk_ref, svo_ref, step >= steps // 2)):
        @pl.when(here)
        def _():
            qk_ref[:, :heads] = dot(ln_ref[...], grad_ref[0], TN).astype(bf16)
            qk_ref[:, heads:] = dot(ln_ref[...], grad_ref[1], TN).astype(bf16)
            vo_ref[:, :heads] = dot(ln_ref[...], grad_ref[2], TN).astype(bf16)
            vo_ref[:, heads:] = dot(g_ref[...], mixed_ref[...], TN).astype(bf16)


def weight_grad(ln, grads, grad_qkv, mixed):
    rows, width = ln.shape
    heads = mixed.shape[1]
    half = width // 2
    tile = min(512, half)
    near = half // tile
    column = pl.BlockSpec((rows, tile), lambda i: (0, i))
    kept = pl.BlockSpec((tile, 2 * heads), lambda i: (jnp.minimum(i, near - 1), 0))
    sent = pl.BlockSpec((tile, 2 * heads), lambda i: (jnp.maximum(i - near, 0), 0))
    return pl.pallas_call(
        weight_grad_kernel,
        grid=(2 * near,),
        in_specs=[
            column,
            column,
            pl.BlockSpec((3, rows, heads), lambda i: (0, 0, 0), pipeline_mode=once),
            pl.BlockSpec((rows, heads), lambda i: (0, 0), pipeline_mode=once),
        ],
        out_specs=[kept, kept, sent, sent, pl.BlockSpec((3, 1, heads), lambda i: (0, 0, 0))],
        out_shape=[shape((half, 2 * heads), bf16)] * 4 + [shape((3, 1, heads), f32)],
        compiler_params=params(48),
        cost_estimate=cost(8 * rows * width * heads, 20 << 20),
        name="weight_grad",
    )(ln, grads, grad_qkv, mixed)


def normalize(rows_in):
    row_mean = jnp.mean(rows_in, -1, keepdims=True)
    centred = rows_in - row_mean
    variance = jnp.mean(centred * centred, -1, keepdims=True)
    inv_scale = lax.rsqrt(variance + eps)
    return (centred * inv_scale, inv_scale)


def rotary_tables(row_count, col_count):
    half_rot = ROT // 2
    column = jnp.arange(col_count) % HEAD_DIM
    exponent = (2 * (column % half_rot)).astype(jnp.float32) / ROT
    frequency = jnp.exp(-math.log(10000.0) * exponent)
    angles = jnp.arange(row_count).astype(jnp.float32)[:, None] * frequency[None, :]
    inside = column < ROT
    cosine = jnp.where(inside, jnp.cos(angles), 1.0)
    sine_part = jnp.sin(angles)
    ahead_sin = jnp.where(column < half_rot, -sine_part, 0.0)
    behind_sin = jnp.where(inside & (column >= half_rot), sine_part, 0.0)
    return (cosine, ahead_sin, behind_sin)


def flip(array, axis_name, bit):
    size = lax.axis_size(axis_name)
    return lax.ppermute(array, axis_name, [(i, i ^ (1 << bit)) for i in range(size)])


def bits_of(size):
    return size.bit_length() - 1


def swap_blocks(array, index, axis, blocks):
    for bit in range(bits_of(blocks)):
        dims = array.shape
        parts = dims[:axis] + (blocks >> (bit + 1), 2, 1 << bit, dims[axis] // blocks)
        view = array.reshape(parts + dims[axis + 1 :])
        other = jnp.flip(view, axis=axis + 1)
        array = jnp.where((index >> bit) & 1 == 1, other, view).reshape(dims)
    return array


def reversed_bits(value, bits):
    return sum(((value >> k) & 1) << (bits - 1 - k) for k in range(bits))


def xor_columns(array, index, blocks):
    width = array.shape[-1] // blocks
    bits = bits_of(blocks)
    pieces = [
        lax.dynamic_slice_in_dim(
            array, (index ^ reversed_bits(p, bits)) * width, width, array.ndim - 1
        )
        for p in range(blocks)
    ]
    return jnp.concatenate(pieces, -1)


def plain_columns(array, index, blocks):
    width = array.shape[-1] // blocks
    bits = bits_of(blocks)
    pieces = []
    for q in range(blocks):
        place = reversed_bits(index ^ q, bits)
        pieces.append(lax.dynamic_slice_in_dim(array, place * width, width, array.ndim - 1))
    return jnp.concatenate(pieces, -1)


def gather_first(shard, order):
    return {0: shard, 1 << order[0]: flip(shard, "dp", order[0])}


def gather_second(blocks, order):
    masks = sorted(blocks)
    bit = order[len(bin(len(blocks))) - 3]
    return flip(jnp.concatenate([blocks[m] for m in masks], 0), "dp", bit)


def with_arrived(blocks, arrived, order):
    rows = blocks[0].shape[0]
    bit = order[len(bin(len(blocks))) - 3]
    fresh = dict(blocks)
    for i, m in enumerate(sorted(blocks)):
        fresh[m | (1 << bit)] = arrived[i * rows : (i + 1) * rows]
    return fresh


def gather_upper(blocks, order, arrived=None):
    while len(blocks) < (1 << len(order)):
        if arrived is None:
            arrived = gather_second(blocks, order)
        blocks = with_arrived(blocks, arrived, order)
        arrived = None
    return blocks


def gather_core(blocks, order):
    bits = len(order) + 1
    near = jnp.concatenate([blocks[reversed_bits(p, bits)] for p in range(1 << len(order))], 0)
    return near, flip(near, "dp", 0)


def by_position(kept, order, rows):
    bits = len(order) + 1
    count = 1 << (bits - 1)
    return {reversed_bits(p, bits): kept[p * rows : (p + 1) * rows] for p in range(count)}


def merge(kept, arrived):
    return (kept.astype(f32) + arrived.astype(f32)).astype(bf16)


def scatter_start(blocks, bit):
    given = [m for m in blocks if (m >> bit) & 1]
    return flip(jnp.concatenate([blocks[m] for m in given], 0), "dp", bit)


def scatter_end(blocks, arrived, bit, last):
    rows = blocks[0].shape[0]
    fresh = {}
    for i, m in enumerate([m for m in blocks if (m >> bit) & 1]):
        target = m ^ (1 << bit)
        total = blocks[target].astype(f32) + arrived[i * rows : (i + 1) * rows].astype(f32)
        fresh[target] = total if last else total.astype(bf16)
    return fresh


def route_order(last):
    return [b for b in range(bits_of(lax.axis_size("dp")) - 1, -1, -1) if b != last]


def route_first(block, last):
    return jnp.stack([block, flip(block, "dp", route_order(last)[0])], 0)


def route_rest(stack, wanted, index, last):
    order = route_order(last)
    for bit in order[1:]:
        stack = jnp.concatenate([stack, flip(stack, "dp", bit)], 0)

    def place(mask):
        return sum(((mask >> bit) & 1) << k for k, bit in enumerate(order))

    mine = wanted[index]
    theirs = wanted[index ^ (1 << last)]
    given = lax.dynamic_index_in_dim(stack, place(index ^ theirs), 0, keepdims=False)
    held = lax.dynamic_index_in_dim(stack, place(index ^ mine), 0, keepdims=False)
    arrived = flip(given, "dp", last)
    return jnp.where(((index ^ mine) >> last) & 1 == 1, arrived, held)


def gather_small(vector, data_index, tensor_index):
    data_count, tensor_count = lax.axis_size("dp"), lax.axis_size("tensor")
    stack = vector[None]
    for bit in range(bits_of(tensor_count)):
        stack = jnp.concatenate([stack, flip(stack, "tensor", bit)], 0)
    for bit in range(bits_of(data_count)):
        stack = jnp.concatenate([stack, flip(stack, "dp", bit)], 0)
    stack = swap_blocks(stack, data_index * tensor_count + tensor_index, 0, stack.shape[0])
    return stack.reshape(data_count, tensor_count, vector.shape[0])


def scatter_small(blocks, data_index, tensor_index):
    data_count, tensor_count = lax.axis_size("dp"), lax.axis_size("tensor")
    stack = swap_blocks(blocks, data_index * tensor_count + tensor_index, 0, blocks.shape[0])
    for bit in range(bits_of(data_count) - 1, -1, -1):
        half = stack.shape[0] // 2
        stack = stack[:half] + flip(stack[half:], "dp", bit)
    for bit in range(bits_of(tensor_count) - 1, -1, -1):
        half = stack.shape[0] // 2
        stack = stack[:half] + flip(stack[half:], "tensor", bit)
    return stack[0]


def after(values, *others):
    held = lax.optimization_barrier((tuple(values), tuple(others)))
    return held[0]


def shards(
    hidden_in,
    cotangent,
    lengths,
    slot_of_seq,
    seq_of_slot,
    qkv_weight,
    out_weight,
    fc1_weight,
    fc2_weight,
    ln_gain,
    ln_bias,
    qkv_bias,
    out_bias,
    fc1_bias,
    fc2_bias,
):
    rows_here = hidden_in.shape[1]
    width = hidden_in.shape[2]
    tensor_count = lax.axis_size("tensor")
    data_count = lax.axis_size("dp")
    tensor_index = lax.axis_index("tensor")
    data_index = lax.axis_index("dp")
    seq_len = rows_here * tensor_count
    heads_local = qkv_weight.shape[2]
    hidden_local = fc1_weight.shape[1]
    block = width // data_count
    length = lengths[seq_of_slot[data_index]]
    bits = bits_of(data_count)
    x_first = list(range(1, bits))
    y_first = x_first[::-1]
    tile_f = min(512, hidden_local)

    half_rows = rows_here // 2
    lasts = (bits - 1, bits - 2)
    halves = (hidden_in[0, :half_rows], hidden_in[0, half_rows:])
    firsts = [route_first(h, last) for h, last in zip(halves, lasts)]
    qk_shard = qkv_weight[:, :2].reshape(block, 2 * heads_local)
    vo_shard = jnp.concatenate([qkv_weight[:, 2], out_weight], 1)
    qk_shard, vo_shard = after((qk_shard, vo_shard), *firsts)
    qk_blocks = gather_first(qk_shard, x_first)
    vo_blocks = gather_first(vo_shard, y_first)
    routed = jnp.concatenate(
        [route_rest(f, seq_of_slot, data_index, last) for f, last in zip(firsts, lasts)], 0
    )
    slot_rows = xor_columns(routed, data_index, data_count)
    rows_full = lax.all_gather(slot_rows, "tensor", axis=0, tiled=True)

    positions = tensor_index * rows_here + jnp.arange(rows_here, dtype=jnp.int32)
    valid = (positions < length)[:, None]
    cot_plain, = after((cotangent[0],), routed)
    cot_rows = xor_columns(cot_plain, data_index, data_count)
    grad_low = jnp.where(valid, cot_rows, jnp.zeros_like(cot_rows))
    grads = lax.all_gather(grad_low, "tensor", axis=0, tiled=True)

    w_qk = gather_core(gather_upper(qk_blocks, x_first), x_first)
    w_vo = gather_core(gather_upper(vo_blocks, y_first), y_first)
    fc1_shard, fc2_shard = after(
        (fc1_weight, fc2_weight), routed, *qk_blocks.values(), *vo_blocks.values()
    )
    fc1_blocks = gather_first(fc1_shard, x_first)
    fc2_blocks = gather_first(fc2_shard, y_first)
    fc1_next = gather_second(fc1_blocks, x_first)
    fc2_next = gather_second(fc2_blocks, y_first)

    small = jnp.concatenate([ln_gain, ln_bias, out_bias, fc2_bias, qkv_bias, fc1_bias])
    gathered = gather_small(small, data_index, tensor_index)
    s = ln_gain.shape[0]
    vectors = [
        xor_columns(gathered[:, :, i * s : (i + 1) * s].reshape(width), data_index, data_count)
        for i in range(4)
    ]
    gain, shift, bias_a, bias_b = [v.astype(f32) for v in vectors]
    q = qkv_bias.shape[0]
    bias_qkv = lax.dynamic_slice_in_dim(
        gathered[:, :, 4 * s : 4 * s + q].reshape(3, width), tensor_index * heads_local, heads_local, 1
    ).astype(f32)
    bias_fc1 = lax.dynamic_slice_in_dim(
        gathered[:, :, 4 * s + q :].reshape(1, hidden_local * tensor_count),
        tensor_index * hidden_local,
        hidden_local,
        1,
    ).astype(f32)

    full_normed, _ = normalize(rows_full.astype(f32))
    ln = (full_normed * gain + shift).astype(bf16)
    tables = rotary_tables(seq_len, PAIR)
    size = length.reshape(1)
    qkv = project(ln, w_qk, w_vo, bias_qkv, tables)
    fc1_next, fc2_next = after((fc1_next, fc2_next), qkv)
    w_fc1 = gather_core(gather_upper(fc1_blocks, x_first, fc1_next), x_first)
    w_fc2 = gather_core(gather_upper(fc2_blocks, y_first, fc2_next), y_first)
    attend_in, = after((qkv,), w_fc1[0], w_fc2[0])
    mixed, totals = attend(attend_in, size)
    branch_part, hidden, slope = feed(ln, mixed, w_vo, w_fc1, w_fc2, bias_fc1, tile_f)
    branch_sum = lax.psum_scatter(branch_part, "tensor", scatter_dimension=0, tiled=True)

    feed_sum, k1, s1, k2, s2, grad_fc1_b = feed_back(ln, grads, w_fc1, w_fc2, hidden, slope, tile_f)
    c1, c2 = flip(s1, "dp", 0), flip(s2, "dp", 0)
    grads_again, = after((grads,), feed_sum)
    grad_mixed = mixed_grad(grads_again, w_vo, heads_local)
    grad_qkv = attend_back(qkv, grad_mixed, totals, size, tables)
    grad_qkv, = after((grad_qkv,), branch_sum)
    ln_part = ln_grad(grad_qkv, w_qk, w_vo, feed_sum)
    grad_ln = lax.psum_scatter(ln_part, "tensor", scatter_dimension=0, tiled=True).astype(f32)
    k1, k2 = after((k1, k2), ln_part)
    m1 = by_position(merge(k1, c1), x_first, block)
    m2 = by_position(merge(k2, c2), y_first, block)
    f1, f2 = scatter_start(m1, x_first[0]), scatter_start(m2, y_first[0])
    mixed_again, = after((mixed,), m1, m2)
    kqk, kvo, sqk, svo, grad_qkv_b = weight_grad(ln, grads, grad_qkv, mixed_again)
    cqk, cvo = flip(sqk, "dp", 0), flip(svo, "dp", 0)
    mqk = by_position(merge(kqk, cqk), x_first, block)
    mvo = by_position(merge(kvo, cvo), y_first, block)
    fqk, fvo = scatter_start(mqk, x_first[0]), scatter_start(mvo, y_first[0])
    m1, m2 = after((m1, m2), mqk, mvo)
    for step in range(len(x_first)):
        last = step == len(x_first) - 1
        m1 = scatter_end(m1, f1, x_first[step], last)
        m2 = scatter_end(m2, f2, y_first[step], last)
        if not last:
            f1, f2 = scatter_start(m1, x_first[step + 1]), scatter_start(m2, y_first[step + 1])
            grad_ln, = after((grad_ln,), m1, m2)

    grad_bias = jnp.sum(grad_low.astype(f32), axis=0)
    slot_f32 = slot_rows.astype(f32)
    normed, inv_scale = normalize(slot_f32)
    grad_gain = jnp.sum(grad_ln * normed, axis=0)
    grad_shift = jnp.sum(grad_ln, axis=0)
    grad_norm = grad_ln * gain
    grad_from_norm = inv_scale * (
        grad_norm
        - jnp.mean(grad_norm, -1, keepdims=True)
        - normed * jnp.mean(grad_norm * normed, -1, keepdims=True)
    )
    grad_slot = (cot_rows.astype(f32) + grad_from_norm).astype(bf16)
    grad_slot = plain_columns(grad_slot, data_index, data_count)
    out_firsts = [
        route_first(h, last)
        for h, last in zip((grad_slot[:half_rows], grad_slot[half_rows:]), lasts)
    ]
    mqk, mvo = after((mqk, mvo), *out_firsts)
    for step in range(len(x_first)):
        last = step == len(x_first) - 1
        mqk = scatter_end(mqk, fqk, x_first[step], last)
        mvo = scatter_end(mvo, fvo, y_first[step], last)
        if not last:
            fqk, fvo = scatter_start(mqk, x_first[step + 1]), scatter_start(mvo, y_first[step + 1])
    grad_fc1_w, grad_fc2_w, grad_qk_w, grad_vo_w = m1[0], m2[0], mqk[0], mvo[0]
    grad_out_w = grad_vo_w[:, heads_local:]
    grad_qkv_w = jnp.stack(
        [grad_qk_w[:, :heads_local], grad_qk_w[:, heads_local:], grad_vo_w[:, :heads_local]], 1
    )
    grad_input = jnp.concatenate(
        [route_rest(f, slot_of_seq, data_index, last) for f, last in zip(out_firsts, lasts)], 0
    )[None]

    branch = branch_sum.astype(f32) + bias_a + bias_b
    block_out = (slot_f32 + jnp.where(valid, branch, 0.0)).astype(bf16)
    block_out = plain_columns(block_out, data_index, data_count)[None]

    devices = data_count * tensor_count
    full_qkv_b = lax.dynamic_update_slice_in_dim(
        jnp.zeros((3, width), f32), grad_qkv_b[:, 0], tensor_index * heads_local, 1
    )
    full_fc1_b = lax.dynamic_update_slice_in_dim(
        jnp.zeros((hidden_local * tensor_count,), f32), grad_fc1_b[0], tensor_index * hidden_local, 0
    )
    sums = jnp.concatenate(
        [
            plain_columns(v, data_index, data_count).reshape(devices, s)
            for v in (grad_gain, grad_shift, grad_bias)
        ]
        + [full_qkv_b.reshape(devices, q), full_fc1_b.reshape(devices, -1)],
        1,
    )
    total = scatter_small(sums, data_index, tensor_index)
    return (
        block_out,
        grad_input,
        grad_qkv_w,
        grad_out_w,
        grad_fc1_w,
        grad_fc2_w,
        total[:s],
        total[s : 2 * s],
        total[3 * s : 3 * s + q],
        total[2 * s : 3 * s],
        total[3 * s + q :],
        total[2 * s : 3 * s],
    )


def solution(mesh):
    in_specs = (
        P("dp", "tensor", None),
        P("dp", "tensor", None),
        P(),
        P(),
        P(),
        P("dp", None, "tensor"),
        P("dp", "tensor"),
        P("dp", "tensor"),
        P("dp", "tensor"),
        P(("dp", "tensor")),
        P(("dp", "tensor")),
        P(("dp", "tensor")),
        P(("dp", "tensor")),
        P(("dp", "tensor")),
        P(("dp", "tensor")),
    )
    out_specs = (
        P("dp", "tensor", None),
        P("dp", "tensor", None),
        P("dp", None, "tensor"),
        P("dp", "tensor"),
        P("dp", "tensor"),
        P("dp", "tensor"),
        P(("dp", "tensor")),
        P(("dp", "tensor")),
        P(("dp", "tensor")),
        P(("dp", "tensor")),
        P(("dp", "tensor")),
        P(("dp", "tensor")),
    )
    return jax.shard_map(shards, mesh=mesh, in_specs=in_specs, out_specs=out_specs, check_vma=False)
```

```python
import functools
import math

import jax
import jax.numpy as jnp
from jax import lax
from jax.experimental import pallas as pl
from jax.experimental.pallas import tpu as pltpu
from jax.sharding import PartitionSpec as P

HEAD_DIM = 64
ROT = 32
PAIR = 2 * HEAD_DIM
VMEM = 63 * 1024 * 1024
SHARE = 0.4


eps = 1e-05
masked_score = -1e30
f32 = jnp.float32
bf16 = jnp.bfloat16
NN = (((1,), (0,)), ((), ()))
NT = (((1,), (1,)), ((), ()))
TN = (((0,), (0,)), ((), ()))
once = pl.Buffered(1)


def dot(a, b, dims):
    return lax.dot_general(a, b, dims, preferred_element_type=f32)


def params(mib):
    return pltpu.CompilerParams(vmem_limit_bytes=VMEM)


def cost(flops, nbytes, exps=0):
    return pl.CostEstimate(
        flops=int(flops * SHARE), bytes_accessed=int(nbytes * SHARE), transcendentals=int(exps * SHARE)
    )


def shape(dims, dtype):
    return jax.ShapeDtypeStruct(dims, dtype)


def turned(field, tables):
    cosine, ahead, behind = tables
    half = ROT // 2
    wide = field.shape[1]
    return (
        field * cosine
        + pltpu.roll(field, wide - half, 1) * ahead
        + pltpu.roll(field, half, 1) * behind
    )


def turned_back(grad, tables):
    cosine, ahead, behind = tables
    half = ROT // 2
    wide = grad.shape[1]
    return (
        grad * cosine
        + pltpu.roll(grad * ahead, half, 1)
        + pltpu.roll(grad * behind, wide - half, 1)
    )


def norm_kernel(x_ref, gain_ref, shift_ref, *rest):
    out_ref = rest[-1]
    rows = x_ref[...].astype(f32)
    centred = rows - jnp.mean(rows, -1, keepdims=True)
    scale = lax.rsqrt(jnp.mean(centred * centred, -1, keepdims=True) + eps)
    out_ref[...] = (centred * scale * gain_ref[...] + shift_ref[...]).astype(bf16)


def norm_wave(rows_in, gain, shift, wave, held):
    rows, width = rows_in.shape
    tile = min(128, rows)
    steps = rows // tile
    vector = pl.BlockSpec((1, width), lambda i: (0, 0))
    extra = [] if held is None else [held]
    return pl.pallas_call(
        norm_kernel,
        grid=(steps,),
        in_specs=[pl.BlockSpec((tile, width), lambda i: (i, 0)), vector, vector]
        + [pl.BlockSpec(memory_space=pl.ANY)] * len(extra),
        out_specs=pl.BlockSpec((tile, width), lambda i: (i + wave * steps, 0)),
        out_shape=shape((2 * rows, width), bf16),
        input_output_aliases={3: 0} if extra else {},
        compiler_params=params(32),
        cost_estimate=cost(10 * rows * width, 4 * rows * width),
        name="norm_wave",
    )(rows_in, gain, shift, *extra)


def project_rows(kind, ln_ref, weight, bias_ref, tables, out_ref):
    raw = dot(ln_ref[...], weight, NN) + bias_ref[0]

    @pl.when(kind < 2)
    def _():
        for pair in range(raw.shape[1] // PAIR):
            cols = slice(pair * PAIR, (pair + 1) * PAIR)
            out_ref[0, :, cols] = turned(raw[:, cols], [t[...] for t in tables]).astype(bf16)

    @pl.when(kind == 2)
    def _():
        out_ref[0] = raw.astype(bf16)


def assemble_start(refs, plan, column, size, buffer, sems):
    for j, (which, row, place, count) in enumerate(plan):
        pltpu.make_async_copy(
            refs[which].at[pl.ds(row, count), pl.ds(column, size)],
            buffer.at[pl.ds(place, count), :],
            sems.at[j],
        ).start()


def assemble_wait(refs, plan, column, size, buffer, sems):
    for j, (which, row, place, count) in enumerate(plan):
        pltpu.make_async_copy(
            refs[which].at[pl.ds(row, count), pl.ds(column, size)],
            buffer.at[pl.ds(place, count), :],
            sems.at[j],
        ).wait()


def project_first_kernel(qk_plan, vo_plan, ln_ref, bias_ref, c_ref, a_ref, b_ref, *rest):
    n = len({p[0] for p in qk_plan})
    qk_refs, vo_refs = rest[:n], rest[n : 2 * n]
    out_ref, w_ref, buffer, sems, out_sems = rest[2 * n :]
    kind = pl.program_id(0)
    heads = buffer.shape[2]
    sources = (
        (qk_refs, qk_plan, 0),
        (qk_refs, qk_plan, heads),
        (vo_refs, vo_plan, 0),
        (vo_refs, vo_plan, heads),
    )

    def drain(k):
        pltpu.make_async_copy(buffer.at[k % 2], w_ref.at[k], out_sems.at[k % 2]).wait()

    for k in range(4):
        refs, plan, column = sources[k]
        slot = k % 2

        @pl.when(kind == k)
        def _():
            if k == 0:
                assemble_start(refs, plan, column, heads, buffer.at[slot], sems.at[slot])
            assemble_wait(refs, plan, column, heads, buffer.at[slot], sems.at[slot])
            pltpu.make_async_copy(buffer.at[slot], w_ref.at[k], out_sems.at[slot]).start()
            if k >= 1:
                drain(k - 1)
            if k < 3:
                nrefs, nplan, ncolumn = sources[k + 1]
                assemble_start(
                    nrefs, nplan, ncolumn, heads, buffer.at[1 - slot], sems.at[1 - slot]
                )
            else:
                drain(k)

    @pl.when(kind < 3)
    def _():
        project_rows(kind, ln_ref, buffer[kind % 2], bias_ref, (c_ref, a_ref, b_ref), out_ref)


def project_first(ln, qk, vo, bias, tables):
    rows, width = ln.shape[0] // 2, ln.shape[1]
    heads = bias.shape[1]
    table = pl.BlockSpec((rows, PAIR), lambda i: (0, 0), pipeline_mode=once)
    hbm = pl.BlockSpec(memory_space=pl.ANY)
    last = lambda i: jnp.minimum(i, 2)
    return pl.pallas_call(
        functools.partial(project_first_kernel, qk[1], vo[1]),
        grid=(4,),
        in_specs=[
            pl.BlockSpec((rows, width), lambda i: (0, 0), pipeline_mode=once),
            pl.BlockSpec((1, 1, heads), lambda i: (last(i), 0, 0)),
            table,
            table,
            table,
        ]
        + [hbm] * (len(qk[0]) + len(vo[0])),
        out_specs=[pl.BlockSpec((1, rows, heads), lambda i: (last(i), 0, 0)), hbm],
        out_shape=[shape((3, 2 * rows, heads), bf16), shape((4, width, heads), bf16)],
        scratch_shapes=[
            pltpu.VMEM((2, width, heads), bf16),
            pltpu.SemaphoreType.DMA((2, len(qk[1]))),
            pltpu.SemaphoreType.DMA((2,)),
        ],
        compiler_params=params(48),
        cost_estimate=cost(6 * rows * width * heads, 22 << 20),
        name="project_first",
    )(ln, bias[:, None, :], *tables, *qk[0], *vo[0])


def project_second_kernel(ln_ref, w_ref, bias_ref, c_ref, a_ref, b_ref, held_ref, out_ref):
    project_rows(pl.program_id(0), ln_ref, w_ref[0], bias_ref, (c_ref, a_ref, b_ref), out_ref)


def project_second(ln, weights, bias, tables, held):
    rows, width = ln.shape[0] // 2, ln.shape[1]
    heads = bias.shape[1]
    table = pl.BlockSpec((rows, PAIR), lambda i: (1, 0), pipeline_mode=once)
    return pl.pallas_call(
        project_second_kernel,
        grid=(3,),
        in_specs=[
            pl.BlockSpec((rows, width), lambda i: (1, 0), pipeline_mode=once),
            pl.BlockSpec((1, width, heads), lambda i: (i, 0, 0)),
            pl.BlockSpec((1, 1, heads), lambda i: (i, 0, 0)),
            table,
            table,
            table,
            pl.BlockSpec(memory_space=pl.ANY),
        ],
        out_specs=pl.BlockSpec((1, rows, heads), lambda i: (i, 1, 0)),
        out_shape=shape(held.shape, bf16),
        input_output_aliases={6: 0},
        compiler_params=params(48),
        cost_estimate=cost(6 * rows * width * heads, 12 << 20),
        name="project_second",
    )(ln, weights, bias[:, None, :], *tables, held)


def head_lanes(head):
    lane = lax.broadcasted_iota(jnp.int32, (1, PAIR), 1)
    return (lane // HEAD_DIM) == (head % 2)


def masked_scores(keys, queries, first, length):
    scores = dot(keys, queries, NT)
    key = lax.broadcasted_iota(jnp.int32, scores.shape, 0)
    row = first + lax.broadcasted_iota(jnp.int32, (1, scores.shape[1]), 1)
    return jnp.where(key <= jnp.minimum(row, length - 1), scores, masked_score)


def chunk_places(rows, chunks):
    size = rows // chunks
    return [((c % 2) * (chunks // 2) + c // 2) * size for c in range(chunks)], size


def in_sequence(value, chunks):
    places, size = chunk_places(value.shape[0], chunks)
    return jnp.concatenate([value[p : p + size] for p in places], 0)


def attend_kernel(block, chunks, len_ref, q_ref, k_ref, v_ref, *rest):
    out_ref, total_ref, q_mine, k_all, v_turned = rest[-5:]
    head = pl.program_id(0)
    lanes = head_lanes(head)
    rows = q_ref.shape[1]
    zero = jnp.zeros((rows, PAIR), bf16)
    scale = jnp.asarray(1.0 / math.sqrt(HEAD_DIM), bf16)
    q_mine[...] = in_sequence(jnp.where(lanes, q_ref[0] * scale, zero), chunks)
    k_all[...] = in_sequence(k_ref[0], chunks)
    v_turned[...] = in_sequence(jnp.where(lanes, v_ref[0], zero), chunks).T
    length = len_ref[0]
    places, size = chunk_places(rows, chunks)
    for first in range(0, rows, block):
        n = first + block
        r = slice(first, n)
        scores = masked_scores(k_all[:n, :], q_mine[r, :], first, length)
        top = jnp.max(scores, 0, keepdims=True)
        exped = jnp.exp(scores - top)
        total = jnp.sum(exped, 0, keepdims=True)
        probs = (exped * (1.0 / total)).astype(bf16)
        mixed = dot(v_turned[:, :n], probs, NN).T.astype(bf16)
        total_ref[0, :, r] = top + jnp.log(total)

        @pl.when(head % 2 == 0)
        def _():
            for c in range(block // size):
                place = places[first // size + c]
                out_ref[place : place + size, :] = mixed[c * size : (c + 1) * size]

        @pl.when(head % 2 == 1)
        def _():
            for c in range(block // size):
                place = places[first // size + c]
                out_ref[place : place + size, :] += mixed[c * size : (c + 1) * size]


def attend(qkv, length, chunks, part, held):
    _, rows, width = qkv.shape
    heads = width // HEAD_DIM
    here = heads // 2
    off = part * here
    kind = lambda c: pl.BlockSpec((1, rows, PAIR), lambda h, n: (c, 0, (h + off) // 2))
    extra = [] if held is None else list(held)
    return pl.pallas_call(
        functools.partial(attend_kernel, min(512, rows), chunks),
        grid_spec=pltpu.PrefetchScalarGridSpec(
            num_scalar_prefetch=1,
            grid=(here,),
            in_specs=[kind(0), kind(1), kind(2)]
            + [pl.BlockSpec(memory_space=pl.ANY)] * len(extra),
            out_specs=[
                pl.BlockSpec((rows, PAIR), lambda h, n: (0, (h + off) // 2)),
                pl.BlockSpec((1, 1, rows), lambda h, n: (h + off, 0, 0)),
            ],
            scratch_shapes=[
                pltpu.VMEM((rows, PAIR), bf16),
                pltpu.VMEM((rows, PAIR), bf16),
                pltpu.VMEM((PAIR, rows), bf16),
            ],
        ),
        out_shape=[shape((rows, width), bf16), shape((heads, 1, rows), f32)],
        input_output_aliases={4 + k: k for k in range(len(extra))},
        compiler_params=params(48),
        cost_estimate=cost(8 * rows * rows * width, 2 << 20, rows * rows * here),
        name="attend",
    )(length, qkv, qkv, qkv, *extra)


def attend_back_kernel(
    block, chunks, len_ref, q_ref, k_ref, v_ref, do_ref, total_ref, c_ref, a_ref, b_ref, *rest
):
    grad_ref, q_mine, do_mine, k_all, v_all, k_turned, key_sum, value_sum = rest[-8:]
    head = pl.program_id(0)
    lanes = head_lanes(head)
    rows = q_ref.shape[1]
    zero = jnp.zeros((rows, PAIR), bf16)
    scale = 1.0 / math.sqrt(HEAD_DIM)
    q_mine[...] = in_sequence(jnp.where(lanes, q_ref[0] * jnp.asarray(scale, bf16), zero), chunks)
    do_mine[...] = in_sequence(jnp.where(lanes, do_ref[...], zero), chunks)
    keys = in_sequence(k_ref[0], chunks)
    k_all[...] = keys
    v_all[...] = in_sequence(v_ref[0], chunks)
    k_turned[...] = jnp.where(lanes, keys, zero).T
    length = len_ref[0]
    places, size = chunk_places(rows, chunks)

    def put(kind, first, value):
        value = value.astype(bf16)

        @pl.when(head % 2 == 0)
        def _():
            for c in range(block // size):
                place = places[first // size + c]
                grad_ref[kind, place : place + size, :] = value[c * size : (c + 1) * size]

        @pl.when(head % 2 == 1)
        def _():
            for c in range(block // size):
                place = places[first // size + c]
                grad_ref[kind, place : place + size, :] += value[c * size : (c + 1) * size]

    tables_of = lambda r: (c_ref[r, :], a_ref[r, :], b_ref[r, :])
    for first in range(rows - block, -1, -block):
        n = first + block
        r = slice(first, n)
        scores = masked_scores(k_all[:n, :], q_mine[r, :], first, length)
        probs = jnp.exp(scores - total_ref[0, :, r])
        grad_probs = dot(v_all[:n, :], do_mine[r, :], NT)
        product = probs * grad_probs
        delta = jnp.sum(product, 0, keepdims=True)
        grad_scores = (product - probs * delta).astype(bf16)
        grad_keys = dot(grad_scores, q_mine[r, :], NN)
        grad_values = dot(probs.astype(bf16), do_mine[r, :], NN)
        if n == rows:
            key_sum[...] = grad_keys
            value_sum[...] = grad_values
        else:
            key_sum[:n, :] += grad_keys
            value_sum[:n, :] += grad_values
        grad_query = dot(k_turned[:, :n], grad_scores, NN).T * scale
        put(0, first, turned_back(grad_query, tables_of(r)))
    for first in range(0, rows, block):
        r = slice(first, first + block)
        put(1, first, turned_back(key_sum[r, :], tables_of(r)))
        put(2, first, value_sum[r, :])


def attend_back(qkv, grad_mixed, totals, length, tables, chunks):
    _, rows, width = qkv.shape
    heads = width // HEAD_DIM
    kind = lambda c: pl.BlockSpec((1, rows, PAIR), lambda h, n: (c, 0, h // 2))
    table = pl.BlockSpec((rows, PAIR), lambda h, n: (0, 0))
    return pl.pallas_call(
        functools.partial(attend_back_kernel, min(512, rows), chunks),
        grid_spec=pltpu.PrefetchScalarGridSpec(
            num_scalar_prefetch=1,
            grid=(heads,),
            in_specs=[
                kind(0),
                kind(1),
                kind(2),
                pl.BlockSpec((rows, PAIR), lambda h, n: (0, h // 2)),
                pl.BlockSpec((1, 1, rows), lambda h, n: (h, 0, 0)),
                table,
                table,
                table,
            ],
            out_specs=pl.BlockSpec((3, rows, PAIR), lambda h, n: (0, 0, h // 2)),
            scratch_shapes=[pltpu.VMEM((rows, PAIR), bf16)] * 4
            + [pltpu.VMEM((PAIR, rows), bf16)]
            + [pltpu.VMEM((rows, PAIR), f32)] * 2,
        ),
        out_shape=shape((3, rows, width), bf16),
        compiler_params=params(48),
        cost_estimate=cost(40 * rows * rows * width, 8 << 20, rows * rows * heads),
        name="attend_back",
    )(length, qkv, qkv, qkv, grad_mixed, totals, *tables)


def feed_kernel(tile, tile_f, steps, plan1, plan2, ln_ref, mixed_ref, wo_ref, bias_ref, *rest):
    n1 = len({p[0] for p in plan1})
    w1_refs, w2_refs = rest[:n1], rest[n1 : 2 * n1]
    (first_ref, second_ref, hidden_ref, slope_ref, full1_ref, full2_ref, acc, buf1, buf2, sems1,
     sems2, out_sems) = rest[2 * n1 :]
    step = pl.program_id(0)
    slot = lax.rem(step, 2)
    rows = ln_ref.shape[0]
    c0 = math.sqrt(2.0 / math.pi)
    c1 = 0.044715

    def start(s, at):
        column = pl.multiple_of(s * tile_f, tile_f)
        assemble_start(w1_refs, plan1, column, tile_f, buf1.at[at], sems1.at[at])
        assemble_start(w2_refs, plan2, column, tile_f, buf2.at[at], sems2.at[at])

    def outward(s, at):
        column = pl.multiple_of(s * tile_f, tile_f)
        return (
            pltpu.make_async_copy(
                buf1.at[at], full1_ref.at[:, pl.ds(column, tile_f)], out_sems.at[at, 0]
            ),
            pltpu.make_async_copy(
                buf2.at[at], full2_ref.at[:, pl.ds(column, tile_f)], out_sems.at[at, 1]
            ),
        )

    @pl.when(step == 0)
    def _():
        start(0, 0)

    column = pl.multiple_of(step * tile_f, tile_f)
    assemble_wait(w1_refs, plan1, column, tile_f, buf1.at[slot], sems1.at[slot])
    assemble_wait(w2_refs, plan2, column, tile_f, buf2.at[slot], sems2.at[slot])
    for copy in outward(step, slot):
        copy.start()

    @pl.when(step > 0)
    def _():
        for copy in outward(step - 1, 1 - slot):
            copy.wait()

    @pl.when(step < steps - 1)
    def _():
        start(step + 1, 1 - slot)

    @pl.loop(0, rows // tile)
    def _(m):
        r = pl.ds(pl.multiple_of(m * tile, tile), tile)
        pre = dot(ln_ref[r, :], buf1[slot], NN) + bias_ref[...]
        square = pre * pre
        bent = jnp.tanh(c0 * (pre + c1 * (square * pre)))
        half_pre = 0.5 * pre
        hidden = (half_pre * (1.0 + bent)).astype(bf16)
        hidden_ref[r, :] = hidden
        slope_ref[r, :] = 0.5 * (1.0 + bent) + half_pre * (1.0 - bent * bent) * (
            c0 * (1.0 + (3.0 * c1) * square)
        )
        part = dot(hidden, buf2[slot], NT)

        @pl.when(step == 0)
        def _():
            acc[r, :] = part + dot(mixed_ref[r, :], wo_ref[0], NT)

        @pl.when((step > 0) & (step < steps - 1))
        def _():
            acc[r, :] += part

        for wave, wave_ref in enumerate((first_ref, second_ref)):
            @pl.when((step == steps - 1) & (m == wave))
            def _():
                wave_ref[...] = (acc[r, :] + part).astype(bf16)

    @pl.when(step == steps - 1)
    def _():
        for copy in outward(step, slot):
            copy.wait()


def feed(ln, mixed, weights, w1, w2, bias, tile_f):
    rows, width = ln.shape
    hidden = bias.shape[1]
    heads = mixed.shape[1]
    steps = hidden // tile_f
    whole = lambda dims: pl.BlockSpec(dims, lambda i: (0, 0), pipeline_mode=once)
    by_row = pl.BlockSpec((rows, tile_f), lambda i: (0, i))
    hbm = pl.BlockSpec(memory_space=pl.ANY)
    return pl.pallas_call(
        functools.partial(feed_kernel, rows // 2, tile_f, steps, w1[1], w2[1]),
        grid=(steps,),
        in_specs=[
            whole((rows, width)),
            whole((rows, heads)),
            pl.BlockSpec((1, width, heads), lambda i: (3, 0, 0), pipeline_mode=once),
            pl.BlockSpec((1, tile_f), lambda i: (0, i)),
        ]
        + [hbm] * (len(w1[0]) + len(w2[0])),
        out_specs=[whole((rows // 2, width))] * 2 + [by_row, by_row, hbm, hbm],
        out_shape=[
            shape((rows // 2, width), bf16),
            shape((rows // 2, width), bf16),
            shape((rows, hidden), bf16),
            shape((rows, hidden), f32),
            shape((width, hidden), bf16),
            shape((width, hidden), bf16),
        ],
        scratch_shapes=[
            pltpu.VMEM((rows, width), f32),
            pltpu.VMEM((2, width, tile_f), bf16),
            pltpu.VMEM((2, width, tile_f), bf16),
            pltpu.SemaphoreType.DMA((2, len(w1[1]))),
            pltpu.SemaphoreType.DMA((2, len(w2[1]))),
            pltpu.SemaphoreType.DMA((2, 2)),
        ],
        compiler_params=params(58),
        cost_estimate=cost(4 * rows * width * hidden, 56 << 20, rows * hidden),
        name="feed",
    )(ln, mixed, weights, bias, *w1[0], *w2[0])


def column_products(left_ref, right_ref, near_ref, far_ref, tile):
    half = left_ref.shape[1] // 2

    @pl.loop(0, half // tile)
    def _(k):
        c = pl.ds(pl.multiple_of(k * tile, tile), tile)
        far = pl.ds(pl.multiple_of(half + k * tile, tile), tile)
        near_ref[c, :] = dot(left_ref[:, c], right_ref[...], TN).astype(bf16)
        far_ref[c, :] = dot(left_ref[:, far], right_ref[...], TN).astype(bf16)


def back_rows_kernel(first, g_ref, w1_ref, w2_ref, slope_ref, wo_ref, *rest):
    sum_ref, pre_ref, mixed_ref, all_ref, bias_ref = rest[-5:]
    step = pl.program_id(0)

    @pl.when(step == 0)
    def _():
        all_ref[...] = g_ref[...]
        mixed_ref[...] = dot(g_ref[...], wo_ref[0], NN).astype(bf16)

    grad = (dot(g_ref[...], w2_ref[...], NN) * slope_ref[...]).astype(bf16)
    pre_ref[...] = grad
    bias_ref[...] = jnp.sum(grad.astype(f32), axis=0, keepdims=True)
    part = dot(grad, w1_ref[...], NT)

    @pl.when(step == 0)
    def _():
        sum_ref[...] = part

    @pl.when(step > 0)
    def _():
        sum_ref[...] += part


def back_rows(grads, w1, w2, slope, weights, tile_f, wave, held):
    rows, width = grads.shape
    units = slope.shape[1]
    heads = weights.shape[2]
    weight = pl.BlockSpec((width, tile_f), lambda i: (0, i))
    extra = [] if held is None else list(held)
    return pl.pallas_call(
        functools.partial(back_rows_kernel, wave == 0),
        grid=(units // tile_f,),
        in_specs=[
            pl.BlockSpec((rows, width), lambda i: (0, 0), pipeline_mode=once),
            weight,
            weight,
            pl.BlockSpec((rows, tile_f), lambda i: (wave, i)),
            pl.BlockSpec((1, width, heads), lambda i: (3, 0, 0), pipeline_mode=once),
        ]
        + [pl.BlockSpec(memory_space=pl.ANY)] * len(extra),
        out_specs=[
            pl.BlockSpec((rows, width), lambda i: (0, 0), pipeline_mode=once),
            pl.BlockSpec((rows, tile_f), lambda i: (wave, i)),
            pl.BlockSpec((rows, heads), lambda i: (wave, 0), pipeline_mode=once),
            pl.BlockSpec((rows, width), lambda i: (wave, 0), pipeline_mode=once),
            pl.BlockSpec((1, tile_f), lambda i: (0, i)),
        ],
        out_shape=[
            shape((rows, width), f32),
            shape((2 * rows, units), bf16),
            shape((2 * rows, heads), bf16),
            shape((2 * rows, width), bf16),
            shape((1, units), f32),
        ],
        input_output_aliases={5 + k: 1 + k for k in range(len(extra))},
        compiler_params=params(58),
        cost_estimate=cost(4 * rows * width * units, 30 << 20),
        name="back_rows",
    )(grads, w1, w2, slope, weights, *extra)


def feed_weight_kernel(tile, ln_ref, pre_ref, near_ref, far_ref):
    column_products(ln_ref, pre_ref, near_ref, far_ref, tile)


def feed_weight(ln, grad_pre, tile_f):
    rows, width = ln.shape
    units = grad_pre.shape[1]
    half = pl.BlockSpec((width // 2, tile_f), lambda i: (0, i))
    return pl.pallas_call(
        functools.partial(feed_weight_kernel, min(512, width // 2)),
        grid=(units // tile_f,),
        in_specs=[
            pl.BlockSpec((rows, width), lambda i: (0, 0), pipeline_mode=once),
            pl.BlockSpec((rows, tile_f), lambda i: (0, i)),
        ],
        out_specs=[half, half],
        out_shape=[shape((width // 2, units), bf16)] * 2,
        compiler_params=params(48),
        cost_estimate=cost(2 * rows * width * units, 16 << 20),
        name="feed_weight",
    )(ln, grad_pre)


def ln_grad_kernel(grad_ref, w_ref, sum_ref, out_ref):
    total = sum_ref[...]
    for kind in range(3):
        total += dot(grad_ref[kind], w_ref[kind], NT)
    out_ref[...] = total.astype(bf16)


def ln_grad(grad_qkv, weights, partial_sum, wave):
    _, rows, heads = grad_qkv.shape
    width = partial_sum.shape[1]
    tile = min(256, rows // 2)
    steps = rows // 2 // tile
    return pl.pallas_call(
        ln_grad_kernel,
        grid=(steps,),
        in_specs=[
            pl.BlockSpec((3, tile, heads), lambda i: (0, i + wave * steps, 0)),
            pl.BlockSpec((3, width, heads), lambda i: (0, 0, 0), pipeline_mode=once),
            pl.BlockSpec((tile, width), lambda i: (i, 0)),
        ],
        out_specs=pl.BlockSpec((tile, width), lambda i: (i, 0)),
        out_shape=shape((rows // 2, width), bf16),
        compiler_params=params(48),
        cost_estimate=cost(3 * rows * width * heads, 14 << 20),
        name="ln_grad",
    )(grad_qkv, weights, partial_sum)


def weight_grad_kernel(ln_ref, g_ref, grad_ref, mixed_ref, kqk_ref, kvo_ref, sqk_ref, svo_ref, bias_ref):
    heads = mixed_ref.shape[1]
    step = pl.program_id(0)
    steps = pl.num_programs(0)
    for kind in range(3):
        @pl.when(step == 0)
        def _():
            bias_ref[kind] = jnp.sum(grad_ref[kind].astype(f32), axis=0, keepdims=True)

    for qk_ref, vo_ref, here in ((kqk_ref, kvo_ref, step < steps // 2), (sqk_ref, svo_ref, step >= steps // 2)):
        @pl.when(here)
        def _():
            qk_ref[:, :heads] = dot(ln_ref[...], grad_ref[0], TN).astype(bf16)
            qk_ref[:, heads:] = dot(ln_ref[...], grad_ref[1], TN).astype(bf16)
            vo_ref[:, :heads] = dot(ln_ref[...], grad_ref[2], TN).astype(bf16)
            vo_ref[:, heads:] = dot(g_ref[...], mixed_ref[...], TN).astype(bf16)


def weight_grad(ln, grads, grad_qkv, mixed):
    rows, width = ln.shape
    heads = mixed.shape[1]
    half = width // 2
    tile = min(512, half)
    near = half // tile
    column = pl.BlockSpec((rows, tile), lambda i: (0, i))
    kept = pl.BlockSpec((tile, 2 * heads), lambda i: (jnp.minimum(i, near - 1), 0))
    sent = pl.BlockSpec((tile, 2 * heads), lambda i: (jnp.maximum(i - near, 0), 0))
    return pl.pallas_call(
        weight_grad_kernel,
        grid=(2 * near,),
        in_specs=[
            column,
            column,
            pl.BlockSpec((3, rows, heads), lambda i: (0, 0, 0), pipeline_mode=once),
            pl.BlockSpec((rows, heads), lambda i: (0, 0), pipeline_mode=once),
        ],
        out_specs=[kept, kept, sent, sent, pl.BlockSpec((3, 1, heads), lambda i: (0, 0, 0))],
        out_shape=[shape((half, 2 * heads), bf16)] * 4 + [shape((3, 1, heads), f32)],
        compiler_params=params(48),
        cost_estimate=cost(8 * rows * width * heads, 20 << 20),
        name="weight_grad",
    )(ln, grads, grad_qkv, mixed)


def merge_kernel(kept_give, kept_hold, come_give, come_hold, give_ref, hold_ref):
    give_ref[...] = (kept_give[...].astype(f32) + come_give[...].astype(f32)).astype(bf16)
    hold_ref[...] = (kept_hold[...].astype(f32) + come_hold[...].astype(f32)).astype(bf16)


def merge(kept, arrived, rule, part=(0, 1)):
    rows, width = kept.shape[0], kept.shape[1] // part[1]
    count, odd = rule
    block = rows // count
    half = count // 2
    wide = min(1024, width)
    off = part[0] * (width // wide)
    give = pl.BlockSpec((block, wide), lambda i, j: (2 * i + 1 if odd else i + half, j + off))
    hold = pl.BlockSpec((block, wide), lambda i, j: (2 * i if odd else i, j + off))
    out = pl.BlockSpec((block, wide), lambda i, j: (i, j))
    return pl.pallas_call(
        merge_kernel,
        grid=(half, width // wide),
        in_specs=[give, hold, give, hold],
        out_specs=[out, out],
        out_shape=[shape((rows // 2, width), bf16)] * 2,
        compiler_params=params(32),
        cost_estimate=cost(rows * width, 6 * rows * width),
        name="merge",
    )(kept, kept, arrived, arrived)


def norm_back_kernel(
    blocks, index_ref, sum_ref, rows_ref, cot_ref, gain_ref, out_ref, gain_sum_ref, shift_sum_ref, held
):
    grad_ln = sum_ref[...].astype(f32)
    rows = rows_ref[...].astype(f32)
    centred = rows - jnp.mean(rows, -1, keepdims=True)
    inv_scale = lax.rsqrt(jnp.mean(centred * centred, -1, keepdims=True) + eps)
    normed = centred * inv_scale
    grad_norm = grad_ln * gain_ref[...]
    product = grad_ln * normed
    back = inv_scale * (
        grad_norm
        - jnp.mean(grad_norm, -1, keepdims=True)
        - normed * jnp.mean(grad_norm * normed, -1, keepdims=True)
    )
    held[...] = (cot_ref[...].astype(f32) + back).astype(bf16)
    gain_sum_ref[...] = jnp.sum(product, 0, keepdims=True)
    shift_sum_ref[...] = jnp.sum(grad_ln, 0, keepdims=True)
    wide = rows.shape[1] // blocks
    bits = blocks.bit_length() - 1
    for q in range(blocks):
        place = reversed_bits(index_ref[0] ^ q, bits) * wide
        out_ref[:, q * wide : (q + 1) * wide] = held[:, pl.ds(pl.multiple_of(place, wide), wide)]


def norm_back(total, rows_in, cot, gain, index, blocks):
    rows, width = rows_in.shape
    whole = pl.BlockSpec((rows, width), lambda i, n: (0, 0))
    vector = pl.BlockSpec((1, width), lambda i, n: (0, 0))
    return pl.pallas_call(
        functools.partial(norm_back_kernel, blocks),
        grid_spec=pltpu.PrefetchScalarGridSpec(
            num_scalar_prefetch=1,
            grid=(1,),
            in_specs=[whole, whole, whole, vector],
            out_specs=[whole, vector, vector],
            scratch_shapes=[pltpu.VMEM((rows, width), bf16)],
        ),
        out_shape=[shape((rows, width), bf16), shape((1, width), f32), shape((1, width), f32)],
        compiler_params=params(32),
        cost_estimate=cost(20 * rows * width, 8 * rows * width),
        name="norm_back",
    )(index.reshape(1), total, rows_in, cot, gain)


def normalize(rows_in):
    row_mean = jnp.mean(rows_in, -1, keepdims=True)
    centred = rows_in - row_mean
    variance = jnp.mean(centred * centred, -1, keepdims=True)
    inv_scale = lax.rsqrt(variance + eps)
    return (centred * inv_scale, inv_scale)


def rotary_tables(rows, col_count):
    half_rot = ROT // 2
    column = jnp.arange(col_count) % HEAD_DIM
    exponent = (2 * (column % half_rot)).astype(jnp.float32) / ROT
    frequency = jnp.exp(-math.log(10000.0) * exponent)
    angles = rows.astype(jnp.float32)[:, None] * frequency[None, :]
    inside = column < ROT
    cosine = jnp.where(inside, jnp.cos(angles), 1.0)
    sine_part = jnp.sin(angles)
    ahead_sin = jnp.where(column < half_rot, -sine_part, 0.0)
    behind_sin = jnp.where(inside & (column >= half_rot), sine_part, 0.0)
    return (cosine, ahead_sin, behind_sin)


def flip(array, axis_name, bit):
    size = lax.axis_size(axis_name)
    return lax.ppermute(array, axis_name, [(i, i ^ (1 << bit)) for i in range(size)])


def bits_of(size):
    return size.bit_length() - 1


def swap_blocks(array, index, axis, blocks):
    for bit in range(bits_of(blocks)):
        dims = array.shape
        parts = dims[:axis] + (blocks >> (bit + 1), 2, 1 << bit, dims[axis] // blocks)
        view = array.reshape(parts + dims[axis + 1 :])
        other = jnp.flip(view, axis=axis + 1)
        array = jnp.where((index >> bit) & 1 == 1, other, view).reshape(dims)
    return array


def reversed_bits(value, bits):
    return sum(((value >> k) & 1) << (bits - 1 - k) for k in range(bits))


def xor_columns(array, index, blocks):
    width = array.shape[-1] // blocks
    bits = bits_of(blocks)
    pieces = [
        lax.dynamic_slice_in_dim(
            array, (index ^ reversed_bits(p, bits)) * width, width, array.ndim - 1
        )
        for p in range(blocks)
    ]
    return jnp.concatenate(pieces, -1)


def plain_columns(array, index, blocks):
    width = array.shape[-1] // blocks
    bits = bits_of(blocks)
    pieces = []
    for q in range(blocks):
        place = reversed_bits(index ^ q, bits)
        pieces.append(lax.dynamic_slice_in_dim(array, place * width, width, array.ndim - 1))
    return jnp.concatenate(pieces, -1)


def gather_step(stacks, bit):
    return stacks + [(flip(rows, "dp", bit), [m | (1 << bit) for m in masks]) for rows, masks in stacks]


def gather_plan(stacks, block, bits):
    plan = []
    for which, (_, masks) in enumerate(stacks):
        for i, m in enumerate(masks):
            plan.append((which, i * block, reversed_bits(m, bits) * block, block))
    return [s[0] for s in stacks], tuple(plan)


def core_copies(stacks):
    return [(flip(rows, "dp", 0), [m | 1 for m in masks]) for rows, masks in stacks]


def route_order(last):
    return [b for b in range(bits_of(lax.axis_size("dp")) - 1, -1, -1) if b != last]


def route_first(block, last):
    return jnp.stack([block, flip(block, "dp", route_order(last)[0])], 0)


def route_rest(stack, wanted, index, last):
    order = route_order(last)
    for bit in order[1:]:
        stack = jnp.concatenate([stack, flip(stack, "dp", bit)], 0)

    def place(mask):
        return sum(((mask >> bit) & 1) << k for k, bit in enumerate(order))

    mine = wanted[index]
    theirs = wanted[index ^ (1 << last)]
    given = lax.dynamic_index_in_dim(stack, place(index ^ theirs), 0, keepdims=False)
    held = lax.dynamic_index_in_dim(stack, place(index ^ mine), 0, keepdims=False)
    arrived = flip(given, "dp", last)
    return jnp.where(((index ^ mine) >> last) & 1 == 1, arrived, held)


def gather_small(stack, axis_name):
    for bit in range(bits_of(lax.axis_size(axis_name))):
        stack = jnp.concatenate([stack, flip(stack, axis_name, bit)], 0)
    return stack


def scatter_small(blocks, data_index, tensor_index):
    data_count, tensor_count = lax.axis_size("dp"), lax.axis_size("tensor")
    stack = swap_blocks(blocks, data_index * tensor_count + tensor_index, 0, blocks.shape[0])
    for bit in range(bits_of(data_count) - 1, -1, -1):
        half = stack.shape[0] // 2
        stack = stack[:half] + flip(stack[half:], "dp", bit)
    for bit in range(bits_of(tensor_count) - 1, -1, -1):
        half = stack.shape[0] // 2
        stack = stack[:half] + flip(stack[half:], "tensor", bit)
    return stack[0]


def after(values, *others):
    held = lax.optimization_barrier((tuple(values), tuple(others)))
    return held[0]


def shards(
    hidden_in,
    cotangent,
    lengths,
    slot_of_seq,
    seq_of_slot,
    qkv_weight,
    out_weight,
    fc1_weight,
    fc2_weight,
    ln_gain,
    ln_bias,
    qkv_bias,
    out_bias,
    fc1_bias,
    fc2_bias,
):
    rows_here = hidden_in.shape[1]
    width = hidden_in.shape[2]
    tensor_count = lax.axis_size("tensor")
    data_count = lax.axis_size("dp")
    tensor_index = lax.axis_index("tensor")
    data_index = lax.axis_index("dp")
    seq_len = rows_here * tensor_count
    heads_local = qkv_weight.shape[2]
    hidden_local = fc1_weight.shape[1]
    block = width // data_count
    length = lengths[seq_of_slot[data_index]]
    bits = bits_of(data_count)
    x_first = list(range(1, bits))
    y_first = x_first[::-1]
    tile_f = min(512, hidden_local)

    chunks = 2 * tensor_count
    lasts = (bits - 1, bits - 2)
    wave_rows = rows_here // 2
    quarter = wave_rows // 2

    def send(rows):
        half = rows.shape[0] // 2
        return [route_first(h, last) for h, last in zip((rows[:half], rows[half:]), lasts)]

    def receive(firsts, wanted):
        return jnp.concatenate(
            [route_rest(f, wanted, data_index, last) for f, last in zip(firsts, lasts)], 0
        )

    firsts = send(hidden_in[0])
    vectors = [ln_gain, ln_bias, out_bias, fc2_bias, qkv_bias, fc1_bias]
    s = ln_gain.shape[0]
    vectors = after(vectors, *firsts)
    small = jnp.concatenate([v.reshape(-1, s) for v in vectors], 0)
    stack = gather_small(gather_small(small[None], "tensor"), "dp")
    routed = receive(firsts, seq_of_slot)
    routed, stack = after((routed, stack))
    gathered = swap_blocks(stack, data_index * tensor_count + tensor_index, 0, stack.shape[0])
    gathered = gathered.reshape(data_count, tensor_count, -1)
    rows_here_all = xor_columns(routed, data_index, data_count)
    rows_a, rows_b = rows_here_all[:wave_rows], rows_here_all[wave_rows:]
    full_a = lax.all_gather(rows_a, "tensor", axis=0, tiled=True)
    full_b = lax.all_gather(rows_b, "tensor", axis=0, tiled=True)

    qk_shard = qkv_weight[:, :2].reshape(block, 2 * heads_local)
    vo_shard = jnp.concatenate([qkv_weight[:, 2], out_weight], 1)
    qk_shard, vo_shard = after((qk_shard, vo_shard), routed)
    qk_stacks = gather_step([(qk_shard, [0])], x_first[0])
    vo_stacks = gather_step([(vo_shard, [0])], y_first[0])
    for step in range(1, len(x_first)):
        qk_stacks = gather_step(qk_stacks, x_first[step])
        vo_stacks = gather_step(vo_stacks, y_first[step])

    def held_back(groups, *values):
        flat = [rows for stacks in groups for rows, _ in stacks]
        out = list(after(tuple(flat) + values))
        fresh = [[(out.pop(0), masks) for _, masks in stacks] for stacks in groups]
        return fresh, out

    (qk_stacks, vo_stacks), (fc1_shard, fc2_shard, row_ids) = held_back(
        (qk_stacks, vo_stacks), fc1_weight, fc2_weight, jnp.arange(seq_len, dtype=jnp.int32)
    )
    qk = gather_plan(qk_stacks + core_copies(qk_stacks), block, bits)
    vo = gather_plan(vo_stacks + core_copies(vo_stacks), block, bits)
    fc1_stacks = gather_step([(fc1_shard, [0])], x_first[0])
    fc2_stacks = gather_step([(fc2_shard, [0])], y_first[0])

    positions = tensor_index * rows_here + jnp.arange(rows_here, dtype=jnp.int32)
    valid = (positions < length)[:, None]
    cot_plain, = after((cotangent[0],), routed)
    cot_rows = xor_columns(cot_plain, data_index, data_count)
    cot_a, cot_b = cot_rows[:wave_rows], cot_rows[wave_rows:]
    low = jnp.where(valid, cot_rows, jnp.zeros_like(cot_rows))
    low_a, low_b = low[:wave_rows], low[wave_rows:]
    grads_a, grads_b = after((low_a, low_b), rows_b)
    grads_a = lax.all_gather(grads_a, "tensor", axis=0, tiled=True)
    grads_b = lax.all_gather(grads_b, "tensor", axis=0, tiled=True)

    vectors = [
        xor_columns(gathered[:, :, i * s : (i + 1) * s].reshape(1, width), data_index, data_count)
        for i in range(4)
    ]
    gain, shift, bias_a, bias_b = [v.astype(f32) for v in vectors]
    q = qkv_bias.shape[0]
    bias_qkv = lax.dynamic_slice_in_dim(
        gathered[:, :, 4 * s : 4 * s + q].reshape(3, width), tensor_index * heads_local, heads_local, 1
    ).astype(f32)
    bias_fc1 = lax.dynamic_slice_in_dim(
        gathered[:, :, 4 * s + q :].reshape(1, hidden_local * tensor_count),
        tensor_index * hidden_local,
        hidden_local,
        1,
    ).astype(f32)

    tables = rotary_tables(row_ids, PAIR)
    wave_tables = [
        v.reshape(tensor_count, 2, wave_rows, PAIR).swapaxes(0, 1).reshape(seq_len, PAIR) for v in tables
    ]
    size = length.reshape(1)
    ln_a = norm_wave(full_a, gain, shift, 0, None)
    qkv_a, weights = project_first(ln_a, qk, vo, bias_qkv, wave_tables)
    (fc1_stacks, fc2_stacks), (weights,) = held_back((fc1_stacks, fc2_stacks), weights)
    fc1_far, fc2_far = core_copies(fc1_stacks), core_copies(fc2_stacks)
    for step in range(1, len(x_first)):
        fc1_stacks = gather_step(fc1_stacks, x_first[step])
        fc2_stacks = gather_step(fc2_stacks, y_first[step])
    (fc1_far, fc2_far), (ln_a, full_b, weights) = held_back(
        (fc1_far, fc2_far), ln_a, full_b, weights
    )
    ln = norm_wave(full_b, gain, shift, 1, ln_a)
    qkv = project_second(ln, weights, bias_qkv, wave_tables, qkv_a)
    attended = attend(qkv, size, chunks, 0, None)
    (fc1_stacks, fc2_stacks), attended = held_back((fc1_stacks, fc2_stacks), *attended)
    fc1_far = fc1_far + core_copies(fc1_stacks[2:])
    fc2_far = fc2_far + core_copies(fc2_stacks[2:])
    mixed, totals = attend(qkv, size, chunks, 1, attended)
    w1 = gather_plan(fc1_stacks + fc1_far, block, bits)
    w2 = gather_plan(fc2_stacks + fc2_far, block, bits)
    branch_a, branch_b, hidden, slope, full1, full2 = feed(
        ln, mixed, weights, w1, w2, bias_fc1, tile_f
    )

    count = data_count // 2
    steps = len(x_first)
    x_rule = lambda step: (1 << (steps - step), False)
    y_rule = lambda step: (1 << (steps - step), True)
    feed_a, *waves, bias_a1 = back_rows(grads_a, full1, full2, slope, weights, tile_f, 0, None)
    waves, grads_b, branch_a, branch_b = after((waves, grads_b, branch_a, branch_b))
    branch_a = lax.psum_scatter(branch_a, "tensor", scatter_dimension=0, tiled=True)
    branch_b = lax.psum_scatter(branch_b, "tensor", scatter_dimension=0, tiled=True)
    feed_b, grad_pre, grad_mixed, grads, bias_b1 = back_rows(
        grads_b, full1, full2, slope, weights, tile_f, 1, waves
    )
    grad_fc1_b = bias_a1 + bias_b1
    k2, s2 = feed_weight(grads, hidden, tile_f)
    f2 = flip(s2, "dp", 0)
    grad_pre, = after((grad_pre,), s2)
    k1, s1 = feed_weight(ln, grad_pre, tile_f)
    f1 = flip(s1, "dp", 0)
    k2, f2 = after((k2, f2), s1)
    give2, hold2 = merge(k2, f2, y_rule(0))
    f2 = flip(give2, "dp", y_first[0])
    k1, f1 = after((k1, f1), give2)
    give1, hold1 = merge(k1, f1, x_rule(0))
    f1 = flip(give1, "dp", x_first[0])
    grad_mixed, = after((grad_mixed,), give1)
    grad_qkv = attend_back(qkv, grad_mixed, totals, size, tables, chunks)
    kqk, kvo, sqk, svo, grad_qkv_b = weight_grad(ln, grads, grad_qkv, mixed)
    fq, fv = flip(sqk, "dp", 0), flip(svo, "dp", 0)
    grad_qkv, branch_a, branch_b, f2, f1 = after((grad_qkv, branch_a, branch_b, f2, f1), sqk)
    part_a = ln_grad(grad_qkv, weights, feed_a, 0)
    sum_a = lax.psum_scatter(part_a, "tensor", scatter_dimension=0, tiled=True)
    later_sum, = after((feed_b,), part_a)
    part_b = ln_grad(grad_qkv, weights, later_sum, 1)
    sum_b = lax.psum_scatter(part_b, "tensor", scatter_dimension=0, tiled=True)
    hold2, f2, hold1, f1, fq, fv = after((hold2, f2, hold1, f1, fq, fv), part_b)

    def all_steps(held, arrived, rule, order):
        give = held
        for step in range(1, steps):
            give, held = merge(held, arrived, rule(step))
            arrived = flip(give, "dp", order[step])
        return held, arrived, give

    hold2, f2, give2 = all_steps(hold2, f2, y_rule, y_first)
    hold1, f1, give1 = all_steps(hold1, f1, x_rule, x_first)
    kqk, kvo = after((kqk, kvo), give2, give1)
    giveq, holdq = merge(kqk, fq, x_rule(0))
    givev, holdv = merge(kvo, fv, y_rule(0))
    fq, fv = flip(giveq, "dp", x_first[0]), flip(givev, "dp", y_first[0])
    sum_a, f2, f1 = after((sum_a, f2, f1), giveq, givev)

    slots_f32 = [r.astype(f32) for r in (rows_a, rows_b)]
    slot_a, gain_a, shift_a = norm_back(sum_a, rows_a, cot_a, gain, data_index, data_count)
    back_a = send(slot_a)
    holdq, fq, holdv, fv = after((holdq, fq, holdv, fv), slot_a)
    holdq, fq, giveq = all_steps(holdq, fq, x_rule, x_first)
    holdv, fv, givev = all_steps(holdv, fv, y_rule, y_first)
    input_a = receive(back_a, slot_of_seq)
    sum_b, input_a = after((sum_b, input_a), giveq, givev)
    slot_b, gain_b, shift_b = norm_back(sum_b, rows_b, cot_b, gain, data_index, data_count)
    back_b = send(slot_b)
    hold1, f1, hold2, f2, holdq, fq, holdv, fv, back_b, gain_b, shift_b = after(
        (hold1, f1, hold2, f2, holdq, fq, holdv, fv, back_b, gain_b, shift_b)
    )
    input_b = receive(back_b, slot_of_seq)
    grad_input = jnp.concatenate([input_a, input_b], 0)[None]
    grad_gain, grad_shift = (gain_a + gain_b)[0], (shift_a + shift_b)[0]

    def final(held, arrived):
        return held.astype(f32) + arrived.astype(f32)

    grad_fc1_w, grad_fc2_w = final(hold1, f1), final(hold2, f2)
    grad_qk_w, grad_vo_w = final(holdq, fq), final(holdv, fv)
    grad_out_w = grad_vo_w[:, heads_local:]
    grad_qkv_w = jnp.stack(
        [grad_qk_w[:, :heads_local], grad_qk_w[:, heads_local:], grad_vo_w[:, :heads_local]], 1
    )
    branch = jnp.concatenate([branch_a, branch_b], 0).astype(f32) + bias_a + bias_b
    block_out = jnp.concatenate(slots_f32, 0) + jnp.where(valid, branch, 0.0)
    block_out = plain_columns(block_out.astype(bf16), data_index, data_count)[None]
    grad_bias = jnp.sum(low_a.astype(f32), axis=0) + jnp.sum(low_b.astype(f32), axis=0)

    devices = data_count * tensor_count
    full_qkv_b = lax.dynamic_update_slice_in_dim(
        jnp.zeros((3, width), f32), grad_qkv_b[:, 0], tensor_index * heads_local, 1
    )
    full_fc1_b = lax.dynamic_update_slice_in_dim(
        jnp.zeros((hidden_local * tensor_count,), f32), grad_fc1_b[0], tensor_index * hidden_local, 0
    )
    sums = jnp.concatenate(
        [
            plain_columns(v, data_index, data_count).reshape(devices, s)
            for v in (grad_gain, grad_shift, grad_bias)
        ]
        + [full_qkv_b.reshape(devices, q), full_fc1_b.reshape(devices, -1)],
        1,
    )
    total = scatter_small(sums, data_index, tensor_index)
    return (
        block_out,
        grad_input,
        grad_qkv_w,
        grad_out_w,
        grad_fc1_w,
        grad_fc2_w,
        total[:s],
        total[s : 2 * s],
        total[3 * s : 3 * s + q],
        total[2 * s : 3 * s],
        total[3 * s + q :],
        total[2 * s : 3 * s],
    )


def solution(mesh):
    in_specs = (
        P("dp", "tensor", None),
        P("dp", "tensor", None),
        P(),
        P(),
        P(),
        P("dp", None, "tensor"),
        P("dp", "tensor"),
        P("dp", "tensor"),
        P("dp", "tensor"),
        P(("dp", "tensor")),
        P(("dp", "tensor")),
        P(("dp", "tensor")),
        P(("dp", "tensor")),
        P(("dp", "tensor")),
        P(("dp", "tensor")),
    )
    out_specs = (
        P("dp", "tensor", None),
        P("dp", "tensor", None),
        P("dp", None, "tensor"),
        P("dp", "tensor"),
        P("dp", "tensor"),
        P("dp", "tensor"),
        P(("dp", "tensor")),
        P(("dp", "tensor")),
        P(("dp", "tensor")),
        P(("dp", "tensor")),
        P(("dp", "tensor")),
        P(("dp", "tensor")),
    )
    return jax.shard_map(shards, mesh=mesh, in_specs=in_specs, out_specs=out_specs, check_vma=False)
```

```python
import functools
import math

import jax
import jax.numpy as jnp
from jax import lax
from jax.experimental import pallas as pl
from jax.experimental.pallas import tpu as pltpu
from jax.sharding import PartitionSpec as P

HEAD_DIM = 64
ROT = 32
PAIR = 2 * HEAD_DIM
VMEM = 63 * 1024 * 1024
SHARE = 0.4


eps = 1e-05
masked_score = -1e30
f32 = jnp.float32
bf16 = jnp.bfloat16
NN = (((1,), (0,)), ((), ()))
NT = (((1,), (1,)), ((), ()))
TN = (((0,), (0,)), ((), ()))
once = pl.Buffered(1)


def dot(a, b, dims):
    return lax.dot_general(a, b, dims, preferred_element_type=f32)


def params(mib):
    return pltpu.CompilerParams(vmem_limit_bytes=VMEM)


def cost(flops, nbytes, exps=0):
    return pl.CostEstimate(
        flops=int(flops * SHARE), bytes_accessed=int(nbytes * SHARE), transcendentals=int(exps * SHARE)
    )


def shape(dims, dtype):
    return jax.ShapeDtypeStruct(dims, dtype)


def turned(field, tables):
    cosine, ahead, behind = tables
    half = ROT // 2
    wide = field.shape[1]
    return (
        field * cosine
        + pltpu.roll(field, wide - half, 1) * ahead
        + pltpu.roll(field, half, 1) * behind
    )


def turned_back(grad, tables):
    cosine, ahead, behind = tables
    half = ROT // 2
    wide = grad.shape[1]
    return (
        grad * cosine
        + pltpu.roll(grad * ahead, half, 1)
        + pltpu.roll(grad * behind, wide - half, 1)
    )


def norm_kernel(blocks, at_ref, x_ref, gain_ref, shift_ref, *rest):
    out_ref, plain = rest[-2:]
    rows = x_ref[...].astype(f32)
    centred = rows - jnp.mean(rows, -1, keepdims=True)
    scale = lax.rsqrt(jnp.mean(centred * centred, -1, keepdims=True) + eps)
    plain[...] = (centred * scale * gain_ref[...] + shift_ref[...]).astype(bf16)
    wide = plain.shape[1] // blocks
    bits = blocks.bit_length() - 1
    for p in range(blocks):
        place = (at_ref[1] ^ reversed_bits(p, bits)) * wide
        out_ref[0, 0, :, p * wide : (p + 1) * wide] = plain[:, pl.ds(pl.multiple_of(place, wide), wide)]


def norm_wave(rows_in, count, at, gain, shift, blocks, wave, held):
    rows, width = rows_in.shape[0] // count, rows_in.shape[1]
    vector = pl.BlockSpec((1, width), lambda j, n: (0, 0))
    extra = [] if held is None else [held]
    return pl.pallas_call(
        functools.partial(norm_kernel, blocks),
        grid_spec=pltpu.PrefetchScalarGridSpec(
            num_scalar_prefetch=1,
            grid=(count,),
            in_specs=[pl.BlockSpec((rows, width), lambda j, n: (j, 0)), vector, vector]
            + [pl.BlockSpec(memory_space=pl.ANY)] * len(extra),
            out_specs=pl.BlockSpec((1, 1, rows, width), lambda j, n: (j, wave, 0, 0)),
            scratch_shapes=[pltpu.VMEM((rows, width), bf16)],
        ),
        out_shape=shape((count, 2, rows, width), bf16),
        input_output_aliases={4: 0} if extra else {},
        compiler_params=params(32),
        cost_estimate=cost(10 * count * rows * width, 4 * count * rows * width),
        name="norm_wave",
    )(at, rows_in, gain, shift, *extra)


def project_rows(kind, ln_ref, weight, bias_ref, tables, out_ref):
    rows = ln_ref.shape[0] * ln_ref.shape[2]
    many, size = ln_ref.shape[0], ln_ref.shape[2]
    raw = dot(ln_ref[...].reshape(rows, ln_ref.shape[3]), weight, NN) + bias_ref[0]

    @pl.when(kind < 2)
    def _():
        here = [t[...].reshape(rows, PAIR) for t in tables]
        for pair in range(raw.shape[1] // PAIR):
            cols = slice(pair * PAIR, (pair + 1) * PAIR)
            out_ref[0, :, 0, :, cols] = (
                turned(raw[:, cols], here).astype(bf16).reshape(many, size, PAIR)
            )

    @pl.when(kind == 2)
    def _():
        out_ref[0, :, 0] = raw.astype(bf16).reshape(many, size, raw.shape[1])


def assemble_start(refs, plan, column, size, buffer, sems):
    for j, (which, row, place, count) in enumerate(plan):
        pltpu.make_async_copy(
            refs[which].at[pl.ds(row, count), pl.ds(column, size)],
            buffer.at[pl.ds(place, count), :],
            sems.at[j],
        ).start()


def assemble_wait(refs, plan, column, size, buffer, sems):
    for j, (which, row, place, count) in enumerate(plan):
        pltpu.make_async_copy(
            refs[which].at[pl.ds(row, count), pl.ds(column, size)],
            buffer.at[pl.ds(place, count), :],
            sems.at[j],
        ).wait()


def project_first_kernel(qk_plan, vo_plan, ln_ref, bias_ref, c_ref, a_ref, b_ref, *rest):
    n = len({p[0] for p in qk_plan})
    qk_refs, vo_refs = rest[:n], rest[n : 2 * n]
    out_ref, w_ref, buffer, sems, out_sems = rest[2 * n :]
    kind = pl.program_id(0)
    heads = buffer.shape[2]
    sources = (
        (qk_refs, qk_plan, 0),
        (qk_refs, qk_plan, heads),
        (vo_refs, vo_plan, 0),
        (vo_refs, vo_plan, heads),
    )

    def drain(k):
        pltpu.make_async_copy(buffer.at[k % 2], w_ref.at[k], out_sems.at[k % 2]).wait()

    for k in range(4):
        refs, plan, column = sources[k]
        slot = k % 2

        @pl.when(kind == k)
        def _():
            if k == 0:
                assemble_start(refs, plan, column, heads, buffer.at[slot], sems.at[slot])
            assemble_wait(refs, plan, column, heads, buffer.at[slot], sems.at[slot])
            pltpu.make_async_copy(buffer.at[slot], w_ref.at[k], out_sems.at[slot]).start()
            if k >= 1:
                drain(k - 1)
            if k < 3:
                nrefs, nplan, ncolumn = sources[k + 1]
                assemble_start(
                    nrefs, nplan, ncolumn, heads, buffer.at[1 - slot], sems.at[1 - slot]
                )
            else:
                drain(k)

    @pl.when(kind < 3)
    def _():
        project_rows(kind, ln_ref, buffer[kind % 2], bias_ref, (c_ref, a_ref, b_ref), out_ref)


def project_first(ln, qk, vo, bias, tables):
    many, _, size, width = ln.shape
    heads = bias.shape[1]
    table = pl.BlockSpec((many, 1, size, PAIR), lambda i: (0, 0, 0, 0), pipeline_mode=once)
    hbm = pl.BlockSpec(memory_space=pl.ANY)
    last = lambda i: jnp.minimum(i, 2)
    return pl.pallas_call(
        functools.partial(project_first_kernel, qk[1], vo[1]),
        grid=(4,),
        in_specs=[
            pl.BlockSpec((many, 1, size, width), lambda i: (0, 0, 0, 0), pipeline_mode=once),
            pl.BlockSpec((1, 1, heads), lambda i: (last(i), 0, 0)),
            table,
            table,
            table,
        ]
        + [hbm] * (len(qk[0]) + len(vo[0])),
        out_specs=[
            pl.BlockSpec((1, many, 1, size, heads), lambda i: (last(i), 0, 0, 0, 0)),
            hbm,
        ],
        out_shape=[shape((3, many, 2, size, heads), bf16), shape((4, width, heads), bf16)],
        scratch_shapes=[
            pltpu.VMEM((2, width, heads), bf16),
            pltpu.SemaphoreType.DMA((2, len(qk[1]))),
            pltpu.SemaphoreType.DMA((2,)),
        ],
        compiler_params=params(48),
        cost_estimate=cost(6 * many * size * width * heads, 22 << 20),
        name="project_first",
    )(ln, bias[:, None, :], *tables, *qk[0], *vo[0])


def project_second_kernel(ln_ref, w_ref, bias_ref, c_ref, a_ref, b_ref, held_ref, out_ref):
    project_rows(pl.program_id(0), ln_ref, w_ref[0], bias_ref, (c_ref, a_ref, b_ref), out_ref)


def project_second(ln, weights, bias, tables, held):
    many, _, size, width = ln.shape
    heads = bias.shape[1]
    table = pl.BlockSpec((many, 1, size, PAIR), lambda i: (0, 1, 0, 0), pipeline_mode=once)
    return pl.pallas_call(
        project_second_kernel,
        grid=(3,),
        in_specs=[
            pl.BlockSpec((many, 1, size, width), lambda i: (0, 1, 0, 0), pipeline_mode=once),
            pl.BlockSpec((1, width, heads), lambda i: (i, 0, 0)),
            pl.BlockSpec((1, 1, heads), lambda i: (i, 0, 0)),
            table,
            table,
            table,
            pl.BlockSpec(memory_space=pl.ANY),
        ],
        out_specs=pl.BlockSpec((1, many, 1, size, heads), lambda i: (i, 0, 1, 0, 0)),
        out_shape=shape(held.shape, bf16),
        input_output_aliases={6: 0},
        compiler_params=params(48),
        cost_estimate=cost(6 * many * size * width * heads, 12 << 20),
        name="project_second",
    )(ln, weights, bias[:, None, :], *tables, held)


def head_lanes(head):
    lane = lax.broadcasted_iota(jnp.int32, (1, PAIR), 1)
    return (lane // HEAD_DIM) == (head % 2)


def masked_scores(keys, queries, first, length):
    scores = dot(keys, queries, NT)
    key = lax.broadcasted_iota(jnp.int32, scores.shape, 0)
    row = first + lax.broadcasted_iota(jnp.int32, (1, scores.shape[1]), 1)
    return jnp.where(key <= jnp.minimum(row, length - 1), scores, masked_score)


def attend_kernel(block, len_ref, q_ref, k_ref, v_ref, out_ref, total_ref, q_mine, v_turned):
    head = pl.program_id(0)
    lanes = head_lanes(head)
    rows = q_ref.shape[1]
    zero = jnp.zeros((rows, PAIR), bf16)
    scale = jnp.asarray(1.0 / math.sqrt(HEAD_DIM), bf16)
    q_mine[...] = jnp.where(lanes, q_ref[0] * scale, zero)
    v_turned[...] = jnp.where(lanes, v_ref[0], zero).T
    length = len_ref[0]
    for first in range(0, rows, block):
        n = first + block
        r = slice(first, n)
        scores = masked_scores(k_ref[0, :n, :], q_mine[r, :], first, length)
        top = jnp.max(scores, 0, keepdims=True)
        exped = jnp.exp(scores - top)
        total = jnp.sum(exped, 0, keepdims=True)
        mixed = dot(v_turned[:, :n], exped.astype(bf16), NN) * (1.0 / total)
        mixed = mixed.T.astype(bf16)
        total_ref[0, :, r] = top + jnp.log(total)

        @pl.when(head % 2 == 0)
        def _():
            out_ref[r, :] = mixed

        @pl.when(head % 2 == 1)
        def _():
            out_ref[r, :] = out_ref[r, :] + mixed


def attend(qkv, length):
    _, rows, width = qkv.shape
    heads = width // HEAD_DIM
    kind = lambda c: pl.BlockSpec((1, rows, PAIR), lambda h, n: (c, 0, h // 2))
    return pl.pallas_call(
        functools.partial(attend_kernel, min(512, rows)),
        grid_spec=pltpu.PrefetchScalarGridSpec(
            num_scalar_prefetch=1,
            grid=(heads,),
            in_specs=[kind(0), kind(1), kind(2)],
            out_specs=[
                pl.BlockSpec((rows, PAIR), lambda h, n: (0, h // 2)),
                pl.BlockSpec((1, 1, rows), lambda h, n: (h, 0, 0)),
            ],
            scratch_shapes=[pltpu.VMEM((rows, PAIR), bf16), pltpu.VMEM((PAIR, rows), bf16)],
        ),
        out_shape=[shape((rows, width), bf16), shape((heads, 1, rows), f32)],
        compiler_params=params(48),
        cost_estimate=cost(16 * rows * rows * width, 4 << 20, rows * rows * heads),
        name="attend",
    )(length, qkv, qkv, qkv)


def attend_back_kernel(
    block, len_ref, q_ref, k_ref, v_ref, do_ref, total_ref, c_ref, a_ref, b_ref,
    grad_ref, q_mine, do_mine, k_turned, key_sum, value_sum,
):
    head = pl.program_id(0)
    lanes = head_lanes(head)
    rows = q_ref.shape[1]
    zero = jnp.zeros((rows, PAIR), bf16)
    scale = 1.0 / math.sqrt(HEAD_DIM)
    q_mine[...] = jnp.where(lanes, q_ref[0] * jnp.asarray(scale, bf16), zero)
    do_mine[...] = jnp.where(lanes, do_ref[...], zero)
    k_turned[...] = jnp.where(lanes, k_ref[0], zero).T
    length = len_ref[0]

    def put(kind, r, value):
        value = value.astype(bf16)

        @pl.when(head % 2 == 0)
        def _():
            grad_ref[kind, r, :] = value

        @pl.when(head % 2 == 1)
        def _():
            grad_ref[kind, r, :] = grad_ref[kind, r, :] + value

    tables_of = lambda r: (c_ref[r, :], a_ref[r, :], b_ref[r, :])
    for first in range(rows - block, -1, -block):
        n = first + block
        r = slice(first, n)
        scores = masked_scores(k_ref[0, :n, :], q_mine[r, :], first, length)
        probs = jnp.exp(scores - total_ref[0, :, r])
        grad_probs = dot(v_ref[0, :n, :], do_mine[r, :], NT)
        product = probs * grad_probs
        delta = jnp.sum(product, 0, keepdims=True)
        grad_scores = (product - probs * delta).astype(bf16)
        keys = dot(grad_scores, q_mine[r, :], NN)
        vals = dot(probs.astype(bf16), do_mine[r, :], NN)
        if n == rows:
            key_sum[...] = keys
            value_sum[...] = vals
        else:
            key_sum[:n, :] += keys
            value_sum[:n, :] += vals
        grad_query = dot(k_turned[:, :n], grad_scores, NN).T * scale
        put(0, r, turned_back(grad_query, tables_of(r)))
    for first in range(0, rows, block):
        r = slice(first, first + block)
        put(1, r, turned_back(key_sum[r, :], tables_of(r)))
        put(2, r, value_sum[r, :])


def attend_back(qkv, grad_mixed, totals, length, tables):
    _, rows, width = qkv.shape
    heads = width // HEAD_DIM
    kind = lambda c: pl.BlockSpec((1, rows, PAIR), lambda h, n: (c, 0, h // 2))
    table_spec = pl.BlockSpec((rows, PAIR), lambda h, n: (0, 0))
    return pl.pallas_call(
        functools.partial(attend_back_kernel, min(512, rows)),
        grid_spec=pltpu.PrefetchScalarGridSpec(
            num_scalar_prefetch=1,
            grid=(heads,),
            in_specs=[
                kind(0),
                kind(1),
                kind(2),
                pl.BlockSpec((rows, PAIR), lambda h, n: (0, h // 2)),
                pl.BlockSpec((1, 1, rows), lambda h, n: (h, 0, 0)),
                table_spec,
                table_spec,
                table_spec,
            ],
            out_specs=pl.BlockSpec((3, rows, PAIR), lambda h, n: (0, 0, h // 2)),
            scratch_shapes=[
                pltpu.VMEM((rows, PAIR), bf16),
                pltpu.VMEM((rows, PAIR), bf16),
                pltpu.VMEM((PAIR, rows), bf16),
                pltpu.VMEM((rows, PAIR), f32),
                pltpu.VMEM((rows, PAIR), f32),
            ],
        ),
        out_shape=shape((3, rows, width), bf16),
        compiler_params=params(48),
        cost_estimate=cost(40 * rows * rows * width, 8 << 20, rows * rows * heads),
        name="attend_back",
    )(length, qkv, qkv, qkv, grad_mixed, totals, *tables)


def feed_kernel(tile, tile_f, steps, plan1, plan2, ln_ref, mixed_ref, wo_ref, bias_ref, *rest):
    n1 = len({p[0] for p in plan1})
    w1_refs, w2_refs = rest[:n1], rest[n1 : 2 * n1]
    (branch_ref, hidden_ref, slope_ref, full1_ref, full2_ref, acc, buf1, buf2, sems1, sems2,
     out_sems) = rest[2 * n1 :]
    step = pl.program_id(0)
    slot = lax.rem(step, 2)
    rows = ln_ref.shape[0]
    c0 = math.sqrt(2.0 / math.pi)
    c1 = 0.044715

    def start(s, at):
        column = pl.multiple_of(s * tile_f, tile_f)
        assemble_start(w1_refs, plan1, column, tile_f, buf1.at[at], sems1.at[at])
        assemble_start(w2_refs, plan2, column, tile_f, buf2.at[at], sems2.at[at])

    def outward(s, at):
        column = pl.multiple_of(s * tile_f, tile_f)
        return (
            pltpu.make_async_copy(
                buf1.at[at], full1_ref.at[:, pl.ds(column, tile_f)], out_sems.at[at, 0]
            ),
            pltpu.make_async_copy(
                buf2.at[at], full2_ref.at[:, pl.ds(column, tile_f)], out_sems.at[at, 1]
            ),
        )

    @pl.when(step == 0)
    def _():
        start(0, 0)

    column = pl.multiple_of(step * tile_f, tile_f)
    assemble_wait(w1_refs, plan1, column, tile_f, buf1.at[slot], sems1.at[slot])
    assemble_wait(w2_refs, plan2, column, tile_f, buf2.at[slot], sems2.at[slot])
    for copy in outward(step, slot):
        copy.start()

    @pl.when(step > 0)
    def _():
        for copy in outward(step - 1, 1 - slot):
            copy.wait()

    @pl.when(step < steps - 1)
    def _():
        start(step + 1, 1 - slot)

    for first in range(0, rows, tile):
        r = slice(first, first + tile)
        pre = dot(ln_ref[r, :], buf1[slot], NN) + bias_ref[...]
        square = pre * pre
        bent = jnp.tanh(c0 * (pre + c1 * (square * pre)))
        half_pre = 0.5 * pre
        hidden = (half_pre * (1.0 + bent)).astype(bf16)
        hidden_ref[r, :] = hidden
        slope_ref[r, :] = 0.5 * (1.0 + bent) + half_pre * (1.0 - bent * bent) * (
            c0 * (1.0 + (3.0 * c1) * square)
        )

    for first in range(0, rows, tile):
        r = slice(first, first + tile)
        part = dot(hidden_ref[r, :], buf2[slot], NT)

        @pl.when(step == 0)
        def _():
            acc[r, :] = part + dot(mixed_ref[r, :], wo_ref[0], NT)

        @pl.when((step > 0) & (step < steps - 1))
        def _():
            acc[r, :] += part

        @pl.when(step == steps - 1)
        def _():
            branch_ref[r, :] = (acc[r, :] + part).astype(bf16)

    @pl.when(step == steps - 1)
    def _():
        for copy in outward(step, slot):
            copy.wait()


def feed(ln, mixed, weights, w1, w2, bias, tile_f):
    rows, width = ln.shape
    hidden = bias.shape[1]
    heads = mixed.shape[1]
    steps = hidden // tile_f
    whole = lambda dims: pl.BlockSpec(dims, lambda i: (0, 0), pipeline_mode=once)
    by_row = pl.BlockSpec((rows, tile_f), lambda i: (0, i))
    hbm = pl.BlockSpec(memory_space=pl.ANY)
    return pl.pallas_call(
        functools.partial(feed_kernel, rows // 2, tile_f, steps, w1[1], w2[1]),
        grid=(steps,),
        in_specs=[
            whole((rows, width)),
            whole((rows, heads)),
            pl.BlockSpec((1, width, heads), lambda i: (3, 0, 0), pipeline_mode=once),
            pl.BlockSpec((1, tile_f), lambda i: (0, i)),
        ]
        + [hbm] * (len(w1[0]) + len(w2[0])),
        out_specs=[whole((rows, width)), by_row, by_row, hbm, hbm],
        out_shape=[
            shape((rows, width), bf16),
            shape((rows, hidden), bf16),
            shape((rows, hidden), f32),
            shape((width, hidden), bf16),
            shape((width, hidden), bf16),
        ],
        scratch_shapes=[
            pltpu.VMEM((rows, width), f32),
            pltpu.VMEM((2, width, tile_f), bf16),
            pltpu.VMEM((2, width, tile_f), bf16),
            pltpu.SemaphoreType.DMA((2, len(w1[1]))),
            pltpu.SemaphoreType.DMA((2, len(w2[1]))),
            pltpu.SemaphoreType.DMA((2, 2)),
        ],
        compiler_params=params(58),
        cost_estimate=cost(4 * rows * width * hidden, 56 << 20, rows * hidden),
        name="feed",
    )(ln, mixed, weights, bias, *w1[0], *w2[0])


def back_kernel(tile, g_ref, w1_ref, w2_ref, slope_ref, wo_ref, sum_ref, pre_ref, mixed_ref, bias_ref):
    step = pl.program_id(0)
    rows = g_ref.shape[0]

    @pl.when(step == 0)
    def _():
        mixed_ref[...] = dot(g_ref[...], wo_ref[0], NN).astype(bf16)

    for first in range(0, rows, tile):
        r = slice(first, first + tile)
        pre_ref[r, :] = (dot(g_ref[r, :], w2_ref[...], NN) * slope_ref[r, :]).astype(bf16)

    bias_ref[...] = jnp.sum(pre_ref[...].astype(f32), axis=0, keepdims=True)
    for first in range(0, rows, tile):
        r = slice(first, first + tile)
        part = dot(pre_ref[r, :], w1_ref[...], NT)

        @pl.when(step == 0)
        def _():
            sum_ref[r, :] = part

        @pl.when(step > 0)
        def _():
            sum_ref[r, :] += part


def back(grads, w1, w2, slope, weights, tile_f):
    rows, width = grads.shape
    units = slope.shape[1]
    heads = weights.shape[2]
    weight = pl.BlockSpec((width, tile_f), lambda i: (0, i))
    whole = lambda dims: pl.BlockSpec(dims, lambda i: (0, 0), pipeline_mode=once)
    by_row = pl.BlockSpec((rows, tile_f), lambda i: (0, i))
    return pl.pallas_call(
        functools.partial(back_kernel, min(512, rows)),
        grid=(units // tile_f,),
        in_specs=[
            whole((rows, width)),
            weight,
            weight,
            by_row,
            pl.BlockSpec((1, width, heads), lambda i: (3, 0, 0), pipeline_mode=once),
        ],
        out_specs=[
            whole((rows, width)),
            by_row,
            whole((rows, heads)),
            pl.BlockSpec((1, tile_f), lambda i: (0, i)),
        ],
        out_shape=[
            shape((rows, width), f32),
            shape((rows, units), bf16),
            shape((rows, heads), bf16),
            shape((1, units), f32),
        ],
        compiler_params=params(58),
        cost_estimate=cost(4 * rows * width * units, 40 << 20),
        name="back",
    )(grads, w1, w2, slope, weights)


def feed_weight_kernel(left_ref, right_ref, near_ref, far_ref):
    half = left_ref.shape[1] // 2
    far_ref[...] = dot(left_ref[:, half:], right_ref[...], TN).astype(bf16)
    near_ref[...] = dot(left_ref[:, :half], right_ref[...], TN).astype(bf16)


def feed_weight(left, right, tile_f):
    rows, width = left.shape
    units = right.shape[1]
    half = pl.BlockSpec((width // 2, tile_f), lambda i: (0, i))
    return pl.pallas_call(
        feed_weight_kernel,
        grid=(units // tile_f,),
        in_specs=[
            pl.BlockSpec((rows, width), lambda i: (0, 0), pipeline_mode=once),
            pl.BlockSpec((rows, tile_f), lambda i: (0, i)),
        ],
        out_specs=[half, half],
        out_shape=[shape((width // 2, units), bf16)] * 2,
        compiler_params=params(48),
        cost_estimate=cost(2 * rows * width * units, 16 << 20),
        name="feed_weight",
    )(left, right)


def ln_grad_kernel(grad_ref, w_ref, sum_ref, out_ref):
    total = sum_ref[...]
    for kind in range(3):
        total += dot(grad_ref[kind], w_ref[kind], NT)
    out_ref[...] = total.astype(bf16)


def ln_grad(grad_qkv, weights, partial_sum):
    _, rows, heads = grad_qkv.shape
    width = partial_sum.shape[1]
    tile = min(512, rows)
    return pl.pallas_call(
        ln_grad_kernel,
        grid=(rows // tile,),
        in_specs=[
            pl.BlockSpec((3, tile, heads), lambda i: (0, i, 0)),
            pl.BlockSpec((3, width, heads), lambda i: (0, 0, 0), pipeline_mode=once),
            pl.BlockSpec((tile, width), lambda i: (i, 0)),
        ],
        out_specs=pl.BlockSpec((tile, width), lambda i: (i, 0)),
        out_shape=shape((rows, width), bf16),
        compiler_params=params(48),
        cost_estimate=cost(6 * rows * width * heads, 22 << 20),
        name="ln_grad",
    )(grad_qkv, weights, partial_sum)


def weight_grad_kernel(ln_ref, g_ref, grad_ref, mixed_ref, kqk_ref, kvo_ref, sqk_ref, svo_ref, bias_ref):
    heads = mixed_ref.shape[1]
    step = pl.program_id(0)
    steps = pl.num_programs(0)
    for kind in range(3):
        @pl.when(step == 0)
        def _():
            bias_ref[kind] = jnp.sum(grad_ref[kind].astype(f32), axis=0, keepdims=True)

    for qk_ref, vo_ref, here in ((kqk_ref, kvo_ref, step < steps // 2), (sqk_ref, svo_ref, step >= steps // 2)):
        @pl.when(here)
        def _():
            qk_ref[:, :heads] = dot(ln_ref[...], grad_ref[0], TN).astype(bf16)
            qk_ref[:, heads:] = dot(ln_ref[...], grad_ref[1], TN).astype(bf16)
            vo_ref[:, :heads] = dot(ln_ref[...], grad_ref[2], TN).astype(bf16)
            vo_ref[:, heads:] = dot(g_ref[...], mixed_ref[...], TN).astype(bf16)


def weight_grad(ln, grads, grad_qkv, mixed):
    rows, width = ln.shape
    heads = mixed.shape[1]
    half = width // 2
    tile = min(512, half)
    near = half // tile
    column = pl.BlockSpec((rows, tile), lambda i: (0, i))
    kept = pl.BlockSpec((tile, 2 * heads), lambda i: (jnp.minimum(i, near - 1), 0))
    sent = pl.BlockSpec((tile, 2 * heads), lambda i: (jnp.maximum(i - near, 0), 0))
    return pl.pallas_call(
        weight_grad_kernel,
        grid=(2 * near,),
        in_specs=[
            column,
            column,
            pl.BlockSpec((3, rows, heads), lambda i: (0, 0, 0), pipeline_mode=once),
            pl.BlockSpec((rows, heads), lambda i: (0, 0), pipeline_mode=once),
        ],
        out_specs=[kept, kept, sent, sent, pl.BlockSpec((3, 1, heads), lambda i: (0, 0, 0))],
        out_shape=[shape((half, 2 * heads), bf16)] * 4 + [shape((3, 1, heads), f32)],
        compiler_params=params(48),
        cost_estimate=cost(8 * rows * width * heads, 20 << 20),
        name="weight_grad",
    )(ln, grads, grad_qkv, mixed)


def give_kernel(*refs):
    total = refs[0][...].astype(f32)
    for ref in refs[1:-1]:
        total += ref[...].astype(f32)
    refs[-1][...] = total.astype(bf16)


def give(full, partial_sums, count, low, part=(0, 1)):
    rows, width = full[0].shape[0], full[0].shape[1] // part[1]
    block = rows // count
    level = len(partial_sums) + 1
    out_count = count >> level
    wide = min(1024, width)
    off = part[0] * (width // wide)
    place = (lambda i: (2 * i + 1) << (level - 1)) if low else (lambda i: out_count + i)
    spec = lambda k, o: pl.BlockSpec(
        (block, wide), lambda i, j: (place(i) >> k if low else place(i), j + o)
    )
    return pl.pallas_call(
        give_kernel,
        grid=(out_count, width // wide),
        in_specs=[spec(0, off) for _ in full] + [spec(k + 1, 0) for k in range(level - 1)],
        out_specs=pl.BlockSpec((block, wide), lambda i, j: (i, j)),
        out_shape=shape((out_count * block, width), bf16),
        compiler_params=params(32),
        cost_estimate=cost(out_count * block * width * 2, 6 * out_count * block * width),
        name="give",
    )(*full, *partial_sums)


def norm_back_kernel(
    blocks, at_ref, sum_ref, rows_ref, cot_ref, gain_ref, out_ref, gain_sum_ref, shift_sum_ref, held
):
    wide = rows_ref.shape[1] // blocks
    bits = blocks.bit_length() - 1
    for q in range(blocks):
        place = pl.multiple_of(reversed_bits(at_ref[1] ^ q, bits) * wide, wide)
        held[:, q * wide : (q + 1) * wide] = sum_ref[:, pl.ds(place, wide)]
    grad_ln = held[...].astype(f32)
    rows = rows_ref[...].astype(f32)
    centred = rows - jnp.mean(rows, -1, keepdims=True)
    inv_scale = lax.rsqrt(jnp.mean(centred * centred, -1, keepdims=True) + eps)
    normed = centred * inv_scale
    grad_norm = grad_ln * gain_ref[...]
    back = inv_scale * (
        grad_norm
        - jnp.mean(grad_norm, -1, keepdims=True)
        - normed * jnp.mean(grad_norm * normed, -1, keepdims=True)
    )
    out_ref[...] = (cot_ref[...].astype(f32) + back).astype(bf16)
    gain_sum_ref[...] = jnp.sum(grad_ln * normed, 0, keepdims=True)
    shift_sum_ref[...] = jnp.sum(grad_ln, 0, keepdims=True)


def norm_back(total, rows_in, cot, gain, at, blocks):
    rows, width = rows_in.shape
    whole = pl.BlockSpec((rows, width), lambda i, n: (0, 0))
    vector = pl.BlockSpec((1, width), lambda i, n: (0, 0))
    return pl.pallas_call(
        functools.partial(norm_back_kernel, blocks),
        grid_spec=pltpu.PrefetchScalarGridSpec(
            num_scalar_prefetch=1,
            grid=(1,),
            in_specs=[whole, whole, whole, vector],
            out_specs=[whole, vector, vector],
            scratch_shapes=[pltpu.VMEM((rows, width), bf16)],
        ),
        out_shape=[shape((rows, width), bf16), shape((1, width), f32), shape((1, width), f32)],
        compiler_params=params(32),
        cost_estimate=cost(20 * rows * width, 8 * rows * width),
        name="norm_back",
    )(at, total, rows_in, cot, gain)


def final_kernel(parts, levels, *refs):
    full, rest, out_ref = refs[:2], refs[2:-1], refs[-1]
    base = full[0][...].astype(f32) + full[1][...].astype(f32)
    for part in range(parts):
        @pl.when(pl.program_id(0) == part)
        def _():
            total = base
            for ref in rest[part * levels : (part + 1) * levels]:
                total += ref[...].astype(f32)
            out_ref[...] = total


def final(full, sums, block):
    parts, levels = len(sums), len(sums[0])
    width = full[0].shape[1]
    wide = width // parts
    piece = pl.BlockSpec((block, wide), lambda i: (0, i))
    held = pl.BlockSpec((block, wide), lambda i: (0, 0))
    return pl.pallas_call(
        functools.partial(final_kernel, parts, levels),
        grid=(parts,),
        in_specs=[piece, piece] + [held] * (parts * levels),
        out_specs=piece,
        out_shape=shape((block, width), f32),
        compiler_params=params(32),
        cost_estimate=cost(4 * block * width, 12 * block * width),
        name="final",
    )(*full, *[f for s in sums for f in s])


def finish_kernel(blocks, at_ref, sum_ref, rows_ref, bias_a_ref, bias_b_ref, out_ref, held):
    rows, width = rows_ref.shape
    wide = width // blocks
    bits = blocks.bit_length() - 1
    for q in range(blocks):
        place = pl.multiple_of(reversed_bits(at_ref[1] ^ q, bits) * wide, wide)
        held[:, q * wide : (q + 1) * wide] = sum_ref[:, pl.ds(place, wide)]
    branch = held[...].astype(f32) + bias_a_ref[...] + bias_b_ref[...]
    position = at_ref[0] * rows + lax.broadcasted_iota(jnp.int32, (rows, 1), 0)
    branch = jnp.where(position < at_ref[2], branch, 0.0)
    out_ref[...] = (rows_ref[...].astype(f32) + branch).astype(bf16)


def finish(branch_sum, rows_in, bias_a, bias_b, at, blocks):
    rows, width = rows_in.shape
    whole = pl.BlockSpec((rows, width), lambda i, n: (0, 0))
    vector = pl.BlockSpec((1, width), lambda i, n: (0, 0))
    return pl.pallas_call(
        functools.partial(finish_kernel, blocks),
        grid_spec=pltpu.PrefetchScalarGridSpec(
            num_scalar_prefetch=1,
            grid=(1,),
            in_specs=[whole, whole, vector, vector],
            out_specs=whole,
            scratch_shapes=[pltpu.VMEM((rows, width), bf16)],
        ),
        out_shape=shape((rows, width), bf16),
        compiler_params=params(32),
        cost_estimate=cost(8 * rows * width, 6 * rows * width),
        name="finish",
    )(at, branch_sum, rows_in, bias_a, bias_b)


def rotary_tables(rows, col_count):
    half_rot = ROT // 2
    column = jnp.arange(col_count) % HEAD_DIM
    exponent = (2 * (column % half_rot)).astype(jnp.float32) / ROT
    frequency = jnp.exp(-math.log(10000.0) * exponent)
    angles = rows.astype(jnp.float32)[:, None] * frequency[None, :]
    inside = column < ROT
    cosine = jnp.where(inside, jnp.cos(angles), 1.0)
    sine_part = jnp.sin(angles)
    ahead_sin = jnp.where(column < half_rot, -sine_part, 0.0)
    behind_sin = jnp.where(inside & (column >= half_rot), sine_part, 0.0)
    return (cosine, ahead_sin, behind_sin)


def flip(array, axis_name, bit):
    size = lax.axis_size(axis_name)
    return lax.ppermute(array, axis_name, [(i, i ^ (1 << bit)) for i in range(size)])


def bits_of(size):
    return size.bit_length() - 1


def swap_blocks(array, index, axis, blocks):
    for bit in range(bits_of(blocks)):
        dims = array.shape
        parts = dims[:axis] + (blocks >> (bit + 1), 2, 1 << bit, dims[axis] // blocks)
        view = array.reshape(parts + dims[axis + 1 :])
        other = jnp.flip(view, axis=axis + 1)
        array = jnp.where((index >> bit) & 1 == 1, other, view).reshape(dims)
    return array


def reversed_bits(value, bits):
    return sum(((value >> k) & 1) << (bits - 1 - k) for k in range(bits))


def xor_columns(array, index, blocks):
    width = array.shape[-1] // blocks
    bits = bits_of(blocks)
    pieces = [
        lax.dynamic_slice_in_dim(
            array, (index ^ reversed_bits(p, bits)) * width, width, array.ndim - 1
        )
        for p in range(blocks)
    ]
    return jnp.concatenate(pieces, -1)


def plain_columns(array, index, blocks):
    width = array.shape[-1] // blocks
    bits = bits_of(blocks)
    pieces = []
    for q in range(blocks):
        place = reversed_bits(index ^ q, bits)
        pieces.append(lax.dynamic_slice_in_dim(array, place * width, width, array.ndim - 1))
    return jnp.concatenate(pieces, -1)


def gather_step(stacks, bit):
    return stacks + [(flip(rows, "dp", bit), [m | (1 << bit) for m in masks]) for rows, masks in stacks]


def gather_plan(stacks, block, bits):
    plan = []
    for which, (_, masks) in enumerate(stacks):
        for i, m in enumerate(masks):
            plan.append((which, i * block, reversed_bits(m, bits) * block, block))
    return [s[0] for s in stacks], tuple(plan)


def core_copies(stacks):
    return [(flip(rows, "dp", 0), [m | 1 for m in masks]) for rows, masks in stacks]


def route_order(last):
    return [b for b in range(bits_of(lax.axis_size("dp")) - 1, -1, -1) if b != last]


def route_first(block, last):
    return jnp.stack([block, flip(block, "dp", route_order(last)[0])], 0)


def route_more(stack, last):
    for bit in route_order(last)[1:]:
        stack = jnp.concatenate([stack, flip(stack, "dp", bit)], 0)
    return stack


def route_last(stack, wanted, index, last):
    order = route_order(last)

    def place(mask):
        return sum(((mask >> bit) & 1) << k for k, bit in enumerate(order))

    mine = wanted[index]
    theirs = wanted[index ^ (1 << last)]
    given = lax.dynamic_index_in_dim(stack, place(index ^ theirs), 0, keepdims=False)
    held = lax.dynamic_index_in_dim(stack, place(index ^ mine), 0, keepdims=False)
    arrived = flip(given, "dp", last)
    return jnp.where(((index ^ mine) >> last) & 1 == 1, arrived, held)


def gather_small(stack, axis_name):
    for bit in range(bits_of(lax.axis_size(axis_name))):
        stack = jnp.concatenate([stack, flip(stack, axis_name, bit)], 0)
    return stack


def scatter_first(blocks, data_index, tensor_index):
    stack = swap_blocks(
        blocks, data_index * lax.axis_size("tensor") + tensor_index, 0, blocks.shape[0]
    )
    half = stack.shape[0] // 2
    return stack[:half], flip(stack[half:], "dp", bits_of(lax.axis_size("dp")) - 1)


def scatter_rest(kept, arrived):
    stack = kept + arrived
    for bit in range(bits_of(lax.axis_size("dp")) - 2, -1, -1):
        half = stack.shape[0] // 2
        stack = stack[:half] + flip(stack[half:], "dp", bit)
    for bit in range(bits_of(lax.axis_size("tensor")) - 1, -1, -1):
        half = stack.shape[0] // 2
        stack = stack[:half] + flip(stack[half:], "tensor", bit)
    return stack[0]


def after(values, *others):
    held = lax.optimization_barrier((tuple(values), tuple(others)))
    return held[0]


def shards(
    hidden_in,
    cotangent,
    lengths,
    slot_of_seq,
    seq_of_slot,
    qkv_weight,
    out_weight,
    fc1_weight,
    fc2_weight,
    ln_gain,
    ln_bias,
    qkv_bias,
    out_bias,
    fc1_bias,
    fc2_bias,
):
    rows_here = hidden_in.shape[1]
    width = hidden_in.shape[2]
    tensor_count = lax.axis_size("tensor")
    data_count = lax.axis_size("dp")
    tensor_index = lax.axis_index("tensor")
    data_index = lax.axis_index("dp")
    seq_len = rows_here * tensor_count
    heads_local = qkv_weight.shape[2]
    hidden_local = fc1_weight.shape[1]
    block = width // data_count
    length = lengths[seq_of_slot[data_index]]
    bits = bits_of(data_count)
    x_first = list(range(1, bits))
    y_first = x_first[::-1]
    tile_f = min(512, hidden_local)

    lasts = (bits - 1, bits - 2)
    wave_rows = rows_here // 2
    at = jnp.stack([tensor_index, data_index, length]).astype(jnp.int32)

    def send(rows):
        half = rows.shape[0] // 2
        return [route_first(h, last) for h, last in zip((rows[:half], rows[half:]), lasts)]

    def receive(firsts, wanted):
        return finish_route([route_more(f, last) for f, last in zip(firsts, lasts)], wanted)

    def finish_route(stacks, wanted):
        return jnp.concatenate(
            [route_last(f, wanted, data_index, last) for f, last in zip(stacks, lasts)], 0
        )

    firsts = send(hidden_in[0])
    vectors = [ln_gain, ln_bias, out_bias, fc2_bias, qkv_bias, fc1_bias]
    s = ln_gain.shape[0]
    vectors = after(vectors, *firsts)
    small = jnp.concatenate([v.reshape(-1, s) for v in vectors], 0)
    stack = gather_small(small[None], "tensor")
    routed = receive(firsts, seq_of_slot)
    routed, stack = after((routed, stack))
    stack = gather_small(stack, "dp")
    gathered = swap_blocks(stack, data_index * tensor_count + tensor_index, 0, stack.shape[0])
    gathered = gathered.reshape(data_count, tensor_count, -1)

    rows_a, rows_b = routed[:wave_rows], routed[wave_rows:]
    full_a = lax.all_gather(rows_a, "tensor", axis=0, tiled=True)
    full_b = lax.all_gather(rows_b, "tensor", axis=0, tiled=True)

    qk_shard = qkv_weight[:, :2].reshape(block, 2 * heads_local)
    vo_shard = jnp.concatenate([qkv_weight[:, 2], out_weight], 1)
    qk_shard, vo_shard = after((qk_shard, vo_shard), routed)
    qk_stacks = gather_step([(qk_shard, [0])], x_first[0])
    vo_stacks = gather_step([(vo_shard, [0])], y_first[0])
    for step in range(1, len(x_first)):
        qk_stacks = gather_step(qk_stacks, x_first[step])
        vo_stacks = gather_step(vo_stacks, y_first[step])

    def held_back(groups, *values):
        flat = [rows for stacks in groups for rows, _ in stacks]
        out = list(after(tuple(flat) + values))
        fresh = [[(out.pop(0), masks) for _, masks in stacks] for stacks in groups]
        return fresh, out

    (qk_stacks, vo_stacks), (fc1_shard, fc2_shard, row_ids) = held_back(
        (qk_stacks, vo_stacks), fc1_weight, fc2_weight, jnp.arange(seq_len, dtype=jnp.int32)
    )
    qk = gather_plan(qk_stacks + core_copies(qk_stacks), block, bits)
    vo = gather_plan(vo_stacks + core_copies(vo_stacks), block, bits)
    fc1_stacks = gather_step([(fc1_shard, [0])], x_first[0])
    fc2_stacks = gather_step([(fc2_shard, [0])], y_first[0])

    positions = tensor_index * rows_here + jnp.arange(rows_here, dtype=jnp.int32)
    valid = (positions < length)[:, None]
    cot_rows = cotangent[0]
    low_plain = jnp.where(valid, cot_rows, jnp.zeros_like(cot_rows))
    low, = after((low_plain,), routed)
    low = xor_columns(low, data_index, data_count)
    grads = lax.all_gather(low, "tensor", axis=0, tiled=True)

    gain, shift, bias_a, bias_b = [
        gathered[:, :, i * s : (i + 1) * s].reshape(1, width).astype(f32) for i in range(4)
    ]
    q = qkv_bias.shape[0]
    bias_qkv = lax.dynamic_slice_in_dim(
        gathered[:, :, 4 * s : 4 * s + q].reshape(3, width), tensor_index * heads_local, heads_local, 1
    ).astype(f32)
    bias_fc1 = lax.dynamic_slice_in_dim(
        gathered[:, :, 4 * s + q :].reshape(1, hidden_local * tensor_count),
        tensor_index * hidden_local,
        hidden_local,
        1,
    ).astype(f32)

    tables = after(rotary_tables(row_ids, PAIR))
    wave_tables = [v.reshape(tensor_count, 2, wave_rows, PAIR) for v in tables]
    size = length.reshape(1)
    ln_a = norm_wave(full_a, tensor_count, at, gain, shift, data_count, 0, None)
    qkv_a, weights = project_first(ln_a, qk, vo, bias_qkv, wave_tables)
    (fc1_stacks, fc2_stacks), (weights,) = held_back((fc1_stacks, fc2_stacks), weights)
    fc1_far, fc2_far = core_copies(fc1_stacks), core_copies(fc2_stacks)
    for step in range(1, len(x_first)):
        fc1_stacks = gather_step(fc1_stacks, x_first[step])
        fc2_stacks = gather_step(fc2_stacks, y_first[step])
    (fc1_far, fc2_far), (full_b,) = held_back((fc1_far, fc2_far), full_b)
    ln = norm_wave(full_b, tensor_count, at, gain, shift, data_count, 1, ln_a)
    qkv = project_second(ln, weights, bias_qkv, wave_tables, qkv_a)
    ln, qkv = ln.reshape(seq_len, width), qkv.reshape(3, seq_len, heads_local)
    mixed, totals = attend(qkv, size)
    (fc1_stacks, fc2_stacks), (mixed,) = held_back((fc1_stacks, fc2_stacks), mixed)
    fc1_far = fc1_far + core_copies(fc1_stacks[2:])
    fc2_far = fc2_far + core_copies(fc2_stacks[2:])
    w1 = gather_plan(fc1_stacks + fc1_far, block, bits)
    w2 = gather_plan(fc2_stacks + fc2_far, block, bits)
    branch, hidden, slope, full1, full2 = feed(ln, mixed, weights, w1, w2, bias_fc1, tile_f)
    branch, grads = after((branch, grads))
    branch = lax.psum_scatter(branch, "tensor", scatter_dimension=0, tiled=True)

    count = data_count // 2
    steps = len(x_first)
    feed_sum, grad_pre, grad_mixed, grad_fc1_b = back(grads, full1, full2, slope, weights, tile_f)
    hidden, = after((hidden,), grad_pre)
    k2, s2 = feed_weight(grads, hidden, tile_f)
    c2 = flip(s2, "dp", 0)
    grad_pre, = after((grad_pre,), s2)
    k1, s1 = feed_weight(ln, grad_pre, tile_f)
    c1 = flip(s1, "dp", 0)

    pair = ((0, 2), (1, 2))
    both = (x_first, y_first)

    def first_gives(full):
        return [give(full, [], count, low, part) for part, low in zip(pair, (False, True))]

    def next_gives(full, sums, step):
        return [give(full, s, count, low, p) for s, low, p in zip(sums, (False, True), pair)]

    def send_on(gives, step):
        return [flip(g, "dp", order[step]) for g, order in zip(gives, both)]

    k2, c2 = after((k2, c2), s1)
    gives2 = first_gives([k2, c2])
    sums2 = [[f] for f in send_on(gives2, 0)]
    k1, c1 = after((k1, c1), *gives2)
    gives1 = first_gives([k1, c1])
    sums1 = [[f] for f in send_on(gives1, 0)]
    grad_mixed, = after((grad_mixed,), *gives1)
    grad_qkv = attend_back(qkv, grad_mixed, totals, size, tables)
    grad_qkv, branch, sums2, sums1 = after((grad_qkv, branch, sums2, sums1))
    ln_part = ln_grad(grad_qkv, weights, feed_sum)
    total = lax.psum_scatter(ln_part, "tensor", scatter_dimension=0, tiled=True)
    mixed, = after((mixed,), ln_part)
    kqk, kvo, sqk, svo, grad_qkv_b = weight_grad(ln, grads, grad_qkv, mixed)
    cq, cv = flip(sqk, "dp", 0), flip(svo, "dp", 0)
    k2, = after((k2,), sqk)
    for step in range(1, steps):
        gives2 = next_gives([k2, c2], sums2, step)
        sums2 = [s + [f] for s, f in zip(sums2, send_on(gives2, step))]
    k1, = after((k1,), *gives2)
    for step in range(1, steps):
        gives1 = next_gives([k1, c1], sums1, step)
        sums1 = [s + [f] for s, f in zip(sums1, send_on(gives1, step))]
    kqk, cq, kvo, cv = after((kqk, cq, kvo, cv), *gives1)
    giveq, givev = give([kqk, cq], [], count, False), give([kvo, cv], [], count, True)
    sumsq, sumsv = [flip(giveq, "dp", x_first[0])], [flip(givev, "dp", y_first[0])]
    branch, = after((branch,), giveq, givev)
    block_out = finish(branch, routed, bias_a, bias_b, at, data_count)[None]
    grad_bias = jnp.sum(low_plain.astype(f32), axis=0)
    devices = data_count * tensor_count
    full_qkv_b = lax.dynamic_update_slice_in_dim(
        jnp.zeros((3, width), f32), grad_qkv_b[:, 0], tensor_index * heads_local, 1
    )
    full_fc1_b = lax.dynamic_update_slice_in_dim(
        jnp.zeros((hidden_local * tensor_count,), f32), grad_fc1_b[0], tensor_index * hidden_local, 0
    )
    known = jnp.concatenate(
        [grad_bias.reshape(devices, s), full_qkv_b.reshape(devices, q), full_fc1_b.reshape(devices, -1)],
        1,
    )
    total, known, sumsq, sumsv, sums2, sums1 = after(
        (total, known, sumsq, sumsv, sums2, sums1), block_out
    )
    slot, grad_gain, grad_shift = norm_back(total, routed, cotangent[0], gain, at, data_count)
    firsts = send(slot)
    kqk, kvo = after((kqk, kvo), slot)
    for step in range(1, steps):
        giveq = give([kqk, cq], sumsq, count, False)
        givev = give([kvo, cv], sumsv, count, True)
        sumsq = sumsq + [flip(giveq, "dp", x_first[step])]
        sumsv = sumsv + [flip(givev, "dp", y_first[step])]
    k2, k1 = after((k2, k1), giveq, givev)
    grad_fc2_w, grad_fc1_w = final([k2, c2], sums2, block), final([k1, c1], sums1, block)
    grad_gain, grad_shift, known, firsts = after(
        (grad_gain, grad_shift, known, firsts), grad_fc2_w, grad_fc1_w
    )
    stacks = [route_more(f, last) for f, last in zip(firsts, lasts)]
    sums = jnp.concatenate(
        [v.reshape(devices, s) for v in (grad_gain[0], grad_shift[0])] + [known], 1
    )
    kept, arrived = scatter_first(sums, data_index, tensor_index)
    stacks, kept, arrived = after((stacks, kept, arrived))
    grad_input = finish_route(stacks, slot_of_seq)[None]
    total = scatter_rest(kept, arrived)
    sumsq, sumsv = after((sumsq, sumsv), *stacks)
    grad_qk_w, grad_vo_w = final([kqk, cq], [sumsq], block), final([kvo, cv], [sumsv], block)
    grad_out_w = grad_vo_w[:, heads_local:]
    grad_qkv_w = jnp.stack(
        [grad_qk_w[:, :heads_local], grad_qk_w[:, heads_local:], grad_vo_w[:, :heads_local]], 1
    )
    return (
        block_out,
        grad_input,
        grad_qkv_w,
        grad_out_w,
        grad_fc1_w,
        grad_fc2_w,
        total[:s],
        total[s : 2 * s],
        total[3 * s : 3 * s + q],
        total[2 * s : 3 * s],
        total[3 * s + q :],
        total[2 * s : 3 * s],
    )


def solution(mesh):
    in_specs = (
        P("dp", "tensor", None),
        P("dp", "tensor", None),
        P(),
        P(),
        P(),
        P("dp", None, "tensor"),
        P("dp", "tensor"),
        P("dp", "tensor"),
        P("dp", "tensor"),
        P(("dp", "tensor")),
        P(("dp", "tensor")),
        P(("dp", "tensor")),
        P(("dp", "tensor")),
        P(("dp", "tensor")),
        P(("dp", "tensor")),
    )
    out_specs = (
        P("dp", "tensor", None),
        P("dp", "tensor", None),
        P("dp", None, "tensor"),
        P("dp", "tensor"),
        P("dp", "tensor"),
        P("dp", "tensor"),
        P(("dp", "tensor")),
        P(("dp", "tensor")),
        P(("dp", "tensor")),
        P(("dp", "tensor")),
        P(("dp", "tensor")),
        P(("dp", "tensor")),
    )
    return jax.shard_map(shards, mesh=mesh, in_specs=in_specs, out_specs=out_specs, check_vma=False)
```

```python
import functools
import math

import jax
import jax.numpy as jnp
from jax import lax
from jax.experimental import pallas as pl
from jax.experimental.pallas import tpu as pltpu
from jax.sharding import PartitionSpec as P

HEAD_DIM = 64
ROT = 32
PAIR = 2 * HEAD_DIM
VMEM = 63 * 1024 * 1024
SHARE = 0.4


eps = 1e-05
masked_score = -1e30
f32 = jnp.float32
bf16 = jnp.bfloat16
NN = (((1,), (0,)), ((), ()))
NT = (((1,), (1,)), ((), ()))
TN = (((0,), (0,)), ((), ()))
once = pl.Buffered(1)


def dot(a, b, dims):
    return lax.dot_general(a, b, dims, preferred_element_type=f32)


def params(mib):
    return pltpu.CompilerParams(vmem_limit_bytes=VMEM)


def cost(flops, nbytes, exps=0):
    return pl.CostEstimate(
        flops=int(flops * SHARE), bytes_accessed=int(nbytes * SHARE), transcendentals=int(exps * SHARE)
    )


def shape(dims, dtype):
    return jax.ShapeDtypeStruct(dims, dtype)


def turned(field, tables):
    cosine, ahead, behind = tables
    half = ROT // 2
    wide = field.shape[1]
    return (
        field * cosine
        + pltpu.roll(field, wide - half, 1) * ahead
        + pltpu.roll(field, half, 1) * behind
    )


def turned_back(grad, tables):
    cosine, ahead, behind = tables
    half = ROT // 2
    wide = grad.shape[1]
    return (
        grad * cosine
        + pltpu.roll(grad * ahead, half, 1)
        + pltpu.roll(grad * behind, wide - half, 1)
    )


def norm_kernel(blocks, at_ref, x_ref, gain_ref, shift_ref, *rest):
    out_ref, plain = rest[-2:]
    rows = x_ref[...].astype(f32)
    centred = rows - jnp.mean(rows, -1, keepdims=True)
    scale = lax.rsqrt(jnp.mean(centred * centred, -1, keepdims=True) + eps)
    plain[...] = (centred * scale * gain_ref[...] + shift_ref[...]).astype(bf16)
    wide = plain.shape[1] // blocks
    bits = blocks.bit_length() - 1
    for p in range(blocks):
        place = (at_ref[1] ^ reversed_bits(p, bits)) * wide
        out_ref[0, 0, :, p * wide : (p + 1) * wide] = plain[:, pl.ds(pl.multiple_of(place, wide), wide)]


def norm_wave(rows_in, count, at, gain, shift, blocks, wave, held):
    rows, width = rows_in.shape[0] // count, rows_in.shape[1]
    vector = pl.BlockSpec((1, width), lambda j, n: (0, 0))
    extra = [] if held is None else [held]
    return pl.pallas_call(
        functools.partial(norm_kernel, blocks),
        grid_spec=pltpu.PrefetchScalarGridSpec(
            num_scalar_prefetch=1,
            grid=(count,),
            in_specs=[pl.BlockSpec((rows, width), lambda j, n: (j, 0)), vector, vector]
            + [pl.BlockSpec(memory_space=pl.ANY)] * len(extra),
            out_specs=pl.BlockSpec((1, 1, rows, width), lambda j, n: (j, wave, 0, 0)),
            scratch_shapes=[pltpu.VMEM((rows, width), bf16)],
        ),
        out_shape=shape((count, 2, rows, width), bf16),
        input_output_aliases={4: 0} if extra else {},
        compiler_params=params(32),
        cost_estimate=cost(10 * count * rows * width, 4 * count * rows * width),
        name="norm_wave",
    )(at, rows_in, gain, shift, *extra)


def project_rows(kind, ln_ref, weight, bias_ref, tables, out_ref):
    rows = ln_ref.shape[0] * ln_ref.shape[2]
    many, size = ln_ref.shape[0], ln_ref.shape[2]
    raw = dot(ln_ref[...].reshape(rows, ln_ref.shape[3]), weight, NN) + bias_ref[0]

    @pl.when(kind < 2)
    def _():
        here = [t[...].reshape(rows, PAIR) for t in tables]
        for pair in range(raw.shape[1] // PAIR):
            cols = slice(pair * PAIR, (pair + 1) * PAIR)
            out_ref[0, :, 0, :, cols] = (
                turned(raw[:, cols], here).astype(bf16).reshape(many, size, PAIR)
            )

    @pl.when(kind == 2)
    def _():
        out_ref[0, :, 0] = raw.astype(bf16).reshape(many, size, raw.shape[1])


def assemble_start(refs, plan, column, size, buffer, sems):
    for j, (which, row, place, count) in enumerate(plan):
        pltpu.make_async_copy(
            refs[which].at[pl.ds(row, count), pl.ds(column, size)],
            buffer.at[pl.ds(place, count), :],
            sems.at[j],
        ).start()


def assemble_wait(refs, plan, column, size, buffer, sems):
    for j, (which, row, place, count) in enumerate(plan):
        pltpu.make_async_copy(
            refs[which].at[pl.ds(row, count), pl.ds(column, size)],
            buffer.at[pl.ds(place, count), :],
            sems.at[j],
        ).wait()


def project_first_kernel(qk_plan, vo_plan, ln_ref, bias_ref, c_ref, a_ref, b_ref, *rest):
    n = len({p[0] for p in qk_plan})
    qk_refs, vo_refs = rest[:n], rest[n : 2 * n]
    out_ref, w_ref, buffer, sems, out_sems = rest[2 * n :]
    kind = pl.program_id(0)
    heads = buffer.shape[2]
    sources = (
        (qk_refs, qk_plan, 0),
        (qk_refs, qk_plan, heads),
        (vo_refs, vo_plan, 0),
        (vo_refs, vo_plan, heads),
    )

    def drain(k):
        pltpu.make_async_copy(buffer.at[k % 2], w_ref.at[k], out_sems.at[k % 2]).wait()

    for k in range(4):
        refs, plan, column = sources[k]
        slot = k % 2

        @pl.when(kind == k)
        def _():
            if k == 0:
                assemble_start(refs, plan, column, heads, buffer.at[slot], sems.at[slot])
            assemble_wait(refs, plan, column, heads, buffer.at[slot], sems.at[slot])
            pltpu.make_async_copy(buffer.at[slot], w_ref.at[k], out_sems.at[slot]).start()
            if k >= 1:
                drain(k - 1)
            if k < 3:
                nrefs, nplan, ncolumn = sources[k + 1]
                assemble_start(
                    nrefs, nplan, ncolumn, heads, buffer.at[1 - slot], sems.at[1 - slot]
                )
            else:
                drain(k)

    @pl.when(kind < 3)
    def _():
        project_rows(kind, ln_ref, buffer[kind % 2], bias_ref, (c_ref, a_ref, b_ref), out_ref)


def project_first(ln, qk, vo, bias, tables):
    many, _, size, width = ln.shape
    heads = bias.shape[1]
    table = pl.BlockSpec((many, 1, size, PAIR), lambda i: (0, 0, 0, 0), pipeline_mode=once)
    hbm = pl.BlockSpec(memory_space=pl.ANY)
    last = lambda i: jnp.minimum(i, 2)
    return pl.pallas_call(
        functools.partial(project_first_kernel, qk[1], vo[1]),
        grid=(4,),
        in_specs=[
            pl.BlockSpec((many, 1, size, width), lambda i: (0, 0, 0, 0), pipeline_mode=once),
            pl.BlockSpec((1, 1, heads), lambda i: (last(i), 0, 0)),
            table,
            table,
            table,
        ]
        + [hbm] * (len(qk[0]) + len(vo[0])),
        out_specs=[
            pl.BlockSpec((1, many, 1, size, heads), lambda i: (last(i), 0, 0, 0, 0)),
            hbm,
        ],
        out_shape=[shape((3, many, 2, size, heads), bf16), shape((4, width, heads), bf16)],
        scratch_shapes=[
            pltpu.VMEM((2, width, heads), bf16),
            pltpu.SemaphoreType.DMA((2, len(qk[1]))),
            pltpu.SemaphoreType.DMA((2,)),
        ],
        compiler_params=params(48),
        cost_estimate=cost(6 * many * size * width * heads, 22 << 20),
        name="project_first",
    )(ln, bias[:, None, :], *tables, *qk[0], *vo[0])


def project_second_kernel(ln_ref, w_ref, bias_ref, c_ref, a_ref, b_ref, held_ref, out_ref):
    project_rows(pl.program_id(0), ln_ref, w_ref[0], bias_ref, (c_ref, a_ref, b_ref), out_ref)


def project_second(ln, weights, bias, tables, held):
    many, _, size, width = ln.shape
    heads = bias.shape[1]
    table = pl.BlockSpec((many, 1, size, PAIR), lambda i: (0, 1, 0, 0), pipeline_mode=once)
    return pl.pallas_call(
        project_second_kernel,
        grid=(3,),
        in_specs=[
            pl.BlockSpec((many, 1, size, width), lambda i: (0, 1, 0, 0), pipeline_mode=once),
            pl.BlockSpec((1, width, heads), lambda i: (i, 0, 0)),
            pl.BlockSpec((1, 1, heads), lambda i: (i, 0, 0)),
            table,
            table,
            table,
            pl.BlockSpec(memory_space=pl.ANY),
        ],
        out_specs=pl.BlockSpec((1, many, 1, size, heads), lambda i: (i, 0, 1, 0, 0)),
        out_shape=shape(held.shape, bf16),
        input_output_aliases={6: 0},
        compiler_params=params(48),
        cost_estimate=cost(6 * many * size * width * heads, 12 << 20),
        name="project_second",
    )(ln, weights, bias[:, None, :], *tables, held)


def side_lanes(side):
    lane = lax.broadcasted_iota(jnp.int32, (1, PAIR), 1)
    return (lane // HEAD_DIM) == side


def masked_scores(keys, queries, first, length):
    scores = dot(keys, queries, NT)
    key = lax.broadcasted_iota(jnp.int32, scores.shape, 0)
    row = first + lax.broadcasted_iota(jnp.int32, (1, scores.shape[1]), 1)
    return jnp.where(key <= jnp.minimum(row, length - 1), scores, masked_score)


def attend_kernel(block, len_ref, q_ref, k_ref, v_ref, out_ref, total_ref, q_mine, v_turned):
    rows = q_ref.shape[1]
    zero = jnp.zeros((rows, PAIR), bf16)
    scale = jnp.asarray(1.0 / math.sqrt(HEAD_DIM), bf16)
    length = len_ref[0]
    for side in range(2):
        lanes = side_lanes(side)
        q_mine[side] = jnp.where(lanes, q_ref[0] * scale, zero)
    v_turned[...] = v_ref[0].T
    for first in range(0, rows, block):
        n = first + block
        r = slice(first, n)
        mixed = []
        for side in range(2):
            scores = masked_scores(k_ref[0, :n, :], q_mine[side, r, :], first, length)
            top = jnp.max(scores, 0, keepdims=True)
            exped = jnp.exp(scores - top)
            total = jnp.sum(exped, 0, keepdims=True)
            part = v_turned[side*HEAD_DIM:(side+1)*HEAD_DIM, :n]
            mixed.append(dot(part, exped.astype(bf16), NN) * (1.0 / total))
            total_ref[0, side:side+1, r] = top + jnp.log(total)
        out_ref[r, :] = jnp.concatenate(mixed, 0).T.astype(bf16)


def attend(qkv, length, block=512):
    _, rows, width = qkv.shape
    pairs = width // PAIR
    kind = lambda c: pl.BlockSpec((1, rows, PAIR), lambda h, n: (c, 0, h))
    return pl.pallas_call(functools.partial(attend_kernel, min(block, rows)),
        grid_spec=pltpu.PrefetchScalarGridSpec(num_scalar_prefetch=1, grid=(pairs,),
            in_specs=[kind(0), kind(1), kind(2)],
            out_specs=[pl.BlockSpec((rows, PAIR), lambda h, n: (0, h)), pl.BlockSpec((1, 2, rows), lambda h, n: (h, 0, 0))],
            scratch_shapes=[pltpu.VMEM((2, rows, PAIR), bf16), pltpu.VMEM((PAIR, rows), bf16)]),
        out_shape=[shape((rows, width), bf16), shape((pairs, 2, rows), f32)],
        compiler_params=params(48),
        cost_estimate=cost(16 * rows * rows * width, 4 << 20, rows * rows * 2 * pairs),
        name="attend")(length, qkv, qkv, qkv)


def attend_back_kernel(block, len_ref, q_ref, k_ref, v_ref, do_ref, total_ref, c_ref, a_ref, b_ref, grad_ref, q_mine, do_mine, k_turned, key_sum, value_sum):
    rows = q_ref.shape[1]
    zero = jnp.zeros((rows, PAIR), bf16)
    scale = 1.0 / math.sqrt(HEAD_DIM)
    for side in range(2):
        lanes = side_lanes(side)
        q_mine[side] = jnp.where(lanes, q_ref[0] * jnp.asarray(scale, bf16), zero)
        do_mine[side] = jnp.where(lanes, do_ref[...], zero)
    k_turned[...] = k_ref[0].T
    length = len_ref[0]
    tables_of = lambda r: (c_ref[r, :], a_ref[r, :], b_ref[r, :])
    for first in range(rows - block, -1, -block):
        n = first + block
        r = slice(first, n)
        gk = gv = None
        gq = []
        for side in range(2):
            scores = masked_scores(k_ref[0, :n, :], q_mine[side, r, :], first, length)
            probs = jnp.exp(scores - total_ref[0, side:side+1, r])
            grad_probs = dot(v_ref[0, :n, :], do_mine[side, r, :], NT)
            product = probs * grad_probs
            delta = jnp.sum(product, 0, keepdims=True)
            grad_scores = (product - probs * delta).astype(bf16)
            a = dot(grad_scores, q_mine[side, r, :], NN)
            b = dot(probs.astype(bf16), do_mine[side, r, :], NN)
            gk = a if gk is None else gk + a
            gv = b if gv is None else gv + b
            gq.append(dot(k_turned[side*HEAD_DIM:(side+1)*HEAD_DIM, :n], grad_scores, NN))
        if n == rows:
            key_sum[...] = gk
            value_sum[...] = gv
        else:
            key_sum[:n, :] += gk
            value_sum[:n, :] += gv
        grad_query = jnp.concatenate(gq, 0).T * scale
        grad_ref[0, r, :] = turned_back(grad_query, tables_of(r)).astype(bf16)
    for first in range(0, rows, block):
        r = slice(first, first + block)
        grad_ref[1, r, :] = turned_back(key_sum[r, :], tables_of(r)).astype(bf16)
        grad_ref[2, r, :] = value_sum[r, :].astype(bf16)


def attend_back(qkv, grad_mixed, totals, length, tables, block=512):
    _, rows, width = qkv.shape
    pairs = width // PAIR
    kind = lambda c: pl.BlockSpec((1, rows, PAIR), lambda h, n: (c, 0, h))
    table = pl.BlockSpec((rows, PAIR), lambda h, n: (0, 0))
    return pl.pallas_call(functools.partial(attend_back_kernel, min(block, rows)),
        grid_spec=pltpu.PrefetchScalarGridSpec(num_scalar_prefetch=1, grid=(pairs,),
            in_specs=[kind(0), kind(1), kind(2), pl.BlockSpec((rows, PAIR), lambda h, n: (0, h)), pl.BlockSpec((1, 2, rows), lambda h, n: (h, 0, 0)), table, table, table],
            out_specs=pl.BlockSpec((3, rows, PAIR), lambda h, n: (0, 0, h)),
            scratch_shapes=[pltpu.VMEM((2, rows, PAIR), bf16)]*2+[pltpu.VMEM((PAIR, rows), bf16)]+[pltpu.VMEM((rows, PAIR), f32)]*2),
        out_shape=shape((3, rows, width), bf16),
        compiler_params=params(48),
        cost_estimate=cost(40 * rows * rows * width, 8 << 20, rows * rows * 2 * pairs),
        name="attend_back")(length, qkv, qkv, qkv, grad_mixed, totals, *tables)


def feed_kernel(tile, tile_f, steps, plan1, plan2, ln_ref, mixed_ref, wo_ref, bias_ref, *rest):
    n1 = len({p[0] for p in plan1})
    w1_refs, w2_refs = rest[:n1], rest[n1 : 2 * n1]
    (branch_ref, hidden_ref, slope_ref, full1_ref, full2_ref, acc, buf1, buf2, sems1, sems2,
     out_sems) = rest[2 * n1 :]
    step = pl.program_id(0)
    slot = lax.rem(step, 2)
    rows = ln_ref.shape[0]
    c0 = math.sqrt(2.0 / math.pi)
    c1 = 0.044715

    def start(s, at):
        column = pl.multiple_of(s * tile_f, tile_f)
        assemble_start(w1_refs, plan1, column, tile_f, buf1.at[at], sems1.at[at])
        assemble_start(w2_refs, plan2, column, tile_f, buf2.at[at], sems2.at[at])

    def outward(s, at):
        column = pl.multiple_of(s * tile_f, tile_f)
        return (
            pltpu.make_async_copy(
                buf1.at[at], full1_ref.at[:, pl.ds(column, tile_f)], out_sems.at[at, 0]
            ),
            pltpu.make_async_copy(
                buf2.at[at], full2_ref.at[:, pl.ds(column, tile_f)], out_sems.at[at, 1]
            ),
        )

    @pl.when(step == 0)
    def _():
        start(0, 0)

    column = pl.multiple_of(step * tile_f, tile_f)
    assemble_wait(w1_refs, plan1, column, tile_f, buf1.at[slot], sems1.at[slot])
    assemble_wait(w2_refs, plan2, column, tile_f, buf2.at[slot], sems2.at[slot])
    for copy in outward(step, slot):
        copy.start()

    @pl.when(step > 0)
    def _():
        for copy in outward(step - 1, 1 - slot):
            copy.wait()

    @pl.when(step < steps - 1)
    def _():
        start(step + 1, 1 - slot)

    for first in range(0, rows, tile):
        r = slice(first, first + tile)
        pre = dot(ln_ref[r, :], buf1[slot], NN) + bias_ref[...]
        square = pre * pre
        bent = jnp.tanh(c0 * (pre + c1 * (square * pre)))
        half_pre = 0.5 * pre
        hidden = (half_pre * (1.0 + bent)).astype(bf16)
        hidden_ref[r, :] = hidden
        slope_ref[r, :] = 0.5 * (1.0 + bent) + half_pre * (1.0 - bent * bent) * (
            c0 * (1.0 + (3.0 * c1) * square)
        )

    for first in range(0, rows, tile):
        r = slice(first, first + tile)
        part = dot(hidden_ref[r, :], buf2[slot], NT)

        @pl.when(step == 0)
        def _():
            acc[r, :] = part + dot(mixed_ref[r, :], wo_ref[0], NT)

        @pl.when((step > 0) & (step < steps - 1))
        def _():
            acc[r, :] += part

        @pl.when(step == steps - 1)
        def _():
            branch_ref[r, :] = (acc[r, :] + part).astype(bf16)

    @pl.when(step == steps - 1)
    def _():
        for copy in outward(step, slot):
            copy.wait()


def feed(ln, mixed, weights, w1, w2, bias, tile_f):
    rows, width = ln.shape
    hidden = bias.shape[1]
    heads = mixed.shape[1]
    steps = hidden // tile_f
    whole = lambda dims: pl.BlockSpec(dims, lambda i: (0, 0), pipeline_mode=once)
    by_row = pl.BlockSpec((rows, tile_f), lambda i: (0, i))
    hbm = pl.BlockSpec(memory_space=pl.ANY)
    return pl.pallas_call(
        functools.partial(feed_kernel, rows, tile_f, steps, w1[1], w2[1]),
        grid=(steps,),
        in_specs=[
            whole((rows, width)),
            whole((rows, heads)),
            pl.BlockSpec((1, width, heads), lambda i: (3, 0, 0), pipeline_mode=once),
            pl.BlockSpec((1, tile_f), lambda i: (0, i)),
        ]
        + [hbm] * (len(w1[0]) + len(w2[0])),
        out_specs=[whole((rows, width)), by_row, by_row, hbm, hbm],
        out_shape=[
            shape((rows, width), bf16),
            shape((rows, hidden), bf16),
            shape((rows, hidden), f32),
            shape((width, hidden), bf16),
            shape((width, hidden), bf16),
        ],
        scratch_shapes=[
            pltpu.VMEM((rows, width), f32),
            pltpu.VMEM((2, width, tile_f), bf16),
            pltpu.VMEM((2, width, tile_f), bf16),
            pltpu.SemaphoreType.DMA((2, len(w1[1]))),
            pltpu.SemaphoreType.DMA((2, len(w2[1]))),
            pltpu.SemaphoreType.DMA((2, 2)),
        ],
        compiler_params=params(58),
        cost_estimate=cost(4 * rows * width * hidden, 56 << 20, rows * hidden),
        name="feed",
    )(ln, mixed, weights, bias, *w1[0], *w2[0])


def back_kernel(tile, g_ref, w1_ref, w2_ref, slope_ref, wo_ref, sum_ref, pre_ref, mixed_ref, bias_ref):
    step = pl.program_id(0)
    rows = g_ref.shape[0]

    @pl.when(step == 0)
    def _():
        mixed_ref[...] = dot(g_ref[...], wo_ref[0], NN).astype(bf16)

    for first in range(0, rows, tile):
        r = slice(first, first + tile)
        pre_ref[r, :] = (dot(g_ref[r, :], w2_ref[...], NN) * slope_ref[r, :]).astype(bf16)

    bias_ref[...] = jnp.sum(pre_ref[...].astype(f32), axis=0, keepdims=True)
    for first in range(0, rows, tile):
        r = slice(first, first + tile)
        part = dot(pre_ref[r, :], w1_ref[...], NT)

        @pl.when(step == 0)
        def _():
            sum_ref[r, :] = part

        @pl.when(step > 0)
        def _():
            sum_ref[r, :] += part


def back(grads, w1, w2, slope, weights, tile_f):
    rows, width = grads.shape
    units = slope.shape[1]
    heads = weights.shape[2]
    weight = pl.BlockSpec((width, tile_f), lambda i: (0, i))
    whole = lambda dims: pl.BlockSpec(dims, lambda i: (0, 0), pipeline_mode=once)
    by_row = pl.BlockSpec((rows, tile_f), lambda i: (0, i))
    return pl.pallas_call(
        functools.partial(back_kernel, rows),
        grid=(units // tile_f,),
        in_specs=[
            whole((rows, width)),
            weight,
            weight,
            by_row,
            pl.BlockSpec((1, width, heads), lambda i: (3, 0, 0), pipeline_mode=once),
        ],
        out_specs=[
            whole((rows, width)),
            by_row,
            whole((rows, heads)),
            pl.BlockSpec((1, tile_f), lambda i: (0, i)),
        ],
        out_shape=[
            shape((rows, width), f32),
            shape((rows, units), bf16),
            shape((rows, heads), bf16),
            shape((1, units), f32),
        ],
        compiler_params=params(58),
        cost_estimate=cost(4 * rows * width * units, 40 << 20),
        name="back",
    )(grads, w1, w2, slope, weights)


def feed_weight_kernel(left_ref, right_ref, near_ref, far_ref):
    half = left_ref.shape[1] // 2
    far_ref[...] = dot(left_ref[:, half:], right_ref[...], TN).astype(bf16)
    near_ref[...] = dot(left_ref[:, :half], right_ref[...], TN).astype(bf16)


def feed_weight(left, right, tile_f):
    rows, width = left.shape
    units = right.shape[1]
    half = pl.BlockSpec((width // 2, tile_f), lambda i: (0, i))
    return pl.pallas_call(
        feed_weight_kernel,
        grid=(units // tile_f,),
        in_specs=[
            pl.BlockSpec((rows, width), lambda i: (0, 0), pipeline_mode=once),
            pl.BlockSpec((rows, tile_f), lambda i: (0, i)),
        ],
        out_specs=[half, half],
        out_shape=[shape((width // 2, units), bf16)] * 2,
        compiler_params=params(48),
        cost_estimate=cost(2 * rows * width * units, 16 << 20),
        name="feed_weight",
    )(left, right)


def ln_grad_kernel(grad_ref, w_ref, sum_ref, out_ref):
    total = sum_ref[...]
    for kind in range(3):
        total += dot(grad_ref[kind], w_ref[kind], NT)
    out_ref[...] = total.astype(bf16)


def ln_grad(grad_qkv, weights, partial_sum):
    _, rows, heads = grad_qkv.shape
    width = partial_sum.shape[1]
    tile = 512
    return pl.pallas_call(
        ln_grad_kernel,
        grid=(width // tile,),
        in_specs=[
            pl.BlockSpec((3, rows, heads), lambda i: (0, 0, 0), pipeline_mode=once),
            pl.BlockSpec((3, tile, heads), lambda i: (0, i, 0)),
            pl.BlockSpec((rows, tile), lambda i: (0, i)),
        ],
        out_specs=pl.BlockSpec((rows, tile), lambda i: (0, i)),
        out_shape=shape((rows, width), bf16),
        compiler_params=params(48),
        cost_estimate=cost(6 * rows * width * heads, 22 << 20),
        name="ln_grad",
    )(grad_qkv, weights, partial_sum)


def weight_grad_kernel(ln_ref, g_ref, grad_ref, mixed_ref, kqk_ref, kvo_ref, sqk_ref, svo_ref, bias_ref):
    heads = mixed_ref.shape[1]
    step = pl.program_id(0)
    steps = pl.num_programs(0)
    for kind in range(3):
        @pl.when(step == 0)
        def _():
            bias_ref[kind] = jnp.sum(grad_ref[kind].astype(f32), axis=0, keepdims=True)

    for qk_ref, vo_ref, here in ((kqk_ref, kvo_ref, step < steps // 2), (sqk_ref, svo_ref, step >= steps // 2)):
        @pl.when(here)
        def _():
            qk_ref[:, :heads] = dot(ln_ref[...], grad_ref[0], TN).astype(bf16)
            qk_ref[:, heads:] = dot(ln_ref[...], grad_ref[1], TN).astype(bf16)
            vo_ref[:, :heads] = dot(ln_ref[...], grad_ref[2], TN).astype(bf16)
            vo_ref[:, heads:] = dot(g_ref[...], mixed_ref[...], TN).astype(bf16)


def weight_grad(ln, grads, grad_qkv, mixed):
    rows, width = ln.shape
    heads = mixed.shape[1]
    half = width // 2
    tile = min(512, half)
    near = half // tile
    column = pl.BlockSpec((rows, tile), lambda i: (0, i))
    kept = pl.BlockSpec((tile, 2 * heads), lambda i: (jnp.minimum(i, near - 1), 0))
    sent = pl.BlockSpec((tile, 2 * heads), lambda i: (jnp.maximum(i - near, 0), 0))
    return pl.pallas_call(
        weight_grad_kernel,
        grid=(2 * near,),
        in_specs=[
            column,
            column,
            pl.BlockSpec((3, rows, heads), lambda i: (0, 0, 0), pipeline_mode=once),
            pl.BlockSpec((rows, heads), lambda i: (0, 0), pipeline_mode=once),
        ],
        out_specs=[kept, kept, sent, sent, pl.BlockSpec((3, 1, heads), lambda i: (0, 0, 0))],
        out_shape=[shape((half, 2 * heads), bf16)] * 4 + [shape((3, 1, heads), f32)],
        compiler_params=params(48),
        cost_estimate=cost(8 * rows * width * heads, 20 << 20),
        name="weight_grad",
    )(ln, grads, grad_qkv, mixed)


def give_kernel(counts, *refs):
    outs = refs[sum(counts) :]
    start = 0
    for number, out_ref in zip(counts, outs):
        total = refs[start][...].astype(f32)
        for ref in refs[start + 1 : start + number]:
            total += ref[...].astype(f32)
        out_ref[...] = total.astype(bf16)
        start += number


def give(items, count):
    specs, operands, numbers, outs = [], [], [], []
    for full, arrivals, low, part in items:
        rows, width = full[0].shape[0], full[0].shape[1] // part[1]
        block = rows // count
        level = len(arrivals) + 1
        out_count = count >> level
        place = (lambda i: (2 * i + 1) << (level - 1)) if low else (lambda i: out_count + i)
        for k in range(level):
            for array in full if k == 0 else [arrivals[k - 1]]:
                off = part[0] if k == 0 else 0
                specs.append(
                    pl.BlockSpec(
                        (block, width),
                        lambda i, k=k, off=off, low=low, place=place: (
                            place(i) >> k if low else place(i),
                            off,
                        ),
                    )
                )
                operands.append(array)
        numbers.append(len(full) + level - 1)
        outs.append(shape((out_count * block, width), bf16))
    moved = sum(o.shape[0] * o.shape[1] for o in outs)
    return pl.pallas_call(
        functools.partial(give_kernel, tuple(numbers)),
        grid=(out_count,),
        in_specs=specs,
        out_specs=[pl.BlockSpec((block, o.shape[1]), lambda i: (i, 0)) for o in outs],
        out_shape=outs,
        compiler_params=params(32),
        cost_estimate=cost(moved * 2, 6 * moved),
        name="give",
    )(*operands)


def norm_back_kernel(
    blocks, at_ref, sum_ref, rows_ref, cot_ref, gain_ref, first_ref, second_ref, vector_ref, held
):
    wide = rows_ref.shape[1] // blocks
    bits = blocks.bit_length() - 1
    for q in range(blocks):
        place = pl.multiple_of(reversed_bits(at_ref[1] ^ q, bits) * wide, wide)
        held[:, q * wide : (q + 1) * wide] = sum_ref[:, pl.ds(place, wide)]
    grad_ln = held[...].astype(f32)
    rows = rows_ref[...].astype(f32)
    centred = rows - jnp.mean(rows, -1, keepdims=True)
    inv_scale = lax.rsqrt(jnp.mean(centred * centred, -1, keepdims=True) + eps)
    normed = centred * inv_scale
    grad_norm = grad_ln * gain_ref[...]
    back = inv_scale * (
        grad_norm
        - jnp.mean(grad_norm, -1, keepdims=True)
        - normed * jnp.mean(grad_norm * normed, -1, keepdims=True)
    )
    slot = (cot_ref[...].astype(f32) + back).astype(bf16)
    half = first_ref.shape[0]
    first_ref[...] = slot[:half]
    second_ref[...] = slot[half:]
    vector_ref[0:1] = jnp.sum(grad_ln * normed, 0, keepdims=True)
    vector_ref[1:2] = jnp.sum(grad_ln, 0, keepdims=True)


def norm_back(total, rows_in, cot, gain, at, blocks):
    rows, width = rows_in.shape
    whole = pl.BlockSpec((rows, width), lambda i, n: (0, 0))
    vector = pl.BlockSpec((1, width), lambda i, n: (0, 0))
    return pl.pallas_call(
        functools.partial(norm_back_kernel, blocks),
        grid_spec=pltpu.PrefetchScalarGridSpec(
            num_scalar_prefetch=1,
            grid=(1,),
            in_specs=[whole, whole, whole, vector],
            out_specs=[pl.BlockSpec((rows // 2, width), lambda i, n: (0, 0))] * 2
            + [pl.BlockSpec((2, width), lambda i, n: (0, 0))],
            scratch_shapes=[pltpu.VMEM((rows, width), bf16)],
        ),
        out_shape=[shape((rows // 2, width), bf16)] * 2 + [shape((2, width), f32)],
        compiler_params=params(32),
        cost_estimate=cost(20 * rows * width, 8 * rows * width),
        name="norm_back",
    )(at, total, rows_in, cot, gain)


def final_kernel(parts, levels, *refs):
    full, rest, out_ref = refs[:2], refs[2:-1], refs[-1]
    base = full[0][...].astype(f32) + full[1][...].astype(f32)
    for part in range(parts):
        @pl.when(pl.program_id(0) == part)
        def _():
            total = base
            for ref in rest[part * levels : (part + 1) * levels]:
                total += ref[...].astype(f32)
            out_ref[...] = total


def final(full, sums, block):
    parts, levels = len(sums), len(sums[0])
    width = full[0].shape[1]
    wide = width // parts
    piece = pl.BlockSpec((block, wide), lambda i: (0, i))
    held = pl.BlockSpec((block, wide), lambda i: (0, 0))
    return pl.pallas_call(
        functools.partial(final_kernel, parts, levels),
        grid=(parts,),
        in_specs=[piece, piece] + [held] * (parts * levels),
        out_specs=piece,
        out_shape=shape((block, width), f32),
        compiler_params=params(32),
        cost_estimate=cost(4 * block * width, 12 * block * width),
        name="final",
    )(*full, *[f for s in sums for f in s])


def finish_kernel(blocks, at_ref, sum_ref, rows_ref, bias_a_ref, bias_b_ref, out_ref, held):
    rows, width = rows_ref.shape
    wide = width // blocks
    bits = blocks.bit_length() - 1
    for q in range(blocks):
        place = pl.multiple_of(reversed_bits(at_ref[1] ^ q, bits) * wide, wide)
        held[:, q * wide : (q + 1) * wide] = sum_ref[:, pl.ds(place, wide)]
    branch = held[...].astype(f32) + bias_a_ref[...] + bias_b_ref[...]
    position = at_ref[0] * rows + lax.broadcasted_iota(jnp.int32, (rows, 1), 0)
    branch = jnp.where(position < at_ref[2], branch, 0.0)
    out_ref[...] = (rows_ref[...].astype(f32) + branch).astype(bf16)


def finish(branch_sum, rows_in, bias_a, bias_b, at, blocks):
    rows, width = rows_in.shape
    whole = pl.BlockSpec((rows, width), lambda i, n: (0, 0))
    vector = pl.BlockSpec((1, width), lambda i, n: (0, 0))
    return pl.pallas_call(
        functools.partial(finish_kernel, blocks),
        grid_spec=pltpu.PrefetchScalarGridSpec(
            num_scalar_prefetch=1,
            grid=(1,),
            in_specs=[whole, whole, vector, vector],
            out_specs=whole,
            scratch_shapes=[pltpu.VMEM((rows, width), bf16)],
        ),
        out_shape=shape((rows, width), bf16),
        compiler_params=params(32),
        cost_estimate=cost(8 * rows * width, 6 * rows * width),
        name="finish",
    )(at, branch_sum, rows_in, bias_a, bias_b)


def final_attention_kernel(levels, *refs):
    heads = refs[0].shape[1] // 2
    grad_ref, out_ref = refs[-2:]
    totals = []
    for start in (0, levels + 2):
        total = refs[start][...].astype(f32)
        for ref in refs[start + 1 : start + levels + 2]:
            total += ref[...].astype(f32)
        totals.append(total)
    grad_ref[0] = totals[0][:, :heads]
    grad_ref[1] = totals[0][:, heads:]
    grad_ref[2] = totals[1][:, :heads]
    out_ref[...] = totals[1][:, heads:]


def final_attention(qk, vo, block):
    levels = len(qk) - 2
    width = qk[0].shape[1]
    piece = pl.BlockSpec((block, width), lambda i: (0, 0))
    return pl.pallas_call(
        functools.partial(final_attention_kernel, levels),
        grid=(1,),
        in_specs=[piece] * (2 * levels + 4),
        out_specs=[
            pl.BlockSpec((3, block, width // 2), lambda i: (0, 0, 0)),
            pl.BlockSpec((block, width // 2), lambda i: (0, 0)),
        ],
        out_shape=[shape((3, block, width // 2), f32), shape((block, width // 2), f32)],
        compiler_params=params(32),
        cost_estimate=cost(8 * block * width, 24 * block * width),
        name="final_attention",
    )(*qk, *vo)


def rotary_tables(rows, col_count):
    half_rot = ROT // 2
    column = jnp.arange(col_count) % HEAD_DIM
    exponent = (2 * (column % half_rot)).astype(jnp.float32) / ROT
    frequency = jnp.exp(-math.log(10000.0) * exponent)
    angles = rows.astype(jnp.float32)[:, None] * frequency[None, :]
    inside = column < ROT
    cosine = jnp.where(inside, jnp.cos(angles), 1.0)
    sine_part = jnp.sin(angles)
    ahead_sin = jnp.where(column < half_rot, -sine_part, 0.0)
    behind_sin = jnp.where(inside & (column >= half_rot), sine_part, 0.0)
    return (cosine, ahead_sin, behind_sin)


def flip(array, axis_name, bit):
    size = lax.axis_size(axis_name)
    return lax.ppermute(array, axis_name, [(i, i ^ (1 << bit)) for i in range(size)])


def bits_of(size):
    return size.bit_length() - 1


def swap_blocks(array, index, axis, blocks):
    for bit in range(bits_of(blocks)):
        dims = array.shape
        parts = dims[:axis] + (blocks >> (bit + 1), 2, 1 << bit, dims[axis] // blocks)
        view = array.reshape(parts + dims[axis + 1 :])
        other = jnp.flip(view, axis=axis + 1)
        array = jnp.where((index >> bit) & 1 == 1, other, view).reshape(dims)
    return array


def reversed_bits(value, bits):
    return sum(((value >> k) & 1) << (bits - 1 - k) for k in range(bits))


def xor_columns(array, index, blocks):
    width = array.shape[-1] // blocks
    bits = bits_of(blocks)
    pieces = [
        lax.dynamic_slice_in_dim(
            array, (index ^ reversed_bits(p, bits)) * width, width, array.ndim - 1
        )
        for p in range(blocks)
    ]
    return jnp.concatenate(pieces, -1)


def plain_columns(array, index, blocks):
    width = array.shape[-1] // blocks
    bits = bits_of(blocks)
    pieces = []
    for q in range(blocks):
        place = reversed_bits(index ^ q, bits)
        pieces.append(lax.dynamic_slice_in_dim(array, place * width, width, array.ndim - 1))
    return jnp.concatenate(pieces, -1)


def gather_step(stacks, bit):
    return stacks + [(flip(rows, "dp", bit), [m | (1 << bit) for m in masks]) for rows, masks in stacks]


def gather_plan(stacks, block, bits):
    plan = []
    for which, (_, masks) in enumerate(stacks):
        for i, m in enumerate(masks):
            plan.append((which, i * block, reversed_bits(m, bits) * block, block))
    return [s[0] for s in stacks], tuple(plan)


def core_copies(stacks):
    return [(flip(rows, "dp", 0), [m | 1 for m in masks]) for rows, masks in stacks]


def route_order(last):
    return [b for b in range(bits_of(lax.axis_size("dp")) - 1, -1, -1) if b != last]


def route_first(block, last):
    return jnp.stack([block, flip(block, "dp", route_order(last)[0])], 0)


def route_more(stack, last):
    order = route_order(last)[1:]
    for bit in order[:-1]:
        stack = jnp.concatenate([stack, flip(stack, "dp", bit)], 0)
    return (stack, flip(stack, "dp", order[-1]))


def route_picks(halves, wanted, index, last):
    order = route_order(last)
    count = halves[0].shape[0]

    def pick(want):
        mask = index ^ want
        at = sum(((mask >> bit) & 1) << k for k, bit in enumerate(order))
        found = [lax.dynamic_index_in_dim(h, at % count, 0, keepdims=False) for h in halves]
        return found[0] if len(found) == 1 else jnp.where(at < count, found[0], found[1])

    return pick(wanted[index ^ (1 << last)]), pick(wanted[index])


def route_end(given, held, wanted, index, last):
    arrived = flip(given, "dp", last)
    return jnp.where(((index ^ wanted[index]) >> last) & 1 == 1, arrived, held)


def gather_small(stack, axis_name):
    for bit in range(bits_of(lax.axis_size(axis_name))):
        stack = jnp.concatenate([stack, flip(stack, axis_name, bit)], 0)
    return stack


def scatter_along(stack, axis_name):
    bits = bits_of(lax.axis_size(axis_name))
    stack = stack.reshape((2,) * bits + stack.shape[1:])
    stack = stack.transpose(tuple(range(bits - 1, -1, -1)) + tuple(range(bits, stack.ndim)))
    for bit in range(bits):
        stack = stack[0] + flip(stack[1], axis_name, bit)
    return stack


def after(values, *others):
    held = lax.optimization_barrier((tuple(values), tuple(others)))
    return held[0]


def shards(
    hidden_in,
    cotangent,
    lengths,
    slot_of_seq,
    seq_of_slot,
    qkv_weight,
    out_weight,
    fc1_weight,
    fc2_weight,
    ln_gain,
    ln_bias,
    qkv_bias,
    out_bias,
    fc1_bias,
    fc2_bias,
):
    rows_here = hidden_in.shape[1]
    width = hidden_in.shape[2]
    tensor_count = lax.axis_size("tensor")
    data_count = lax.axis_size("dp")
    tensor_index = lax.axis_index("tensor")
    data_index = lax.axis_index("dp")
    seq_len = rows_here * tensor_count
    heads_local = qkv_weight.shape[2]
    hidden_local = fc1_weight.shape[1]
    block = width // data_count
    length = lengths[seq_of_slot[data_index]]
    bits = bits_of(data_count)
    x_first = list(range(1, bits))
    y_first = x_first[::-1]
    tile_f = min(512, hidden_local)

    lasts = (bits - 1, bits - 2)
    wave_rows = rows_here // 2
    at = jnp.stack([tensor_index, data_index, length]).astype(jnp.int32)

    def send(parts):
        return [route_first(h, last) for h, last in zip(parts, lasts)]

    def picks_of(stacks, wanted):
        return [route_picks(f, wanted, data_index, last) for f, last in zip(stacks, lasts)]

    def route_ends(picks, wanted):
        return jnp.concatenate(
            [route_end(g, k, wanted, data_index, last) for (g, k), last in zip(picks, lasts)], 0
        )

    def receive(firsts, wanted):
        stacks = [route_more(f, last) for f, last in zip(firsts, lasts)]
        stacks = [(jnp.concatenate(halves, 0),) for halves in stacks]
        return route_ends(picks_of(stacks, wanted), wanted)

    firsts = send((hidden_in[0, :wave_rows], hidden_in[0, wave_rows:]))
    vectors = [ln_gain, ln_bias, out_bias, fc2_bias, qkv_bias, fc1_bias]
    s = ln_gain.shape[0]
    vectors = after(vectors, *firsts)
    small = jnp.concatenate([v.reshape(-1, s) for v in vectors], 0)
    stack = gather_small(small[None], "tensor")
    routed = receive(firsts, seq_of_slot)
    routed, stack = after((routed, stack))
    extra_rows = 16
    rows_a, rows_b = routed[:wave_rows], routed[wave_rows:]
    full_a = lax.all_gather(rows_a, "tensor", axis=0, tiled=True)
    full_b = lax.all_gather(rows_b, "tensor", axis=0, tiled=True)

    stack = swap_blocks(stack, tensor_index, 0, tensor_count).reshape(-1)
    extra = jnp.pad(stack, (0, extra_rows * 2 * heads_local - stack.shape[0]))
    qk_shard = jnp.concatenate(
        [qkv_weight[:, :2].reshape(block, 2 * heads_local), extra.reshape(extra_rows, 2 * heads_local)], 0
    )
    vo_shard = jnp.concatenate([qkv_weight[:, 2], out_weight], 1)
    qk_shard, vo_shard = after((qk_shard, vo_shard), routed)
    qk_stacks = gather_step([(qk_shard, [0])], x_first[0])
    vo_stacks = gather_step([(vo_shard, [0])], y_first[0])
    for step in range(1, len(x_first)):
        qk_stacks = gather_step(qk_stacks, x_first[step])
        vo_stacks = gather_step(vo_stacks, y_first[step])

    def held_back(groups, *values):
        flat = [rows for stacks in groups for rows, _ in stacks]
        out = list(after(tuple(flat) + values))
        fresh = [[(out.pop(0), masks) for _, masks in stacks] for stacks in groups]
        return fresh, out

    (qk_stacks, vo_stacks), (fc1_shard, fc2_shard, row_ids) = held_back(
        (qk_stacks, vo_stacks), fc1_weight, fc2_weight, jnp.arange(seq_len, dtype=jnp.int32)
    )
    qk_stacks = qk_stacks + core_copies(qk_stacks)
    qk = gather_plan(qk_stacks, block, bits)
    by_mask = sorted(qk_stacks, key=lambda st: st[1][0])
    gathered = jnp.stack([rows[block:].reshape(-1)[: stack.shape[0]] for rows, _ in by_mask], 0)
    gathered = swap_blocks(gathered, data_index, 0, data_count)
    gathered = gathered.reshape(data_count, tensor_count, -1)
    vo = gather_plan(vo_stacks + core_copies(vo_stacks), block, bits)
    fc1_stacks = gather_step([(fc1_shard, [0])], x_first[0])
    fc2_stacks = gather_step([(fc2_shard, [0])], y_first[0])

    positions = tensor_index * rows_here + jnp.arange(rows_here, dtype=jnp.int32)
    valid = (positions < length)[:, None]
    cot_rows = cotangent[0]
    low_plain = jnp.where(valid, cot_rows, jnp.zeros_like(cot_rows))
    low, = after((low_plain,), routed)
    low = xor_columns(low, data_index, data_count)
    grads = lax.all_gather(low, "tensor", axis=0, tiled=True)

    gain, shift, bias_a, bias_b = [
        gathered[:, :, i * s : (i + 1) * s].reshape(1, width).astype(f32) for i in range(4)
    ]
    q = qkv_bias.shape[0]
    bias_qkv = lax.dynamic_slice_in_dim(
        gathered[:, :, 4 * s : 4 * s + q].reshape(3, width), tensor_index * heads_local, heads_local, 1
    ).astype(f32)
    bias_fc1 = lax.dynamic_slice_in_dim(
        gathered[:, :, 4 * s + q :].reshape(1, hidden_local * tensor_count),
        tensor_index * hidden_local,
        hidden_local,
        1,
    ).astype(f32)

    tables = after(rotary_tables(row_ids, PAIR))
    wave_tables = [v.reshape(tensor_count, 2, wave_rows, PAIR) for v in tables]
    size = length.reshape(1)
    ln_a = norm_wave(full_a, tensor_count, at, gain, shift, data_count, 0, None)
    qkv_a, weights = project_first(ln_a, qk, vo, bias_qkv, wave_tables)
    (fc1_stacks, fc2_stacks), (weights,) = held_back((fc1_stacks, fc2_stacks), weights)
    fc1_far, fc2_far = core_copies(fc1_stacks), core_copies(fc2_stacks)
    for step in range(1, len(x_first)):
        fc1_stacks = gather_step(fc1_stacks, x_first[step])
        fc2_stacks = gather_step(fc2_stacks, y_first[step])
    (fc1_far, fc2_far), (full_b,) = held_back((fc1_far, fc2_far), full_b)
    ln = norm_wave(full_b, tensor_count, at, gain, shift, data_count, 1, ln_a)
    qkv = project_second(ln, weights, bias_qkv, wave_tables, qkv_a)
    ln, qkv = ln.reshape(seq_len, width), qkv.reshape(3, seq_len, heads_local)
    mixed, totals = attend(qkv, size)
    (fc1_stacks, fc2_stacks), (mixed,) = held_back((fc1_stacks, fc2_stacks), mixed)
    fc1_far = fc1_far + core_copies(fc1_stacks[2:])
    fc2_far = fc2_far + core_copies(fc2_stacks[2:])
    w1 = gather_plan(fc1_stacks + fc1_far, block, bits)
    w2 = gather_plan(fc2_stacks + fc2_far, block, bits)
    branch, hidden, slope, full1, full2 = feed(ln, mixed, weights, w1, w2, bias_fc1, tile_f)
    branch, grads = after((branch, grads))
    branch = lax.psum_scatter(branch, "tensor", scatter_dimension=0, tiled=True)

    count = data_count // 2
    steps = len(x_first)
    feed_sum, grad_pre, grad_mixed, grad_fc1_b = back(grads, full1, full2, slope, weights, tile_f)
    hidden, = after((hidden,), grad_pre)
    k2, s2 = feed_weight(grads, hidden, tile_f)
    c2 = flip(s2, "dp", 0)
    grad_pre, = after((grad_pre,), s2)
    k1, s1 = feed_weight(ln, grad_pre, tile_f)
    c1 = flip(s1, "dp", 0)

    pair = ((0, 2), (1, 2))
    both = (x_first, y_first)

    def gives_of(full, sums):
        return give([(full, s, low, p) for s, low, p in zip(sums, (False, True), pair)], count)

    def send_on(gives, step):
        return [flip(g, "dp", order[step]) for g, order in zip(gives, both)]

    k2, c2 = after((k2, c2), s1)
    gives2 = gives_of([k2, c2], ([], []))
    sums2 = [[f] for f in send_on(gives2, 0)]
    k1, c1 = after((k1, c1), *gives2)
    gives1 = gives_of([k1, c1], ([], []))
    sums1 = [[f] for f in send_on(gives1, 0)]
    grad_mixed, = after((grad_mixed,), *gives1)
    grad_qkv = attend_back(qkv, grad_mixed, totals, size, tables)
    kqk, kvo, sqk, svo, grad_qkv_b = weight_grad(ln, grads, grad_qkv, mixed)
    cq, cv = flip(sqk, "dp", 0), flip(svo, "dp", 0)
    grad_qkv, branch, sums2, sums1 = after((grad_qkv, branch, sums2, sums1), sqk)
    ln_part = ln_grad(grad_qkv, weights, feed_sum)
    total = lax.psum_scatter(ln_part, "tensor", scatter_dimension=0, tiled=True)
    kqk, kvo, cq, cv = after((kqk, kvo, cq, cv), ln_part)
    giveq, givev = give(
        [([kqk, cq], [], False, (0, 1)), ([kvo, cv], [], True, (0, 1))], count
    )
    sumsq, sumsv = [flip(giveq, "dp", x_first[0])], [flip(givev, "dp", y_first[0])]
    k2, = after((k2,), giveq, givev)
    for step in range(1, steps):
        gives2 = gives_of([k2, c2], sums2)
        sums2 = [s + [f] for s, f in zip(sums2, send_on(gives2, step))]
    k1, = after((k1,), *gives2)
    for step in range(1, steps):
        gives1 = gives_of([k1, c1], sums1)
        sums1 = [s + [f] for s, f in zip(sums1, send_on(gives1, step))]
    branch, = after((branch,), *gives1)
    block_out = finish(branch, routed, bias_a, bias_b, at, data_count)[None]
    grad_bias = jnp.sum(low_plain.astype(f32), axis=0)
    devices = data_count * tensor_count
    full_qkv_b = lax.dynamic_update_slice_in_dim(
        jnp.zeros((3, width), f32), grad_qkv_b[:, 0], tensor_index * heads_local, 1
    )
    full_fc1_b = lax.dynamic_update_slice_in_dim(
        jnp.zeros((hidden_local * tensor_count,), f32), grad_fc1_b[0], tensor_index * hidden_local, 0
    )
    known = jnp.concatenate(
        [grad_bias.reshape(devices, s), full_qkv_b.reshape(devices, q), full_fc1_b.reshape(devices, -1)],
        1,
    )
    kqk, kvo, sumsq, sumsv = after((kqk, kvo, sumsq, sumsv), block_out)
    for step in range(1, steps):
        giveq, givev = give(
            [([kqk, cq], sumsq, False, (0, 1)), ([kvo, cv], sumsv, True, (0, 1))], count
        )
        sumsq = sumsq + [flip(giveq, "dp", x_first[step])]
        sumsv = sumsv + [flip(givev, "dp", y_first[step])]
    k2, k1, sums2, sums1 = after((k2, k1, sums2, sums1), giveq, givev)
    grad_fc2_w, grad_fc1_w = final([k2, c2], sums2, block), final([k1, c1], sums1, block)
    sumsq, sumsv = after((sumsq, sumsv), grad_fc2_w, grad_fc1_w)
    grad_qkv_w, grad_out_w = final_attention([kqk, cq] + sumsq, [kvo, cv] + sumsv, block)
    grad_qkv_w = grad_qkv_w.swapaxes(0, 1)
    total, known = after((total, known), grad_out_w)
    *slot, vector_sums = norm_back(total, routed, cotangent[0], gain, at, data_count)
    firsts = send(slot)
    vector_sums = vector_sums.reshape(2, devices, s)
    sums = jnp.concatenate([vector_sums[0], vector_sums[1], known], 1)
    sums = swap_blocks(sums, data_index * tensor_count + tensor_index, 0, devices)
    sums = sums.reshape(data_count, tensor_count, -1).swapaxes(0, 1)
    sums = scatter_along(sums, "tensor")
    firsts, sums = after((firsts, sums))
    stacks = [route_more(f, last) for f, last in zip(firsts, lasts)]
    picks = picks_of(stacks, slot_of_seq)
    picks, sums = after((picks, sums))
    grad_input = route_ends(picks, slot_of_seq)[None]
    total = scatter_along(sums, "dp")
    return (
        block_out,
        grad_input,
        grad_qkv_w,
        grad_out_w,
        grad_fc1_w,
        grad_fc2_w,
        total[:s],
        total[s : 2 * s],
        total[3 * s : 3 * s + q],
        total[2 * s : 3 * s],
        total[3 * s + q :],
        total[2 * s : 3 * s],
    )


def solution(mesh):
    in_specs = (
        P("dp", "tensor", None),
        P("dp", "tensor", None),
        P(),
        P(),
        P(),
        P("dp", None, "tensor"),
        P("dp", "tensor"),
        P("dp", "tensor"),
        P("dp", "tensor"),
        P(("dp", "tensor")),
        P(("dp", "tensor")),
        P(("dp", "tensor")),
        P(("dp", "tensor")),
        P(("dp", "tensor")),
        P(("dp", "tensor")),
    )
    out_specs = (
        P("dp", "tensor", None),
        P("dp", "tensor", None),
        P("dp", None, "tensor"),
        P("dp", "tensor"),
        P("dp", "tensor"),
        P("dp", "tensor"),
        P(("dp", "tensor")),
        P(("dp", "tensor")),
        P(("dp", "tensor")),
        P(("dp", "tensor")),
        P(("dp", "tensor")),
        P(("dp", "tensor")),
    )
    return jax.shard_map(shards, mesh=mesh, in_specs=in_specs, out_specs=out_specs, check_vma=False)
```

```python
import functools
import math

import jax
import jax.numpy as jnp
from jax import lax
from jax.experimental import pallas as pl
from jax.experimental.pallas import tpu as pltpu
from jax.sharding import PartitionSpec as P

HEAD_DIM = 64
ROT = 32
PAIR = 2 * HEAD_DIM
VMEM = 63 * 1024 * 1024
SHARE = 0.4


eps = 1e-05
masked_score = -1e30
f32 = jnp.float32
bf16 = jnp.bfloat16
NN = (((1,), (0,)), ((), ()))
NT = (((1,), (1,)), ((), ()))
TN = (((0,), (0,)), ((), ()))
once = pl.Buffered(1)


def dot(a, b, dims):
    return lax.dot_general(a, b, dims, preferred_element_type=f32)


def params(mib):
    return pltpu.CompilerParams(vmem_limit_bytes=VMEM)


def cost(flops, nbytes, exps=0):
    return pl.CostEstimate(
        flops=int(flops * SHARE), bytes_accessed=int(nbytes * SHARE), transcendentals=int(exps * SHARE)
    )


def shape(dims, dtype):
    return jax.ShapeDtypeStruct(dims, dtype)


def turned(field, tables):
    cosine, ahead, behind = tables
    half = ROT // 2
    wide = field.shape[1]
    return (
        field * cosine
        + pltpu.roll(field, wide - half, 1) * ahead
        + pltpu.roll(field, half, 1) * behind
    )


def turned_back(grad, tables):
    cosine, ahead, behind = tables
    half = ROT // 2
    wide = grad.shape[1]
    return (
        grad * cosine
        + pltpu.roll(grad * ahead, half, 1)
        + pltpu.roll(grad * behind, wide - half, 1)
    )


def norm_kernel(blocks, at_ref, x_ref, gain_ref, shift_ref, *rest):
    out_ref, plain = rest[-2:]
    rows = x_ref[...].astype(f32)
    centred = rows - jnp.mean(rows, -1, keepdims=True)
    scale = lax.rsqrt(jnp.mean(centred * centred, -1, keepdims=True) + eps)
    plain[...] = (centred * scale * gain_ref[...] + shift_ref[...]).astype(bf16)
    wide = plain.shape[1] // blocks
    bits = blocks.bit_length() - 1
    for p in range(blocks):
        place = (at_ref[1] ^ reversed_bits(p, bits)) * wide
        out_ref[0, 0, :, p * wide : (p + 1) * wide] = plain[:, pl.ds(pl.multiple_of(place, wide), wide)]


def norm(rows_in, count, at, gain, shift, blocks):
    rows, width = rows_in.shape[0] // count, rows_in.shape[1]
    vector = pl.BlockSpec((1, width), lambda j, n: (0, 0))
    return pl.pallas_call(
        functools.partial(norm_kernel, blocks),
        grid_spec=pltpu.PrefetchScalarGridSpec(
            num_scalar_prefetch=1,
            grid=(count,),
            in_specs=[pl.BlockSpec((rows, width), lambda j, n: (j, 0)), vector, vector],
            out_specs=pl.BlockSpec((1, 1, rows, width), lambda j, n: (j, 0, 0, 0)),
            scratch_shapes=[pltpu.VMEM((rows, width), bf16)],
        ),
        out_shape=shape((count, 1, rows, width), bf16),
        compiler_params=params(32),
        cost_estimate=cost(10 * count * rows * width, 4 * count * rows * width),
        name="norm",
    )(at, rows_in, gain, shift)


def project_rows(kind, ln_ref, weight, bias_ref, tables, out_ref):
    rows = ln_ref.shape[0] * ln_ref.shape[2]
    many, size = ln_ref.shape[0], ln_ref.shape[2]
    raw = dot(ln_ref[...].reshape(rows, ln_ref.shape[3]), weight, NN) + bias_ref[0]

    @pl.when(kind < 2)
    def _():
        here = [t[...].reshape(rows, PAIR) for t in tables]
        for pair in range(raw.shape[1] // PAIR):
            cols = slice(pair * PAIR, (pair + 1) * PAIR)
            out_ref[0, :, 0, :, cols] = (
                turned(raw[:, cols], here).astype(bf16).reshape(many, size, PAIR)
            )

    @pl.when(kind == 2)
    def _():
        out_ref[0, :, 0] = raw.astype(bf16).reshape(many, size, raw.shape[1])


def assemble_start(refs, plan, column, size, buffer, sems):
    for j, (which, row, place, count) in enumerate(plan):
        pltpu.make_async_copy(
            refs[which].at[pl.ds(row, count), pl.ds(column, size)],
            buffer.at[pl.ds(place, count), :],
            sems.at[j],
        ).start()


def assemble_wait(refs, plan, column, size, buffer, sems):
    for j, (which, row, place, count) in enumerate(plan):
        pltpu.make_async_copy(
            refs[which].at[pl.ds(row, count), pl.ds(column, size)],
            buffer.at[pl.ds(place, count), :],
            sems.at[j],
        ).wait()


def project_kernel(qk_plan, vo_plan, ln_ref, bias_ref, c_ref, a_ref, b_ref, *rest):
    n = len({p[0] for p in qk_plan})
    qk_refs, vo_refs = rest[:n], rest[n : 2 * n]
    out_ref, w_ref, buffer, sems, out_sems = rest[2 * n :]
    kind = pl.program_id(0)
    heads = buffer.shape[2]
    sources = (
        (qk_refs, qk_plan, 0),
        (qk_refs, qk_plan, heads),
        (vo_refs, vo_plan, 0),
        (vo_refs, vo_plan, heads),
    )

    def drain(k):
        pltpu.make_async_copy(buffer.at[k % 2], w_ref.at[k], out_sems.at[k % 2]).wait()

    for k in range(4):
        refs, plan, column = sources[k]
        slot = k % 2

        @pl.when(kind == k)
        def _():
            if k == 0:
                assemble_start(refs, plan, column, heads, buffer.at[slot], sems.at[slot])
            assemble_wait(refs, plan, column, heads, buffer.at[slot], sems.at[slot])
            pltpu.make_async_copy(buffer.at[slot], w_ref.at[k], out_sems.at[slot]).start()
            if k >= 1:
                drain(k - 1)
            if k < 3:
                nrefs, nplan, ncolumn = sources[k + 1]
                assemble_start(
                    nrefs, nplan, ncolumn, heads, buffer.at[1 - slot], sems.at[1 - slot]
                )
            else:
                drain(k)

    @pl.when(kind < 3)
    def _():
        project_rows(kind, ln_ref, buffer[kind % 2], bias_ref, (c_ref, a_ref, b_ref), out_ref)


def project(ln, qk, vo, bias, tables):
    many, _, size, width = ln.shape
    heads = bias.shape[1]
    table = pl.BlockSpec((many, 1, size, PAIR), lambda i: (0, 0, 0, 0), pipeline_mode=once)
    hbm = pl.BlockSpec(memory_space=pl.ANY)
    last = lambda i: jnp.minimum(i, 2)
    return pl.pallas_call(
        functools.partial(project_kernel, qk[1], vo[1]),
        grid=(4,),
        in_specs=[
            pl.BlockSpec((many, 1, size, width), lambda i: (0, 0, 0, 0), pipeline_mode=once),
            pl.BlockSpec((1, 1, heads), lambda i: (last(i), 0, 0)),
            table,
            table,
            table,
        ]
        + [hbm] * (len(qk[0]) + len(vo[0])),
        out_specs=[
            pl.BlockSpec((1, many, 1, size, heads), lambda i: (last(i), 0, 0, 0, 0)),
            hbm,
        ],
        out_shape=[shape((3, many, 1, size, heads), bf16), shape((4, width, heads), bf16)],
        scratch_shapes=[
            pltpu.VMEM((2, width, heads), bf16),
            pltpu.SemaphoreType.DMA((2, len(qk[1]))),
            pltpu.SemaphoreType.DMA((2,)),
        ],
        compiler_params=params(48),
        cost_estimate=cost(6 * many * size * width * heads, 22 << 20),
        name="project",
    )(ln, bias[:, None, :], *tables, *qk[0], *vo[0])


def side_lanes(side):
    lane = lax.broadcasted_iota(jnp.int32, (1, PAIR), 1)
    return (lane // HEAD_DIM) == side


def masked_scores(keys, queries, first, length):
    scores = dot(keys, queries, NT)
    key = lax.broadcasted_iota(jnp.int32, scores.shape, 0)
    row = first + lax.broadcasted_iota(jnp.int32, (1, scores.shape[1]), 1)
    return jnp.where(key <= jnp.minimum(row, length - 1), scores, masked_score)


def attend_kernel(block, len_ref, q_ref, k_ref, v_ref, out_ref, total_ref, q_mine, v_turned):
    rows = q_ref.shape[1]
    zero = jnp.zeros((rows, PAIR), bf16)
    scale = jnp.asarray(1.0 / math.sqrt(HEAD_DIM), bf16)
    length = len_ref[0]
    for side in range(2):
        lanes = side_lanes(side)
        q_mine[side] = jnp.where(lanes, q_ref[0] * scale, zero)
    v_turned[...] = v_ref[0].T
    for first in range(0, rows, block):
        n = first + block
        r = slice(first, n)
        mixed = []
        for side in range(2):
            scores = masked_scores(k_ref[0, :n, :], q_mine[side, r, :], first, length)
            top = jnp.max(scores, 0, keepdims=True)
            exped = jnp.exp(scores - top)
            total = jnp.sum(exped, 0, keepdims=True)
            part = v_turned[side*HEAD_DIM:(side+1)*HEAD_DIM, :n]
            mixed.append(dot(part, exped.astype(bf16), NN) * (1.0 / total))
            total_ref[0, side:side+1, r] = top + jnp.log(total)
        out_ref[r, :] = jnp.concatenate(mixed, 0).T.astype(bf16)


def attend(qkv, length, block=512):
    _, rows, width = qkv.shape
    pairs = width // PAIR
    kind = lambda c: pl.BlockSpec((1, rows, PAIR), lambda h, n: (c, 0, h))
    return pl.pallas_call(functools.partial(attend_kernel, min(block, rows)),
        grid_spec=pltpu.PrefetchScalarGridSpec(num_scalar_prefetch=1, grid=(pairs,),
            in_specs=[kind(0), kind(1), kind(2)],
            out_specs=[pl.BlockSpec((rows, PAIR), lambda h, n: (0, h)), pl.BlockSpec((1, 2, rows), lambda h, n: (h, 0, 0))],
            scratch_shapes=[pltpu.VMEM((2, rows, PAIR), bf16), pltpu.VMEM((PAIR, rows), bf16)]),
        out_shape=[shape((rows, width), bf16), shape((pairs, 2, rows), f32)],
        compiler_params=params(48),
        cost_estimate=cost(16 * rows * rows * width, 4 << 20, rows * rows * 2 * pairs),
        name="attend")(length, qkv, qkv, qkv)


def attend_back_kernel(block, len_ref, q_ref, k_ref, v_ref, do_ref, total_ref, c_ref, a_ref, b_ref, grad_ref, q_mine, do_mine, k_turned, key_sum, value_sum):
    rows = q_ref.shape[1]
    zero = jnp.zeros((rows, PAIR), bf16)
    scale = 1.0 / math.sqrt(HEAD_DIM)
    for side in range(2):
        lanes = side_lanes(side)
        q_mine[side] = jnp.where(lanes, q_ref[0] * jnp.asarray(scale, bf16), zero)
        do_mine[side] = jnp.where(lanes, do_ref[...], zero)
    k_turned[...] = k_ref[0].T
    length = len_ref[0]
    tables_of = lambda r: (c_ref[r, :], a_ref[r, :], b_ref[r, :])
    for first in range(rows - block, -1, -block):
        n = first + block
        r = slice(first, n)
        gk = gv = None
        gq = []
        for side in range(2):
            scores = masked_scores(k_ref[0, :n, :], q_mine[side, r, :], first, length)
            probs = jnp.exp(scores - total_ref[0, side:side+1, r])
            grad_probs = dot(v_ref[0, :n, :], do_mine[side, r, :], NT)
            product = probs * grad_probs
            delta = jnp.sum(product, 0, keepdims=True)
            grad_scores = (product - probs * delta).astype(bf16)
            a = dot(grad_scores, q_mine[side, r, :], NN)
            b = dot(probs.astype(bf16), do_mine[side, r, :], NN)
            gk = a if gk is None else gk + a
            gv = b if gv is None else gv + b
            gq.append(dot(k_turned[side*HEAD_DIM:(side+1)*HEAD_DIM, :n], grad_scores, NN))
        if n == rows:
            key_sum[...] = gk
            value_sum[...] = gv
        else:
            key_sum[:n, :] += gk
            value_sum[:n, :] += gv
        grad_query = jnp.concatenate(gq, 0).T * scale
        grad_ref[0, r, :] = turned_back(grad_query, tables_of(r)).astype(bf16)
    for first in range(0, rows, block):
        r = slice(first, first + block)
        grad_ref[1, r, :] = turned_back(key_sum[r, :], tables_of(r)).astype(bf16)
        grad_ref[2, r, :] = value_sum[r, :].astype(bf16)


def attend_back(qkv, grad_mixed, totals, length, tables, block=512):
    _, rows, width = qkv.shape
    pairs = width // PAIR
    kind = lambda c: pl.BlockSpec((1, rows, PAIR), lambda h, n: (c, 0, h))
    table = pl.BlockSpec((rows, PAIR), lambda h, n: (0, 0))
    return pl.pallas_call(functools.partial(attend_back_kernel, min(block, rows)),
        grid_spec=pltpu.PrefetchScalarGridSpec(num_scalar_prefetch=1, grid=(pairs,),
            in_specs=[kind(0), kind(1), kind(2), pl.BlockSpec((rows, PAIR), lambda h, n: (0, h)), pl.BlockSpec((1, 2, rows), lambda h, n: (h, 0, 0)), table, table, table],
            out_specs=pl.BlockSpec((3, rows, PAIR), lambda h, n: (0, 0, h)),
            scratch_shapes=[pltpu.VMEM((2, rows, PAIR), bf16)]*2+[pltpu.VMEM((PAIR, rows), bf16)]+[pltpu.VMEM((rows, PAIR), f32)]*2),
        out_shape=shape((3, rows, width), bf16),
        compiler_params=params(48),
        cost_estimate=cost(40 * rows * rows * width, 8 << 20, rows * rows * 2 * pairs),
        name="attend_back")(length, qkv, qkv, qkv, grad_mixed, totals, *tables)


def feed_kernel(steps, late_steps, plan1, plan2, ln_ref, mixed_ref, wo_ref, bias_ref, *rest):
    n1 = len({p[0] for p in plan1})
    w1_refs, w2_refs = rest[:n1], rest[n1 : 2 * n1]
    (branch_ref, hidden_ref, slope_ref, full1_ref, full2_ref, held, buf1, buf2, sems1, sems2,
     out_sems) = rest[2 * n1 :]
    step = pl.program_id(0)
    slot = lax.rem(step, 2)
    tile_f = buf1.shape[2]
    tile_d = buf2.shape[1]
    c0 = math.sqrt(2.0 / math.pi)
    c1 = 0.044715
    plan2 = sorted(plan2, key=lambda p: p[2])
    per_tile = len(plan2) // late_steps

    def columns(s):
        return pl.ds(pl.multiple_of(s * tile_f, tile_f), tile_f)

    def start1(s):
        at = lax.rem(s, 2)
        column = pl.multiple_of(s * tile_f, tile_f)
        assemble_start(w1_refs, plan1, column, tile_f, buf1.at[at], sems1.at[at])

    def pieces2(tile):
        at = tile % 2
        for j, (which, row, place, count) in enumerate(plan2[tile * per_tile : (tile + 1) * per_tile]):
            yield pltpu.make_async_copy(
                w2_refs[which].at[pl.ds(row, count), :],
                buf2.at[at, pl.ds(place - tile * tile_d, count), :],
                sems2.at[at, j],
            )

    def out1(s, at):
        return pltpu.make_async_copy(buf1.at[at], full1_ref.at[:, columns(s)], out_sems.at[at])

    def out2(tile):
        return pltpu.make_async_copy(
            buf2.at[tile % 2], full2_ref.at[pl.ds(tile * tile_d, tile_d), :], out_sems.at[2 + tile % 2]
        )

    @pl.when(step == 0)
    def _():
        start1(0)
        for copy in pieces2(0):
            copy.start()

    @pl.when(step < steps)
    def _():
        column = pl.multiple_of(step * tile_f, tile_f)
        assemble_wait(w1_refs, plan1, column, tile_f, buf1.at[slot], sems1.at[slot])
        out1(step, slot).start()

        @pl.when(step > 0)
        def _():
            out1(step - 1, 1 - slot).wait()

        @pl.when(step < steps - 1)
        def _():
            start1(step + 1)

        pre = dot(ln_ref[...], buf1[slot], NN) + bias_ref[...]
        square = pre * pre
        bent = jnp.tanh(c0 * (pre + c1 * (square * pre)))
        half_pre = 0.5 * pre
        hidden = (half_pre * (1.0 + bent)).astype(bf16)
        hidden_ref[...] = hidden
        held[step] = hidden
        slope_ref[...] = 0.5 * (1.0 + bent) + half_pre * (1.0 - bent * bent) * (
            c0 * (1.0 + (3.0 * c1) * square)
        )

        @pl.when(step == steps - 1)
        def _():
            out1(step, slot).wait()

    for tile in range(late_steps):
        @pl.when(step == steps + tile)
        def _():
            for copy in pieces2(tile):
                copy.wait()
            out2(tile).start()
            if tile > 0:
                out2(tile - 1).wait()
            if tile < late_steps - 1:
                for copy in pieces2(tile + 1):
                    copy.start()
            total = dot(mixed_ref[...], wo_ref[0], NT)
            for k in range(steps):
                total += dot(held[k], buf2[tile % 2, :, k * tile_f : (k + 1) * tile_f], NT)
            branch_ref[...] = total.astype(bf16)
            if tile == late_steps - 1:
                out2(tile).wait()


def feed(ln, mixed, weights, w1, w2, bias, tile_f):
    rows, width = ln.shape
    hidden = bias.shape[1]
    heads = mixed.shape[1]
    steps = hidden // tile_f
    tile_d = 512
    late_steps = width // tile_d
    whole = lambda dims: pl.BlockSpec(dims, lambda i: (0, 0), pipeline_mode=once)
    early = lambda i: jnp.minimum(i, steps - 1)
    late = lambda i: jnp.maximum(i - steps, 0)
    by_row = pl.BlockSpec((rows, tile_f), lambda i: (0, early(i)))
    hbm = pl.BlockSpec(memory_space=pl.ANY)
    return pl.pallas_call(
        functools.partial(feed_kernel, steps, late_steps, w1[1], w2[1]),
        grid=(steps + late_steps,),
        in_specs=[
            whole((rows, width)),
            whole((rows, heads)),
            pl.BlockSpec((1, tile_d, heads), lambda i: (3, late(i), 0)),
            pl.BlockSpec((1, tile_f), lambda i: (0, early(i))),
        ]
        + [hbm] * (len(w1[0]) + len(w2[0])),
        out_specs=[
            pl.BlockSpec((rows, tile_d), lambda i: (0, late(i))), by_row, by_row, hbm, hbm
        ],
        out_shape=[
            shape((rows, width), bf16),
            shape((rows, hidden), bf16),
            shape((rows, hidden), f32),
            shape((width, hidden), bf16),
            shape((width, hidden), bf16),
        ],
        scratch_shapes=[
            pltpu.VMEM((steps, rows, tile_f), bf16),
            pltpu.VMEM((2, width, tile_f), bf16),
            pltpu.VMEM((2, tile_d, hidden), bf16),
            pltpu.SemaphoreType.DMA((2, len(w1[1]))),
            pltpu.SemaphoreType.DMA((2, len(w2[1]) // late_steps)),
            pltpu.SemaphoreType.DMA((4,)),
        ],
        compiler_params=params(58),
        cost_estimate=cost(4 * rows * width * hidden, 56 << 20, rows * hidden),
        name="feed",
    )(ln, mixed, weights, bias, *w1[0], *w2[0])


def back_kernel(steps, g_ref, w1_ref, w2_ref, slope_ref, wo_ref, sum_ref, pre_ref, mixed_ref, bias_ref, held):
    step = pl.program_id(0)
    tile = pre_ref.shape[1]

    @pl.when(step == 0)
    def _():
        mixed_ref[...] = dot(g_ref[...], wo_ref[0], NN).astype(bf16)

    @pl.when(step < steps)
    def _():
        grad = (dot(g_ref[...], w2_ref[...], NN) * slope_ref[...]).astype(bf16)
        pre_ref[...] = grad
        held[step] = grad
        bias_ref[...] = jnp.sum(grad.astype(f32), axis=0, keepdims=True)

    @pl.when(step >= steps)
    def _():
        total = dot(held[0], w1_ref[:, :tile], NT)
        for k in range(1, steps):
            total += dot(held[k], w1_ref[:, k * tile : (k + 1) * tile], NT)
        sum_ref[...] = total


def back(grads, w1, w2, slope, weights, tile_f):
    rows, width = grads.shape
    units = slope.shape[1]
    heads = weights.shape[2]
    steps = units // tile_f
    tile_d = 512
    whole = lambda dims: pl.BlockSpec(dims, lambda i: (0, 0), pipeline_mode=once)
    early = lambda i: jnp.minimum(i, steps - 1)
    late = lambda i: jnp.maximum(i - steps, 0)
    by_row = pl.BlockSpec((rows, tile_f), lambda i: (0, early(i)))
    return pl.pallas_call(
        functools.partial(back_kernel, steps),
        grid=(steps + width // tile_d,),
        in_specs=[
            whole((rows, width)),
            pl.BlockSpec((tile_d, units), lambda i: (late(i), 0)),
            pl.BlockSpec((width, tile_f), lambda i: (0, early(i))),
            by_row,
            pl.BlockSpec((1, width, heads), lambda i: (3, 0, 0), pipeline_mode=once),
        ],
        out_specs=[
            pl.BlockSpec((rows, tile_d), lambda i: (0, late(i))),
            by_row,
            whole((rows, heads)),
            pl.BlockSpec((1, tile_f), lambda i: (0, early(i))),
        ],
        out_shape=[
            shape((rows, width), f32),
            shape((rows, units), bf16),
            shape((rows, heads), bf16),
            shape((1, units), f32),
        ],
        scratch_shapes=[pltpu.VMEM((steps, rows, tile_f), bf16)],
        compiler_params=params(58),
        cost_estimate=cost(4 * rows * width * units, 40 << 20),
        name="back",
    )(grads, w1, w2, slope, weights)


def feed_weight_kernel(left_ref, right_ref, near_ref, far_ref):
    half = left_ref.shape[1] // 2
    far_ref[...] = dot(left_ref[:, half:], right_ref[...], TN).astype(bf16)
    near_ref[...] = dot(left_ref[:, :half], right_ref[...], TN).astype(bf16)


def feed_weight(left, right, tile_f):
    rows, width = left.shape
    units = right.shape[1]
    half = pl.BlockSpec((width // 2, tile_f), lambda i: (0, i))
    return pl.pallas_call(
        feed_weight_kernel,
        grid=(units // tile_f,),
        in_specs=[
            pl.BlockSpec((rows, width), lambda i: (0, 0), pipeline_mode=once),
            pl.BlockSpec((rows, tile_f), lambda i: (0, i)),
        ],
        out_specs=[half, half],
        out_shape=[shape((width // 2, units), bf16)] * 2,
        compiler_params=params(48),
        cost_estimate=cost(2 * rows * width * units, 16 << 20),
        name="feed_weight",
    )(left, right)


def ln_grad_kernel(grad_ref, w_ref, sum_ref, out_ref):
    total = sum_ref[...]
    for kind in range(3):
        total += dot(grad_ref[kind], w_ref[kind], NT)
    out_ref[...] = total.astype(bf16)


def ln_grad(grad_qkv, weights, partial_sum):
    _, rows, heads = grad_qkv.shape
    width = partial_sum.shape[1]
    tile = 512
    return pl.pallas_call(
        ln_grad_kernel,
        grid=(width // tile,),
        in_specs=[
            pl.BlockSpec((3, rows, heads), lambda i: (0, 0, 0), pipeline_mode=once),
            pl.BlockSpec((3, tile, heads), lambda i: (0, i, 0)),
            pl.BlockSpec((rows, tile), lambda i: (0, i)),
        ],
        out_specs=pl.BlockSpec((rows, tile), lambda i: (0, i)),
        out_shape=shape((rows, width), bf16),
        compiler_params=params(48),
        cost_estimate=cost(6 * rows * width * heads, 22 << 20),
        name="ln_grad",
    )(grad_qkv, weights, partial_sum)


def weight_grad_kernel(ln_ref, g_ref, grad_ref, mixed_ref, kqk_ref, kvo_ref, sqk_ref, svo_ref, bias_ref):
    heads = mixed_ref.shape[1]
    step = pl.program_id(0)
    steps = pl.num_programs(0)
    for kind in range(3):
        @pl.when(step == 0)
        def _():
            bias_ref[kind] = jnp.sum(grad_ref[kind].astype(f32), axis=0, keepdims=True)

    for qk_ref, vo_ref, here in ((kqk_ref, kvo_ref, step < steps // 2), (sqk_ref, svo_ref, step >= steps // 2)):
        @pl.when(here)
        def _():
            qk_ref[:, :heads] = dot(ln_ref[...], grad_ref[0], TN).astype(bf16)
            qk_ref[:, heads:] = dot(ln_ref[...], grad_ref[1], TN).astype(bf16)
            vo_ref[:, :heads] = dot(ln_ref[...], grad_ref[2], TN).astype(bf16)
            vo_ref[:, heads:] = dot(g_ref[...], mixed_ref[...], TN).astype(bf16)


def weight_grad(ln, grads, grad_qkv, mixed):
    rows, width = ln.shape
    heads = mixed.shape[1]
    half = width // 2
    tile = min(512, half)
    near = half // tile
    column = pl.BlockSpec((rows, tile), lambda i: (0, i))
    kept = pl.BlockSpec((tile, 2 * heads), lambda i: (jnp.minimum(i, near - 1), 0))
    sent = pl.BlockSpec((tile, 2 * heads), lambda i: (jnp.maximum(i - near, 0), 0))
    return pl.pallas_call(
        weight_grad_kernel,
        grid=(2 * near,),
        in_specs=[
            column,
            column,
            pl.BlockSpec((3, rows, heads), lambda i: (0, 0, 0), pipeline_mode=once),
            pl.BlockSpec((rows, heads), lambda i: (0, 0), pipeline_mode=once),
        ],
        out_specs=[kept, kept, sent, sent, pl.BlockSpec((3, 1, heads), lambda i: (0, 0, 0))],
        out_shape=[shape((half, 2 * heads), bf16)] * 4 + [shape((3, 1, heads), f32)],
        compiler_params=params(48),
        cost_estimate=cost(8 * rows * width * heads, 20 << 20),
        name="weight_grad",
    )(ln, grads, grad_qkv, mixed)


def give_kernel(counts, *refs):
    outs = refs[sum(counts) :]
    start = 0
    for number, out_ref in zip(counts, outs):
        total = refs[start][...].astype(f32)
        for ref in refs[start + 1 : start + number]:
            total += ref[...].astype(f32)
        out_ref[...] = total.astype(bf16)
        start += number


def give(items, count):
    specs, operands, numbers, outs = [], [], [], []
    for full, arrivals, low, part in items:
        rows, width = full[0].shape[0], full[0].shape[1] // part[1]
        block = rows // count
        level = len(arrivals) + 1
        out_count = count >> level
        place = (lambda i: (2 * i + 1) << (level - 1)) if low else (lambda i: out_count + i)
        for k in range(level):
            for array in full if k == 0 else [arrivals[k - 1]]:
                off = part[0] if k == 0 else 0
                specs.append(
                    pl.BlockSpec(
                        (block, width),
                        lambda i, k=k, off=off, low=low, place=place: (
                            place(i) >> k if low else place(i),
                            off,
                        ),
                    )
                )
                operands.append(array)
        numbers.append(len(full) + level - 1)
        outs.append(shape((out_count * block, width), bf16))
    moved = sum(o.shape[0] * o.shape[1] for o in outs)
    return pl.pallas_call(
        functools.partial(give_kernel, tuple(numbers)),
        grid=(out_count,),
        in_specs=specs,
        out_specs=[pl.BlockSpec((block, o.shape[1]), lambda i: (i, 0)) for o in outs],
        out_shape=outs,
        compiler_params=params(32),
        cost_estimate=cost(moved * 2, 6 * moved),
        name="give",
    )(*operands)


def norm_back_kernel(
    blocks, at_ref, sum_ref, rows_ref, cot_ref, gain_ref, first_ref, second_ref, vector_ref, held
):
    wide = rows_ref.shape[1] // blocks
    bits = blocks.bit_length() - 1
    for q in range(blocks):
        place = pl.multiple_of(reversed_bits(at_ref[1] ^ q, bits) * wide, wide)
        held[:, q * wide : (q + 1) * wide] = sum_ref[:, pl.ds(place, wide)]
    grad_ln = held[...].astype(f32)
    rows = rows_ref[...].astype(f32)
    centred = rows - jnp.mean(rows, -1, keepdims=True)
    inv_scale = lax.rsqrt(jnp.mean(centred * centred, -1, keepdims=True) + eps)
    normed = centred * inv_scale
    grad_norm = grad_ln * gain_ref[...]
    back = inv_scale * (
        grad_norm
        - jnp.mean(grad_norm, -1, keepdims=True)
        - normed * jnp.mean(grad_norm * normed, -1, keepdims=True)
    )
    slot = (cot_ref[...].astype(f32) + back).astype(bf16)
    half = first_ref.shape[0]
    first_ref[...] = slot[:half]
    second_ref[...] = slot[half:]
    vector_ref[0:1] = jnp.sum(grad_ln * normed, 0, keepdims=True)
    vector_ref[1:2] = jnp.sum(grad_ln, 0, keepdims=True)


def norm_back(total, rows_in, cot, gain, at, blocks):
    rows, width = rows_in.shape
    whole = pl.BlockSpec((rows, width), lambda i, n: (0, 0))
    vector = pl.BlockSpec((1, width), lambda i, n: (0, 0))
    return pl.pallas_call(
        functools.partial(norm_back_kernel, blocks),
        grid_spec=pltpu.PrefetchScalarGridSpec(
            num_scalar_prefetch=1,
            grid=(1,),
            in_specs=[whole, whole, whole, vector],
            out_specs=[pl.BlockSpec((rows // 2, width), lambda i, n: (0, 0))] * 2
            + [pl.BlockSpec((2, width), lambda i, n: (0, 0))],
            scratch_shapes=[pltpu.VMEM((rows, width), bf16)],
        ),
        out_shape=[shape((rows // 2, width), bf16)] * 2 + [shape((2, width), f32)],
        compiler_params=params(32),
        cost_estimate=cost(20 * rows * width, 8 * rows * width),
        name="norm_back",
    )(at, total, rows_in, cot, gain)


def final_kernel(parts, levels, *refs):
    full, rest, out_ref = refs[:2], refs[2:-1], refs[-1]
    base = full[0][...].astype(f32) + full[1][...].astype(f32)
    for part in range(parts):
        @pl.when(pl.program_id(0) == part)
        def _():
            total = base
            for ref in rest[part * levels : (part + 1) * levels]:
                total += ref[...].astype(f32)
            out_ref[...] = total


def final(full, sums, block):
    parts, levels = len(sums), len(sums[0])
    width = full[0].shape[1]
    wide = width // parts
    piece = pl.BlockSpec((block, wide), lambda i: (0, i))
    held = pl.BlockSpec((block, wide), lambda i: (0, 0))
    return pl.pallas_call(
        functools.partial(final_kernel, parts, levels),
        grid=(parts,),
        in_specs=[piece, piece] + [held] * (parts * levels),
        out_specs=piece,
        out_shape=shape((block, width), f32),
        compiler_params=params(32),
        cost_estimate=cost(4 * block * width, 12 * block * width),
        name="final",
    )(*full, *[f for s in sums for f in s])


def finish_kernel(blocks, at_ref, sum_ref, rows_ref, bias_a_ref, bias_b_ref, out_ref, held):
    rows, width = rows_ref.shape
    wide = width // blocks
    bits = blocks.bit_length() - 1
    for q in range(blocks):
        place = pl.multiple_of(reversed_bits(at_ref[1] ^ q, bits) * wide, wide)
        held[:, q * wide : (q + 1) * wide] = sum_ref[:, pl.ds(place, wide)]
    branch = held[...].astype(f32) + bias_a_ref[...] + bias_b_ref[...]
    position = at_ref[0] * rows + lax.broadcasted_iota(jnp.int32, (rows, 1), 0)
    branch = jnp.where(position < at_ref[2], branch, 0.0)
    out_ref[...] = (rows_ref[...].astype(f32) + branch).astype(bf16)


def finish(branch_sum, rows_in, bias_a, bias_b, at, blocks):
    rows, width = rows_in.shape
    whole = pl.BlockSpec((rows, width), lambda i, n: (0, 0))
    vector = pl.BlockSpec((1, width), lambda i, n: (0, 0))
    return pl.pallas_call(
        functools.partial(finish_kernel, blocks),
        grid_spec=pltpu.PrefetchScalarGridSpec(
            num_scalar_prefetch=1,
            grid=(1,),
            in_specs=[whole, whole, vector, vector],
            out_specs=whole,
            scratch_shapes=[pltpu.VMEM((rows, width), bf16)],
        ),
        out_shape=shape((rows, width), bf16),
        compiler_params=params(32),
        cost_estimate=cost(8 * rows * width, 6 * rows * width),
        name="finish",
    )(at, branch_sum, rows_in, bias_a, bias_b)


def final_attention_kernel(levels, *refs):
    heads = refs[0].shape[1] // 2
    grad_ref, out_ref = refs[-2:]
    totals = []
    for start in (0, levels + 2):
        total = refs[start][...].astype(f32)
        for ref in refs[start + 1 : start + levels + 2]:
            total += ref[...].astype(f32)
        totals.append(total)
    grad_ref[0] = totals[0][:, :heads]
    grad_ref[1] = totals[0][:, heads:]
    grad_ref[2] = totals[1][:, :heads]
    out_ref[...] = totals[1][:, heads:]


def final_attention(qk, vo, block):
    levels = len(qk) - 2
    width = qk[0].shape[1]
    piece = pl.BlockSpec((block, width), lambda i: (0, 0))
    return pl.pallas_call(
        functools.partial(final_attention_kernel, levels),
        grid=(1,),
        in_specs=[piece] * (2 * levels + 4),
        out_specs=[
            pl.BlockSpec((3, block, width // 2), lambda i: (0, 0, 0)),
            pl.BlockSpec((block, width // 2), lambda i: (0, 0)),
        ],
        out_shape=[shape((3, block, width // 2), f32), shape((block, width // 2), f32)],
        compiler_params=params(32),
        cost_estimate=cost(8 * block * width, 24 * block * width),
        name="final_attention",
    )(*qk, *vo)


def rotary_tables(rows, col_count):
    half_rot = ROT // 2
    column = jnp.arange(col_count) % HEAD_DIM
    exponent = (2 * (column % half_rot)).astype(jnp.float32) / ROT
    frequency = jnp.exp(-math.log(10000.0) * exponent)
    angles = rows.astype(jnp.float32)[:, None] * frequency[None, :]
    inside = column < ROT
    cosine = jnp.where(inside, jnp.cos(angles), 1.0)
    sine_part = jnp.sin(angles)
    ahead_sin = jnp.where(column < half_rot, -sine_part, 0.0)
    behind_sin = jnp.where(inside & (column >= half_rot), sine_part, 0.0)
    return (cosine, ahead_sin, behind_sin)


def flip(array, axis_name, bit):
    size = lax.axis_size(axis_name)
    return lax.ppermute(array, axis_name, [(i, i ^ (1 << bit)) for i in range(size)])


def bits_of(size):
    return size.bit_length() - 1


def swap_blocks(array, index, axis, blocks):
    for bit in range(bits_of(blocks)):
        dims = array.shape
        parts = dims[:axis] + (blocks >> (bit + 1), 2, 1 << bit, dims[axis] // blocks)
        view = array.reshape(parts + dims[axis + 1 :])
        other = jnp.flip(view, axis=axis + 1)
        array = jnp.where((index >> bit) & 1 == 1, other, view).reshape(dims)
    return array


def reversed_bits(value, bits):
    return sum(((value >> k) & 1) << (bits - 1 - k) for k in range(bits))


def xor_columns(array, index, blocks):
    width = array.shape[-1] // blocks
    bits = bits_of(blocks)
    pieces = [
        lax.dynamic_slice_in_dim(
            array, (index ^ reversed_bits(p, bits)) * width, width, array.ndim - 1
        )
        for p in range(blocks)
    ]
    return jnp.concatenate(pieces, -1)


def plain_columns(array, index, blocks):
    width = array.shape[-1] // blocks
    bits = bits_of(blocks)
    pieces = []
    for q in range(blocks):
        place = reversed_bits(index ^ q, bits)
        pieces.append(lax.dynamic_slice_in_dim(array, place * width, width, array.ndim - 1))
    return jnp.concatenate(pieces, -1)


def gather_step(stacks, bit):
    return stacks + [(flip(rows, "dp", bit), [m | (1 << bit) for m in masks]) for rows, masks in stacks]


def joined_step(stacks, bit):
    rows = jnp.concatenate([s[0] for s in stacks], 0)
    return stacks + [(flip(rows, "dp", bit), [m | (1 << bit) for s in stacks for m in s[1]])]


def gather_plan(stacks, block, bits):
    plan = []
    for which, (_, masks) in enumerate(stacks):
        for i, m in enumerate(masks):
            plan.append((which, i * block, reversed_bits(m, bits) * block, block))
    return [s[0] for s in stacks], tuple(plan)


def core_copies(stacks):
    return [(flip(rows, "dp", 0), [m | 1 for m in masks]) for rows, masks in stacks]


def route_order(last):
    return [b for b in range(bits_of(lax.axis_size("dp")) - 1, -1, -1) if b != last]


def route_first(block, last):
    return jnp.stack([block, flip(block, "dp", route_order(last)[0])], 0)


def route_more(stack, last):
    order = route_order(last)[1:]
    for bit in order[:-1]:
        stack = jnp.concatenate([stack, flip(stack, "dp", bit)], 0)
    return (stack, flip(stack, "dp", order[-1]))


def route_picks(halves, wanted, index, last):
    order = route_order(last)
    count = halves[0].shape[0]

    def pick(want):
        mask = index ^ want
        at = sum(((mask >> bit) & 1) << k for k, bit in enumerate(order))
        found = [lax.dynamic_index_in_dim(h, at % count, 0, keepdims=False) for h in halves]
        return found[0] if len(found) == 1 else jnp.where(at < count, found[0], found[1])

    return pick(wanted[index ^ (1 << last)]), pick(wanted[index])


def route_end(given, held, wanted, index, last):
    arrived = flip(given, "dp", last)
    return jnp.where(((index ^ wanted[index]) >> last) & 1 == 1, arrived, held)


def gather_small(stack, axis_name):
    for bit in range(bits_of(lax.axis_size(axis_name))):
        stack = jnp.concatenate([stack, flip(stack, axis_name, bit)], 0)
    return stack


def scatter_along(stack, axis_name):
    bits = bits_of(lax.axis_size(axis_name))
    stack = stack.reshape((2,) * bits + stack.shape[1:])
    stack = stack.transpose(tuple(range(bits - 1, -1, -1)) + tuple(range(bits, stack.ndim)))
    for bit in range(bits):
        stack = stack[0] + flip(stack[1], axis_name, bit)
    return stack


def after(values, *others):
    held = lax.optimization_barrier((tuple(values), tuple(others)))
    return held[0]


def shards(
    hidden_in,
    cotangent,
    lengths,
    slot_of_seq,
    seq_of_slot,
    qkv_weight,
    out_weight,
    fc1_weight,
    fc2_weight,
    ln_gain,
    ln_bias,
    qkv_bias,
    out_bias,
    fc1_bias,
    fc2_bias,
):
    rows_here = hidden_in.shape[1]
    width = hidden_in.shape[2]
    tensor_count = lax.axis_size("tensor")
    data_count = lax.axis_size("dp")
    tensor_index = lax.axis_index("tensor")
    data_index = lax.axis_index("dp")
    seq_len = rows_here * tensor_count
    heads_local = qkv_weight.shape[2]
    hidden_local = fc1_weight.shape[1]
    block = width // data_count
    length = lengths[seq_of_slot[data_index]]
    bits = bits_of(data_count)
    x_first = list(range(1, bits))
    y_first = x_first[::-1]
    tile_f = min(512, hidden_local)

    lasts = (bits - 1, bits - 2)
    wave_rows = rows_here // 2
    at = jnp.stack([tensor_index, data_index, length]).astype(jnp.int32)

    def send(parts):
        return [route_first(h, last) for h, last in zip(parts, lasts)]

    def picks_of(stacks, wanted):
        return [route_picks(f, wanted, data_index, last) for f, last in zip(stacks, lasts)]

    def route_ends(picks, wanted):
        return jnp.concatenate(
            [route_end(g, k, wanted, data_index, last) for (g, k), last in zip(picks, lasts)], 0
        )

    def receive(firsts, wanted):
        stacks = [route_more(f, last) for f, last in zip(firsts, lasts)]
        stacks = [(jnp.concatenate(halves, 0),) for halves in stacks]
        return route_ends(picks_of(stacks, wanted), wanted)

    firsts = send((hidden_in[0, :wave_rows], hidden_in[0, wave_rows:]))
    vectors = [ln_gain, ln_bias, out_bias, fc2_bias, qkv_bias, fc1_bias]
    s = ln_gain.shape[0]
    vectors = after(vectors, *firsts)
    small = jnp.concatenate([v.reshape(-1, s) for v in vectors], 0)
    stack = gather_small(small[None], "tensor")
    routed = receive(firsts, seq_of_slot)
    routed, stack = after((routed, stack))
    extra_rows = 16
    full = lax.all_gather(routed, "tensor", axis=0, tiled=True)

    stack = swap_blocks(stack, tensor_index, 0, tensor_count).reshape(-1)
    extra = jnp.pad(stack, (0, extra_rows * 2 * heads_local - stack.shape[0]))
    qk_shard = jnp.concatenate(
        [qkv_weight[:, :2].reshape(block, 2 * heads_local), extra.reshape(extra_rows, 2 * heads_local)], 0
    )
    vo_shard = jnp.concatenate([qkv_weight[:, 2], out_weight], 1)
    qk_shard, vo_shard = after((qk_shard, vo_shard), routed)
    qk_stacks = gather_step([(qk_shard, [0])], x_first[0])
    vo_stacks = gather_step([(vo_shard, [0])], y_first[0])
    for step in range(1, len(x_first)):
        qk_stacks = gather_step(qk_stacks, x_first[step])
        vo_stacks = gather_step(vo_stacks, y_first[step])

    def held_back(groups, *values):
        flat = [rows for stacks in groups for rows, _ in stacks]
        out = list(after(tuple(flat) + values))
        fresh = [[(out.pop(0), masks) for _, masks in stacks] for stacks in groups]
        return fresh, out

    row_ids, = after((jnp.arange(seq_len, dtype=jnp.int32),), qk_shard)
    tables = rotary_tables(row_ids, PAIR)
    (qk_stacks, vo_stacks), (fc1_shard, fc2_shard, *tables) = held_back(
        (qk_stacks, vo_stacks), fc1_weight, fc2_weight, *tables
    )
    qk_stacks = qk_stacks + core_copies(qk_stacks)
    qk = gather_plan(qk_stacks, block, bits)
    by_mask = sorted(qk_stacks, key=lambda st: st[1][0])
    gathered = jnp.stack([rows[block:].reshape(-1)[: stack.shape[0]] for rows, _ in by_mask], 0)
    gathered = swap_blocks(gathered, data_index, 0, data_count)
    gathered = gathered.reshape(data_count, tensor_count, -1)
    vo = gather_plan(vo_stacks + core_copies(vo_stacks), block, bits)
    fc1_stacks = gather_step([(fc1_shard, [0])], x_first[0])
    fc2_stacks = gather_step([(fc2_shard, [0])], y_first[0])

    positions = tensor_index * rows_here + jnp.arange(rows_here, dtype=jnp.int32)
    valid = (positions < length)[:, None]
    cot_rows = cotangent[0]
    low_plain = jnp.where(valid, cot_rows, jnp.zeros_like(cot_rows))
    low, = after((low_plain,), routed)
    low = xor_columns(low, data_index, data_count)
    grads = lax.all_gather(low, "tensor", axis=0, tiled=True)

    gain, shift, bias_a, bias_b = [
        gathered[:, :, i * s : (i + 1) * s].reshape(1, width).astype(f32) for i in range(4)
    ]
    q = qkv_bias.shape[0]
    bias_qkv = lax.dynamic_slice_in_dim(
        gathered[:, :, 4 * s : 4 * s + q].reshape(3, width), tensor_index * heads_local, heads_local, 1
    ).astype(f32)
    bias_fc1 = lax.dynamic_slice_in_dim(
        gathered[:, :, 4 * s + q :].reshape(1, hidden_local * tensor_count),
        tensor_index * hidden_local,
        hidden_local,
        1,
    ).astype(f32)

    row_tables = [v.reshape(tensor_count, 1, rows_here, PAIR) for v in tables]
    size = length.reshape(1)
    (fc1_stacks, fc2_stacks), (gain, shift) = held_back((fc1_stacks, fc2_stacks), gain, shift)
    fc1_far, fc2_far = core_copies(fc1_stacks), core_copies(fc2_stacks)
    for step in range(1, len(x_first)):
        fc1_stacks = joined_step(fc1_stacks, x_first[step])
        fc2_stacks = joined_step(fc2_stacks, y_first[step])
    ln = norm(full, tensor_count, at, gain, shift, data_count)
    (fc1_far, fc2_far), (ln,) = held_back((fc1_far, fc2_far), ln)
    qkv, weights = project(ln, qk, vo, bias_qkv, row_tables)
    ln, qkv = ln.reshape(seq_len, width), qkv.reshape(3, seq_len, heads_local)
    mixed, totals = attend(qkv, size)
    (fc1_stacks, fc2_stacks), (mixed,) = held_back((fc1_stacks, fc2_stacks), mixed)
    fc1_far = fc1_far + core_copies(fc1_stacks[2:])
    fc2_far = fc2_far + core_copies(fc2_stacks[2:])
    w1 = gather_plan(fc1_stacks + fc1_far, block, bits)
    w2 = gather_plan(fc2_stacks + fc2_far, block, bits)
    branch, hidden, slope, full1, full2 = feed(ln, mixed, weights, w1, w2, bias_fc1, tile_f)
    branch, grads = after((branch, grads))
    branch = lax.psum_scatter(branch, "tensor", scatter_dimension=0, tiled=True)

    count = data_count // 2
    steps = len(x_first)
    feed_sum, grad_pre, grad_mixed, grad_fc1_b = back(grads, full1, full2, slope, weights, tile_f)
    hidden, = after((hidden,), grad_pre)
    k2, s2 = feed_weight(grads, hidden, tile_f)
    c2 = flip(s2, "dp", 0)
    grad_pre, = after((grad_pre,), s2)
    k1, s1 = feed_weight(ln, grad_pre, tile_f)
    c1 = flip(s1, "dp", 0)

    pair = ((0, 2), (1, 2))
    both = (x_first, y_first)

    def gives_of(full, sums):
        return give([(full, s, low, p) for s, low, p in zip(sums, (False, True), pair)], count)

    def send_on(gives, step):
        return [flip(g, "dp", order[step]) for g, order in zip(gives, both)]

    k2, c2 = after((k2, c2), s1)
    gives2 = gives_of([k2, c2], ([], []))
    sums2 = [[f] for f in send_on(gives2, 0)]
    k1, c1 = after((k1, c1), *gives2)
    gives1 = gives_of([k1, c1], ([], []))
    sums1 = [[f] for f in send_on(gives1, 0)]
    grad_mixed, = after((grad_mixed,), *gives1)
    grad_qkv = attend_back(qkv, grad_mixed, totals, size, tables)
    kqk, kvo, sqk, svo, grad_qkv_b = weight_grad(ln, grads, grad_qkv, mixed)
    cq, cv = flip(sqk, "dp", 0), flip(svo, "dp", 0)
    grad_qkv, branch, sums2, sums1 = after((grad_qkv, branch, sums2, sums1), sqk)
    ln_part = ln_grad(grad_qkv, weights, feed_sum)
    total = lax.psum_scatter(ln_part, "tensor", scatter_dimension=0, tiled=True)
    kqk, kvo, cq, cv = after((kqk, kvo, cq, cv), ln_part)
    giveq, givev = give(
        [([kqk, cq], [], False, (0, 1)), ([kvo, cv], [], True, (0, 1))], count
    )
    sumsq, sumsv = [flip(giveq, "dp", x_first[0])], [flip(givev, "dp", y_first[0])]
    k2, = after((k2,), giveq, givev)
    for step in range(1, steps):
        gives2 = gives_of([k2, c2], sums2)
        sums2 = [s + [f] for s, f in zip(sums2, send_on(gives2, step))]
    k1, = after((k1,), *gives2)
    for step in range(1, steps):
        gives1 = gives_of([k1, c1], sums1)
        sums1 = [s + [f] for s, f in zip(sums1, send_on(gives1, step))]
    branch, = after((branch,), *gives1)
    block_out = finish(branch, routed, bias_a, bias_b, at, data_count)[None]
    grad_bias = jnp.sum(low_plain.astype(f32), axis=0)
    devices = data_count * tensor_count
    full_qkv_b = lax.dynamic_update_slice_in_dim(
        jnp.zeros((3, width), f32), grad_qkv_b[:, 0], tensor_index * heads_local, 1
    )
    full_fc1_b = lax.dynamic_update_slice_in_dim(
        jnp.zeros((hidden_local * tensor_count,), f32), grad_fc1_b[0], tensor_index * hidden_local, 0
    )
    known = jnp.concatenate(
        [grad_bias.reshape(devices, s), full_qkv_b.reshape(devices, q), full_fc1_b.reshape(devices, -1)],
        1,
    )
    kqk, kvo, sumsq, sumsv = after((kqk, kvo, sumsq, sumsv), block_out)
    for step in range(1, steps):
        giveq, givev = give(
            [([kqk, cq], sumsq, False, (0, 1)), ([kvo, cv], sumsv, True, (0, 1))], count
        )
        sumsq = sumsq + [flip(giveq, "dp", x_first[step])]
        sumsv = sumsv + [flip(givev, "dp", y_first[step])]
    k2, k1, sums2, sums1 = after((k2, k1, sums2, sums1), giveq, givev)
    grad_fc2_w, grad_fc1_w = final([k2, c2], sums2, block), final([k1, c1], sums1, block)
    sumsq, sumsv = after((sumsq, sumsv), grad_fc2_w, grad_fc1_w)
    grad_qkv_w, grad_out_w = final_attention([kqk, cq] + sumsq, [kvo, cv] + sumsv, block)
    grad_qkv_w = grad_qkv_w.swapaxes(0, 1)
    total, known = after((total, known), grad_out_w)
    *slot, vector_sums = norm_back(total, routed, cotangent[0], gain, at, data_count)
    firsts = send(slot)
    vector_sums = vector_sums.reshape(2, devices, s)
    sums = jnp.concatenate([vector_sums[0], vector_sums[1], known], 1)
    sums = swap_blocks(sums, data_index * tensor_count + tensor_index, 0, devices)
    sums = sums.reshape(data_count, tensor_count, -1).swapaxes(0, 1)
    sums = scatter_along(sums, "tensor")
    firsts, sums = after((firsts, sums))
    stacks = [route_more(f, last) for f, last in zip(firsts, lasts)]
    picks = picks_of(stacks, slot_of_seq)
    picks, sums = after((picks, sums))
    grad_input = route_ends(picks, slot_of_seq)[None]
    total = scatter_along(sums, "dp")
    return (
        block_out,
        grad_input,
        grad_qkv_w,
        grad_out_w,
        grad_fc1_w,
        grad_fc2_w,
        total[:s],
        total[s : 2 * s],
        total[3 * s : 3 * s + q],
        total[2 * s : 3 * s],
        total[3 * s + q :],
        total[2 * s : 3 * s],
    )


def solution(mesh):
    in_specs = (
        P("dp", "tensor", None),
        P("dp", "tensor", None),
        P(),
        P(),
        P(),
        P("dp", None, "tensor"),
        P("dp", "tensor"),
        P("dp", "tensor"),
        P("dp", "tensor"),
        P(("dp", "tensor")),
        P(("dp", "tensor")),
        P(("dp", "tensor")),
        P(("dp", "tensor")),
        P(("dp", "tensor")),
        P(("dp", "tensor")),
    )
    out_specs = (
        P("dp", "tensor", None),
        P("dp", "tensor", None),
        P("dp", None, "tensor"),
        P("dp", "tensor"),
        P("dp", "tensor"),
        P("dp", "tensor"),
        P(("dp", "tensor")),
        P(("dp", "tensor")),
        P(("dp", "tensor")),
        P(("dp", "tensor")),
        P(("dp", "tensor")),
        P(("dp", "tensor")),
    )
    return jax.shard_map(shards, mesh=mesh, in_specs=in_specs, out_specs=out_specs, check_vma=False)
```

```python
import functools
import math

import jax
import jax.numpy as jnp
from jax import lax
from jax.experimental import pallas as pl
from jax.experimental.pallas import tpu as pltpu
from jax.sharding import PartitionSpec as P

HEAD_DIM = 64
ROT = 32
PAIR = 2 * HEAD_DIM
VMEM = 63 * 1024 * 1024
SHARE = 0.4


eps = 1e-05
masked_score = -1e30
f32 = jnp.float32
bf16 = jnp.bfloat16
NN = (((1,), (0,)), ((), ()))
NT = (((1,), (1,)), ((), ()))
TN = (((0,), (0,)), ((), ()))
once = pl.Buffered(1)


def dot(a, b, dims):
    return lax.dot_general(a, b, dims, preferred_element_type=f32)


def params(mib):
    return pltpu.CompilerParams(vmem_limit_bytes=VMEM)


def cost(flops, nbytes, exps=0):
    return pl.CostEstimate(
        flops=int(flops * SHARE), bytes_accessed=int(nbytes * SHARE), transcendentals=int(exps * SHARE)
    )


def shape(dims, dtype):
    return jax.ShapeDtypeStruct(dims, dtype)


def turned(field, tables):
    cosine, ahead, behind = tables
    half = ROT // 2
    wide = field.shape[1]
    return (
        field * cosine
        + pltpu.roll(field, wide - half, 1) * ahead
        + pltpu.roll(field, half, 1) * behind
    )


def turned_back(grad, tables):
    cosine, ahead, behind = tables
    half = ROT // 2
    wide = grad.shape[1]
    return (
        grad * cosine
        + pltpu.roll(grad * ahead, half, 1)
        + pltpu.roll(grad * behind, wide - half, 1)
    )


def norm_kernel(blocks, at_ref, x_ref, gain_ref, shift_ref, *rest):
    out_ref, plain = rest[-2:]
    rows = x_ref[...].astype(f32)
    centred = rows - jnp.mean(rows, -1, keepdims=True)
    scale = lax.rsqrt(jnp.mean(centred * centred, -1, keepdims=True) + eps)
    plain[...] = (centred * scale * gain_ref[...] + shift_ref[...]).astype(bf16)
    wide = plain.shape[1] // blocks
    bits = blocks.bit_length() - 1
    for p in range(blocks):
        place = (at_ref[1] ^ reversed_bits(p, bits)) * wide
        out_ref[0, 0, :, p * wide : (p + 1) * wide] = plain[:, pl.ds(pl.multiple_of(place, wide), wide)]


def norm(rows_in, count, at, gain, shift, blocks):
    rows, width = rows_in.shape[0] // count, rows_in.shape[1]
    vector = pl.BlockSpec((1, width), lambda j, n: (0, 0))
    return pl.pallas_call(
        functools.partial(norm_kernel, blocks),
        grid_spec=pltpu.PrefetchScalarGridSpec(
            num_scalar_prefetch=1,
            grid=(count,),
            in_specs=[pl.BlockSpec((rows, width), lambda j, n: (j, 0)), vector, vector],
            out_specs=pl.BlockSpec((1, 1, rows, width), lambda j, n: (j, 0, 0, 0)),
            scratch_shapes=[pltpu.VMEM((rows, width), bf16)],
        ),
        out_shape=shape((count, 1, rows, width), bf16),
        compiler_params=params(32),
        cost_estimate=cost(10 * count * rows * width, 4 * count * rows * width),
        name="norm",
    )(at, rows_in, gain, shift)


def project_rows(kind, ln_ref, weight, bias_ref, tables, out_ref):
    rows = ln_ref.shape[0] * ln_ref.shape[2]
    many, size = ln_ref.shape[0], ln_ref.shape[2]
    raw = dot(ln_ref[...].reshape(rows, ln_ref.shape[3]), weight, NN) + bias_ref[0]

    @pl.when(kind < 2)
    def _():
        here = [t[...].reshape(rows, PAIR) for t in tables]
        for pair in range(raw.shape[1] // PAIR):
            cols = slice(pair * PAIR, (pair + 1) * PAIR)
            out_ref[0, :, 0, :, cols] = (
                turned(raw[:, cols], here).astype(bf16).reshape(many, size, PAIR)
            )

    @pl.when(kind == 2)
    def _():
        out_ref[0, :, 0] = raw.astype(bf16).reshape(many, size, raw.shape[1])


def assemble_start(refs, plan, column, size, buffer, sems):
    for j, (which, row, place, count) in enumerate(plan):
        pltpu.make_async_copy(
            refs[which].at[pl.ds(row, count), pl.ds(column, size)],
            buffer.at[pl.ds(place, count), :],
            sems.at[j],
        ).start()


def assemble_wait(refs, plan, column, size, buffer, sems):
    for j, (which, row, place, count) in enumerate(plan):
        pltpu.make_async_copy(
            refs[which].at[pl.ds(row, count), pl.ds(column, size)],
            buffer.at[pl.ds(place, count), :],
            sems.at[j],
        ).wait()


def project_kernel(qk_plan, vo_plan, ln_ref, bias_ref, c_ref, a_ref, b_ref, *rest):
    n = len({p[0] for p in qk_plan})
    qk_refs, vo_refs = rest[:n], rest[n : 2 * n]
    out_ref, w_ref, buffer, sems, out_sems = rest[2 * n :]
    kind = pl.program_id(0)
    heads = buffer.shape[2]
    sources = (
        (qk_refs, qk_plan, 0),
        (qk_refs, qk_plan, heads),
        (vo_refs, vo_plan, 0),
        (vo_refs, vo_plan, heads),
    )

    def drain(k):
        pltpu.make_async_copy(buffer.at[k % 2], w_ref.at[k], out_sems.at[k % 2]).wait()

    for k in range(4):
        refs, plan, column = sources[k]
        slot = k % 2

        @pl.when(kind == k)
        def _():
            if k == 0:
                assemble_start(refs, plan, column, heads, buffer.at[slot], sems.at[slot])
            assemble_wait(refs, plan, column, heads, buffer.at[slot], sems.at[slot])
            pltpu.make_async_copy(buffer.at[slot], w_ref.at[k], out_sems.at[slot]).start()
            if k >= 1:
                drain(k - 1)
            if k < 3:
                nrefs, nplan, ncolumn = sources[k + 1]
                assemble_start(
                    nrefs, nplan, ncolumn, heads, buffer.at[1 - slot], sems.at[1 - slot]
                )
            else:
                drain(k)

    @pl.when(kind < 3)
    def _():
        project_rows(kind, ln_ref, buffer[kind % 2], bias_ref, (c_ref, a_ref, b_ref), out_ref)


def project(ln, qk, vo, bias, tables):
    many, _, size, width = ln.shape
    heads = bias.shape[1]
    table = pl.BlockSpec((many, 1, size, PAIR), lambda i: (0, 0, 0, 0), pipeline_mode=once)
    hbm = pl.BlockSpec(memory_space=pl.ANY)
    last = lambda i: jnp.minimum(i, 2)
    return pl.pallas_call(
        functools.partial(project_kernel, qk[1], vo[1]),
        grid=(4,),
        in_specs=[
            pl.BlockSpec((many, 1, size, width), lambda i: (0, 0, 0, 0), pipeline_mode=once),
            pl.BlockSpec((1, 1, heads), lambda i: (last(i), 0, 0)),
            table,
            table,
            table,
        ]
        + [hbm] * (len(qk[0]) + len(vo[0])),
        out_specs=[
            pl.BlockSpec((1, many, 1, size, heads), lambda i: (last(i), 0, 0, 0, 0)),
            hbm,
        ],
        out_shape=[shape((3, many, 1, size, heads), bf16), shape((4, width, heads), bf16)],
        scratch_shapes=[
            pltpu.VMEM((2, width, heads), bf16),
            pltpu.SemaphoreType.DMA((2, len(qk[1]))),
            pltpu.SemaphoreType.DMA((2,)),
        ],
        compiler_params=params(48),
        cost_estimate=cost(6 * many * size * width * heads, 22 << 20),
        name="project",
    )(ln, bias[:, None, :], *tables, *qk[0], *vo[0])


def side_lanes(side):
    lane = lax.broadcasted_iota(jnp.int32, (1, PAIR), 1)
    return (lane // HEAD_DIM) == side


def masked_scores(keys, queries, first, length):
    scores = dot(keys, queries, NT)
    key = lax.broadcasted_iota(jnp.int32, scores.shape, 0)
    row = first + lax.broadcasted_iota(jnp.int32, (1, scores.shape[1]), 1)
    return jnp.where(key <= jnp.minimum(row, length - 1), scores, masked_score)


def attend_kernel(block, len_ref, q_ref, k_ref, v_ref, out_ref, total_ref, q_mine, v_turned):
    rows = q_ref.shape[1]
    zero = jnp.zeros((rows, PAIR), bf16)
    scale = jnp.asarray(1.0 / math.sqrt(HEAD_DIM), bf16)
    length = len_ref[0]
    for side in range(2):
        lanes = side_lanes(side)
        q_mine[side] = jnp.where(lanes, q_ref[0] * scale, zero)
    v_turned[...] = v_ref[0].T
    for first in range(0, rows, block):
        n = first + block
        r = slice(first, n)
        mixed = []
        for side in range(2):
            scores = masked_scores(k_ref[0, :n, :], q_mine[side, r, :], first, length)
            top = jnp.max(scores, 0, keepdims=True)
            exped = jnp.exp(scores - top)
            total = jnp.sum(exped, 0, keepdims=True)
            part = v_turned[side*HEAD_DIM:(side+1)*HEAD_DIM, :n]
            mixed.append(dot(part, exped.astype(bf16), NN) * (1.0 / total))
            total_ref[0, side:side+1, r] = top + jnp.log(total)
        out_ref[r, :] = jnp.concatenate(mixed, 0).T.astype(bf16)


def attend(qkv, length, block=512):
    _, rows, width = qkv.shape
    pairs = width // PAIR
    kind = lambda c: pl.BlockSpec((1, rows, PAIR), lambda h, n: (c, 0, h))
    return pl.pallas_call(functools.partial(attend_kernel, min(block, rows)),
        grid_spec=pltpu.PrefetchScalarGridSpec(num_scalar_prefetch=1, grid=(pairs,),
            in_specs=[kind(0), kind(1), kind(2)],
            out_specs=[pl.BlockSpec((rows, PAIR), lambda h, n: (0, h)), pl.BlockSpec((1, 2, rows), lambda h, n: (h, 0, 0))],
            scratch_shapes=[pltpu.VMEM((2, rows, PAIR), bf16), pltpu.VMEM((PAIR, rows), bf16)]),
        out_shape=[shape((rows, width), bf16), shape((pairs, 2, rows), f32)],
        compiler_params=params(48),
        cost_estimate=cost(16 * rows * rows * width, 4 << 20, rows * rows * 2 * pairs),
        name="attend")(length, qkv, qkv, qkv)


def attend_back_kernel(block, len_ref, q_ref, k_ref, v_ref, do_ref, total_ref, c_ref, a_ref, b_ref, grad_ref, q_mine, do_mine, k_turned, key_sum, value_sum):
    rows = q_ref.shape[1]
    zero = jnp.zeros((rows, PAIR), bf16)
    scale = 1.0 / math.sqrt(HEAD_DIM)
    for side in range(2):
        lanes = side_lanes(side)
        q_mine[side] = jnp.where(lanes, q_ref[0] * jnp.asarray(scale, bf16), zero)
        do_mine[side] = jnp.where(lanes, do_ref[...], zero)
    k_turned[...] = k_ref[0].T
    length = len_ref[0]
    tables_of = lambda r: (c_ref[r, :], a_ref[r, :], b_ref[r, :])
    for first in range(rows - block, -1, -block):
        n = first + block
        r = slice(first, n)
        gk = gv = None
        gq = []
        for side in range(2):
            scores = masked_scores(k_ref[0, :n, :], q_mine[side, r, :], first, length)
            probs = jnp.exp(scores - total_ref[0, side:side+1, r])
            grad_probs = dot(v_ref[0, :n, :], do_mine[side, r, :], NT)
            product = probs * grad_probs
            delta = jnp.sum(product, 0, keepdims=True)
            grad_scores = (product - probs * delta).astype(bf16)
            a = dot(grad_scores, q_mine[side, r, :], NN)
            b = dot(probs.astype(bf16), do_mine[side, r, :], NN)
            gk = a if gk is None else gk + a
            gv = b if gv is None else gv + b
            gq.append(dot(k_turned[side*HEAD_DIM:(side+1)*HEAD_DIM, :n], grad_scores, NN))
        if n == rows:
            key_sum[...] = gk
            value_sum[...] = gv
        else:
            key_sum[:n, :] += gk
            value_sum[:n, :] += gv
        grad_query = jnp.concatenate(gq, 0).T * scale
        grad_ref[0, r, :] = turned_back(grad_query, tables_of(r)).astype(bf16)
    for first in range(0, rows, block):
        r = slice(first, first + block)
        grad_ref[1, r, :] = turned_back(key_sum[r, :], tables_of(r)).astype(bf16)
        grad_ref[2, r, :] = value_sum[r, :].astype(bf16)


def attend_back(qkv, grad_mixed, totals, length, tables, block=512):
    _, rows, width = qkv.shape
    pairs = width // PAIR
    kind = lambda c: pl.BlockSpec((1, rows, PAIR), lambda h, n: (c, 0, h))
    table = pl.BlockSpec((rows, PAIR), lambda h, n: (0, 0))
    return pl.pallas_call(functools.partial(attend_back_kernel, min(block, rows)),
        grid_spec=pltpu.PrefetchScalarGridSpec(num_scalar_prefetch=1, grid=(pairs,),
            in_specs=[kind(0), kind(1), kind(2), pl.BlockSpec((rows, PAIR), lambda h, n: (0, h)), pl.BlockSpec((1, 2, rows), lambda h, n: (h, 0, 0)), table, table, table],
            out_specs=pl.BlockSpec((3, rows, PAIR), lambda h, n: (0, 0, h)),
            scratch_shapes=[pltpu.VMEM((2, rows, PAIR), bf16)]*2+[pltpu.VMEM((PAIR, rows), bf16)]+[pltpu.VMEM((rows, PAIR), f32)]*2),
        out_shape=shape((3, rows, width), bf16),
        compiler_params=params(48),
        cost_estimate=cost(40 * rows * rows * width, 8 << 20, rows * rows * 2 * pairs),
        name="attend_back")(length, qkv, qkv, qkv, grad_mixed, totals, *tables)


def feed_kernel(steps, late_steps, plan1, plan2, ln_ref, mixed_ref, wo_ref, bias_ref, *rest):
    n1 = len({p[0] for p in plan1})
    w1_refs, w2_refs = rest[:n1], rest[n1 : 2 * n1]
    (branch_ref, hidden_ref, slope_ref, full1_ref, full2_ref, held, buf1, buf2, sems1, sems2,
     out_sems) = rest[2 * n1 :]
    step = pl.program_id(0)
    slot = lax.rem(step, 2)
    tile_f = buf1.shape[2]
    tile_d = buf2.shape[1]
    c0 = math.sqrt(2.0 / math.pi)
    c1 = 0.044715
    plan2 = sorted(plan2, key=lambda p: p[2])
    per_tile = len(plan2) // late_steps

    def columns(s):
        return pl.ds(pl.multiple_of(s * tile_f, tile_f), tile_f)

    def start1(s):
        at = lax.rem(s, 2)
        column = pl.multiple_of(s * tile_f, tile_f)
        assemble_start(w1_refs, plan1, column, tile_f, buf1.at[at], sems1.at[at])

    def pieces2(tile):
        at = tile % 2
        for j, (which, row, place, count) in enumerate(plan2[tile * per_tile : (tile + 1) * per_tile]):
            yield pltpu.make_async_copy(
                w2_refs[which].at[pl.ds(row, count), :],
                buf2.at[at, pl.ds(place - tile * tile_d, count), :],
                sems2.at[at, j],
            )

    def out1(s, at):
        return pltpu.make_async_copy(buf1.at[at], full1_ref.at[:, columns(s)], out_sems.at[at])

    def out2(tile):
        return pltpu.make_async_copy(
            buf2.at[tile % 2], full2_ref.at[pl.ds(tile * tile_d, tile_d), :], out_sems.at[2 + tile % 2]
        )

    @pl.when(step == 0)
    def _():
        start1(0)
        for copy in pieces2(0):
            copy.start()

    @pl.when(step < steps)
    def _():
        column = pl.multiple_of(step * tile_f, tile_f)
        assemble_wait(w1_refs, plan1, column, tile_f, buf1.at[slot], sems1.at[slot])
        out1(step, slot).start()

        @pl.when(step > 0)
        def _():
            out1(step - 1, 1 - slot).wait()

        @pl.when(step < steps - 1)
        def _():
            start1(step + 1)

        pre = dot(ln_ref[...], buf1[slot], NN) + bias_ref[...]
        square = pre * pre
        bent = jnp.tanh(c0 * (pre + c1 * (square * pre)))
        half_pre = 0.5 * pre
        hidden = (half_pre * (1.0 + bent)).astype(bf16)
        hidden_ref[...] = hidden
        held[:, columns(step)] = hidden
        slope_ref[...] = 0.5 * (1.0 + bent) + half_pre * (1.0 - bent * bent) * (
            c0 * (1.0 + (3.0 * c1) * square)
        )

        @pl.when(step == steps - 1)
        def _():
            out1(step, slot).wait()

    for tile in range(late_steps):
        @pl.when(step == steps + tile)
        def _():
            for copy in pieces2(tile):
                copy.wait()
            out2(tile).start()
            if tile > 0:
                out2(tile - 1).wait()
            if tile < late_steps - 1:
                for copy in pieces2(tile + 1):
                    copy.start()
            total = dot(held[...], buf2[tile % 2], NT) + dot(mixed_ref[...], wo_ref[0], NT)
            branch_ref[...] = total.astype(bf16)
            if tile == late_steps - 1:
                out2(tile).wait()


def feed(ln, mixed, weights, w1, w2, bias, tile_f):
    rows, width = ln.shape
    hidden = bias.shape[1]
    heads = mixed.shape[1]
    steps = hidden // tile_f
    tile_d = 512
    late_steps = width // tile_d
    whole = lambda dims: pl.BlockSpec(dims, lambda i: (0, 0), pipeline_mode=once)
    early = lambda i: jnp.minimum(i, steps - 1)
    late = lambda i: jnp.maximum(i - steps, 0)
    by_row = pl.BlockSpec((rows, tile_f), lambda i: (0, early(i)))
    hbm = pl.BlockSpec(memory_space=pl.ANY)
    return pl.pallas_call(
        functools.partial(feed_kernel, steps, late_steps, w1[1], w2[1]),
        grid=(steps + late_steps,),
        in_specs=[
            whole((rows, width)),
            whole((rows, heads)),
            pl.BlockSpec((1, tile_d, heads), lambda i: (3, late(i), 0)),
            pl.BlockSpec((1, tile_f), lambda i: (0, early(i))),
        ]
        + [hbm] * (len(w1[0]) + len(w2[0])),
        out_specs=[
            pl.BlockSpec((rows, tile_d), lambda i: (0, late(i))), by_row, by_row, hbm, hbm
        ],
        out_shape=[
            shape((rows, width), bf16),
            shape((rows, hidden), bf16),
            shape((rows, hidden), f32),
            shape((width, hidden), bf16),
            shape((width, hidden), bf16),
        ],
        scratch_shapes=[
            pltpu.VMEM((rows, hidden), bf16),
            pltpu.VMEM((2, width, tile_f), bf16),
            pltpu.VMEM((2, tile_d, hidden), bf16),
            pltpu.SemaphoreType.DMA((2, len(w1[1]))),
            pltpu.SemaphoreType.DMA((2, len(w2[1]) // late_steps)),
            pltpu.SemaphoreType.DMA((4,)),
        ],
        compiler_params=params(58),
        cost_estimate=cost(4 * rows * width * hidden, 56 << 20, rows * hidden),
        name="feed",
    )(ln, mixed, weights, bias, *w1[0], *w2[0])


def back_kernel(steps, g_ref, w1_ref, w2_ref, slope_ref, wo_ref, sum_ref, pre_ref, mixed_ref, bias_ref, held):
    step = pl.program_id(0)
    tile = pre_ref.shape[1]

    @pl.when(step == 0)
    def _():
        mixed_ref[...] = dot(g_ref[...], wo_ref[0], NN).astype(bf16)

    @pl.when(step < steps)
    def _():
        grad = (dot(g_ref[...], w2_ref[...], NN) * slope_ref[...]).astype(bf16)
        pre_ref[...] = grad
        held[:, pl.ds(pl.multiple_of(step * tile, tile), tile)] = grad
        bias_ref[...] = jnp.sum(grad.astype(f32), axis=0, keepdims=True)

    @pl.when(step >= steps)
    def _():
        sum_ref[...] = dot(held[...], w1_ref[...], NT)


def back(grads, w1, w2, slope, weights, tile_f):
    rows, width = grads.shape
    units = slope.shape[1]
    heads = weights.shape[2]
    steps = units // tile_f
    tile_d = 512
    whole = lambda dims: pl.BlockSpec(dims, lambda i: (0, 0), pipeline_mode=once)
    early = lambda i: jnp.minimum(i, steps - 1)
    late = lambda i: jnp.maximum(i - steps, 0)
    by_row = pl.BlockSpec((rows, tile_f), lambda i: (0, early(i)))
    return pl.pallas_call(
        functools.partial(back_kernel, steps),
        grid=(steps + width // tile_d,),
        in_specs=[
            whole((rows, width)),
            pl.BlockSpec((tile_d, units), lambda i: (late(i), 0)),
            pl.BlockSpec((width, tile_f), lambda i: (0, early(i))),
            by_row,
            pl.BlockSpec((1, width, heads), lambda i: (3, 0, 0), pipeline_mode=once),
        ],
        out_specs=[
            pl.BlockSpec((rows, tile_d), lambda i: (0, late(i))),
            by_row,
            whole((rows, heads)),
            pl.BlockSpec((1, tile_f), lambda i: (0, early(i))),
        ],
        out_shape=[
            shape((rows, width), f32),
            shape((rows, units), bf16),
            shape((rows, heads), bf16),
            shape((1, units), f32),
        ],
        scratch_shapes=[pltpu.VMEM((rows, units), bf16)],
        compiler_params=params(58),
        cost_estimate=cost(4 * rows * width * units, 40 << 20),
        name="back",
    )(grads, w1, w2, slope, weights)


def feed_weight_kernel(left_ref, right_ref, near_ref, far_ref):
    half = left_ref.shape[1] // 2
    far_ref[...] = dot(left_ref[:, half:], right_ref[...], TN).astype(bf16)
    near_ref[...] = dot(left_ref[:, :half], right_ref[...], TN).astype(bf16)


def feed_weight(left, right, tile_f):
    rows, width = left.shape
    units = right.shape[1]
    half = pl.BlockSpec((width // 2, tile_f), lambda i: (0, i))
    return pl.pallas_call(
        feed_weight_kernel,
        grid=(units // tile_f,),
        in_specs=[
            pl.BlockSpec((rows, width), lambda i: (0, 0), pipeline_mode=once),
            pl.BlockSpec((rows, tile_f), lambda i: (0, i)),
        ],
        out_specs=[half, half],
        out_shape=[shape((width // 2, units), bf16)] * 2,
        compiler_params=params(48),
        cost_estimate=cost(2 * rows * width * units, 16 << 20),
        name="feed_weight",
    )(left, right)


def ln_grad_kernel(grad_ref, w_ref, sum_ref, out_ref):
    total = sum_ref[...]
    for kind in range(3):
        total += dot(grad_ref[kind], w_ref[kind], NT)
    out_ref[...] = total.astype(bf16)


def ln_grad(grad_qkv, weights, partial_sum):
    _, rows, heads = grad_qkv.shape
    width = partial_sum.shape[1]
    tile = 512
    return pl.pallas_call(
        ln_grad_kernel,
        grid=(width // tile,),
        in_specs=[
            pl.BlockSpec((3, rows, heads), lambda i: (0, 0, 0), pipeline_mode=once),
            pl.BlockSpec((3, tile, heads), lambda i: (0, i, 0)),
            pl.BlockSpec((rows, tile), lambda i: (0, i)),
        ],
        out_specs=pl.BlockSpec((rows, tile), lambda i: (0, i)),
        out_shape=shape((rows, width), bf16),
        compiler_params=params(48),
        cost_estimate=cost(6 * rows * width * heads, 22 << 20),
        name="ln_grad",
    )(grad_qkv, weights, partial_sum)


def weight_grad_kernel(ln_ref, g_ref, grad_ref, mixed_ref, kqk_ref, kvo_ref, sqk_ref, svo_ref, bias_ref):
    heads = mixed_ref.shape[1]
    step = pl.program_id(0)
    steps = pl.num_programs(0)
    for kind in range(3):
        @pl.when(step == 0)
        def _():
            bias_ref[kind] = jnp.sum(grad_ref[kind].astype(f32), axis=0, keepdims=True)

    for qk_ref, vo_ref, here in ((kqk_ref, kvo_ref, step < steps // 2), (sqk_ref, svo_ref, step >= steps // 2)):
        @pl.when(here)
        def _():
            qk_ref[:, :heads] = dot(ln_ref[...], grad_ref[0], TN).astype(bf16)
            qk_ref[:, heads:] = dot(ln_ref[...], grad_ref[1], TN).astype(bf16)
            vo_ref[:, :heads] = dot(ln_ref[...], grad_ref[2], TN).astype(bf16)
            vo_ref[:, heads:] = dot(g_ref[...], mixed_ref[...], TN).astype(bf16)


def weight_grad(ln, grads, grad_qkv, mixed):
    rows, width = ln.shape
    heads = mixed.shape[1]
    half = width // 2
    tile = min(512, half)
    near = half // tile
    column = pl.BlockSpec((rows, tile), lambda i: (0, i))
    kept = pl.BlockSpec((tile, 2 * heads), lambda i: (jnp.minimum(i, near - 1), 0))
    sent = pl.BlockSpec((tile, 2 * heads), lambda i: (jnp.maximum(i - near, 0), 0))
    return pl.pallas_call(
        weight_grad_kernel,
        grid=(2 * near,),
        in_specs=[
            column,
            column,
            pl.BlockSpec((3, rows, heads), lambda i: (0, 0, 0), pipeline_mode=once),
            pl.BlockSpec((rows, heads), lambda i: (0, 0), pipeline_mode=once),
        ],
        out_specs=[kept, kept, sent, sent, pl.BlockSpec((3, 1, heads), lambda i: (0, 0, 0))],
        out_shape=[shape((half, 2 * heads), bf16)] * 4 + [shape((3, 1, heads), f32)],
        compiler_params=params(48),
        cost_estimate=cost(8 * rows * width * heads, 20 << 20),
        name="weight_grad",
    )(ln, grads, grad_qkv, mixed)


def give_kernel(counts, *refs):
    outs = refs[sum(counts) :]
    start = 0
    for number, out_ref in zip(counts, outs):
        total = refs[start][...].astype(f32)
        for ref in refs[start + 1 : start + number]:
            total += ref[...].astype(f32)
        out_ref[...] = total.astype(bf16)
        start += number


def give(items, count):
    specs, operands, numbers, outs = [], [], [], []
    for full, arrivals, low, part in items:
        rows, width = full[0].shape[0], full[0].shape[1] // part[1]
        block = rows // count
        level = len(arrivals) + 1
        out_count = count >> level
        place = (lambda i: (2 * i + 1) << (level - 1)) if low else (lambda i: out_count + i)
        for k in range(level):
            for array in full if k == 0 else [arrivals[k - 1]]:
                off = part[0] if k == 0 else 0
                specs.append(
                    pl.BlockSpec(
                        (block, width),
                        lambda i, k=k, off=off, low=low, place=place: (
                            place(i) >> k if low else place(i),
                            off,
                        ),
                    )
                )
                operands.append(array)
        numbers.append(len(full) + level - 1)
        outs.append(shape((out_count * block, width), bf16))
    moved = sum(o.shape[0] * o.shape[1] for o in outs)
    return pl.pallas_call(
        functools.partial(give_kernel, tuple(numbers)),
        grid=(out_count,),
        in_specs=specs,
        out_specs=[pl.BlockSpec((block, o.shape[1]), lambda i: (i, 0)) for o in outs],
        out_shape=outs,
        compiler_params=params(32),
        cost_estimate=cost(moved * 2, 6 * moved),
        name="give",
    )(*operands)


def norm_back_kernel(
    blocks, at_ref, sum_ref, rows_ref, cot_ref, gain_ref, first_ref, second_ref, vector_ref, held
):
    wide = rows_ref.shape[1] // blocks
    bits = blocks.bit_length() - 1
    for q in range(blocks):
        place = pl.multiple_of(reversed_bits(at_ref[1] ^ q, bits) * wide, wide)
        held[:, q * wide : (q + 1) * wide] = sum_ref[:, pl.ds(place, wide)]
    grad_ln = held[...].astype(f32)
    rows = rows_ref[...].astype(f32)
    centred = rows - jnp.mean(rows, -1, keepdims=True)
    inv_scale = lax.rsqrt(jnp.mean(centred * centred, -1, keepdims=True) + eps)
    normed = centred * inv_scale
    grad_norm = grad_ln * gain_ref[...]
    back = inv_scale * (
        grad_norm
        - jnp.mean(grad_norm, -1, keepdims=True)
        - normed * jnp.mean(grad_norm * normed, -1, keepdims=True)
    )
    slot = (cot_ref[...].astype(f32) + back).astype(bf16)
    half = first_ref.shape[0]
    first_ref[...] = slot[:half]
    second_ref[...] = slot[half:]
    vector_ref[0:1] = jnp.sum(grad_ln * normed, 0, keepdims=True)
    vector_ref[1:2] = jnp.sum(grad_ln, 0, keepdims=True)


def norm_back(total, rows_in, cot, gain, at, blocks):
    rows, width = rows_in.shape
    whole = pl.BlockSpec((rows, width), lambda i, n: (0, 0))
    vector = pl.BlockSpec((1, width), lambda i, n: (0, 0))
    return pl.pallas_call(
        functools.partial(norm_back_kernel, blocks),
        grid_spec=pltpu.PrefetchScalarGridSpec(
            num_scalar_prefetch=1,
            grid=(1,),
            in_specs=[whole, whole, whole, vector],
            out_specs=[pl.BlockSpec((rows // 2, width), lambda i, n: (0, 0))] * 2
            + [pl.BlockSpec((2, width), lambda i, n: (0, 0))],
            scratch_shapes=[pltpu.VMEM((rows, width), bf16)],
        ),
        out_shape=[shape((rows // 2, width), bf16)] * 2 + [shape((2, width), f32)],
        compiler_params=params(32),
        cost_estimate=cost(20 * rows * width, 8 * rows * width),
        name="norm_back",
    )(at, total, rows_in, cot, gain)


def final_kernel(parts, levels, *refs):
    full, rest, out_ref = refs[:2], refs[2:-1], refs[-1]
    base = full[0][...].astype(f32) + full[1][...].astype(f32)
    for part in range(parts):
        @pl.when(pl.program_id(0) == part)
        def _():
            total = base
            for ref in rest[part * levels : (part + 1) * levels]:
                total += ref[...].astype(f32)
            out_ref[...] = total


def final(full, sums, block):
    parts, levels = len(sums), len(sums[0])
    width = full[0].shape[1]
    wide = width // parts
    piece = pl.BlockSpec((block, wide), lambda i: (0, i))
    held = pl.BlockSpec((block, wide), lambda i: (0, 0))
    return pl.pallas_call(
        functools.partial(final_kernel, parts, levels),
        grid=(parts,),
        in_specs=[piece, piece] + [held] * (parts * levels),
        out_specs=piece,
        out_shape=shape((block, width), f32),
        compiler_params=params(32),
        cost_estimate=cost(4 * block * width, 12 * block * width),
        name="final",
    )(*full, *[f for s in sums for f in s])


def finish_kernel(blocks, at_ref, sum_ref, rows_ref, bias_a_ref, bias_b_ref, out_ref, held):
    rows, width = rows_ref.shape
    wide = width // blocks
    bits = blocks.bit_length() - 1
    for q in range(blocks):
        place = pl.multiple_of(reversed_bits(at_ref[1] ^ q, bits) * wide, wide)
        held[:, q * wide : (q + 1) * wide] = sum_ref[:, pl.ds(place, wide)]
    branch = held[...].astype(f32) + bias_a_ref[...] + bias_b_ref[...]
    position = at_ref[0] * rows + lax.broadcasted_iota(jnp.int32, (rows, 1), 0)
    branch = jnp.where(position < at_ref[2], branch, 0.0)
    out_ref[...] = (rows_ref[...].astype(f32) + branch).astype(bf16)


def finish(branch_sum, rows_in, bias_a, bias_b, at, blocks):
    rows, width = rows_in.shape
    whole = pl.BlockSpec((rows, width), lambda i, n: (0, 0))
    vector = pl.BlockSpec((1, width), lambda i, n: (0, 0))
    return pl.pallas_call(
        functools.partial(finish_kernel, blocks),
        grid_spec=pltpu.PrefetchScalarGridSpec(
            num_scalar_prefetch=1,
            grid=(1,),
            in_specs=[whole, whole, vector, vector],
            out_specs=whole,
            scratch_shapes=[pltpu.VMEM((rows, width), bf16)],
        ),
        out_shape=shape((rows, width), bf16),
        compiler_params=params(32),
        cost_estimate=cost(8 * rows * width, 6 * rows * width),
        name="finish",
    )(at, branch_sum, rows_in, bias_a, bias_b)


def final_attention_kernel(levels, *refs):
    heads = refs[0].shape[1] // 2
    grad_ref, out_ref = refs[-2:]
    totals = []
    for start in (0, levels + 2):
        total = refs[start][...].astype(f32)
        for ref in refs[start + 1 : start + levels + 2]:
            total += ref[...].astype(f32)
        totals.append(total)
    grad_ref[0] = totals[0][:, :heads]
    grad_ref[1] = totals[0][:, heads:]
    grad_ref[2] = totals[1][:, :heads]
    out_ref[...] = totals[1][:, heads:]


def final_attention(qk, vo, block):
    levels = len(qk) - 2
    width = qk[0].shape[1]
    piece = pl.BlockSpec((block, width), lambda i: (0, 0))
    return pl.pallas_call(
        functools.partial(final_attention_kernel, levels),
        grid=(1,),
        in_specs=[piece] * (2 * levels + 4),
        out_specs=[
            pl.BlockSpec((3, block, width // 2), lambda i: (0, 0, 0)),
            pl.BlockSpec((block, width // 2), lambda i: (0, 0)),
        ],
        out_shape=[shape((3, block, width // 2), f32), shape((block, width // 2), f32)],
        compiler_params=params(32),
        cost_estimate=cost(8 * block * width, 24 * block * width),
        name="final_attention",
    )(*qk, *vo)


def rotary_tables(rows, col_count):
    half_rot = ROT // 2
    column = jnp.arange(col_count) % HEAD_DIM
    exponent = (2 * (column % half_rot)).astype(jnp.float32) / ROT
    frequency = jnp.exp(-math.log(10000.0) * exponent)
    angles = rows.astype(jnp.float32)[:, None] * frequency[None, :]
    inside = column < ROT
    cosine = jnp.where(inside, jnp.cos(angles), 1.0)
    sine_part = jnp.sin(angles)
    ahead_sin = jnp.where(column < half_rot, -sine_part, 0.0)
    behind_sin = jnp.where(inside & (column >= half_rot), sine_part, 0.0)
    return (cosine, ahead_sin, behind_sin)


def flip(array, axis_name, bit):
    size = lax.axis_size(axis_name)
    return lax.ppermute(array, axis_name, [(i, i ^ (1 << bit)) for i in range(size)])


def bits_of(size):
    return size.bit_length() - 1


def swap_blocks(array, index, axis, blocks):
    for bit in range(bits_of(blocks)):
        dims = array.shape
        parts = dims[:axis] + (blocks >> (bit + 1), 2, 1 << bit, dims[axis] // blocks)
        view = array.reshape(parts + dims[axis + 1 :])
        other = jnp.flip(view, axis=axis + 1)
        array = jnp.where((index >> bit) & 1 == 1, other, view).reshape(dims)
    return array


def reversed_bits(value, bits):
    return sum(((value >> k) & 1) << (bits - 1 - k) for k in range(bits))


def xor_columns(array, index, blocks):
    width = array.shape[-1] // blocks
    bits = bits_of(blocks)
    pieces = [
        lax.dynamic_slice_in_dim(
            array, (index ^ reversed_bits(p, bits)) * width, width, array.ndim - 1
        )
        for p in range(blocks)
    ]
    return jnp.concatenate(pieces, -1)


def plain_columns(array, index, blocks):
    width = array.shape[-1] // blocks
    bits = bits_of(blocks)
    pieces = []
    for q in range(blocks):
        place = reversed_bits(index ^ q, bits)
        pieces.append(lax.dynamic_slice_in_dim(array, place * width, width, array.ndim - 1))
    return jnp.concatenate(pieces, -1)


def gather_step(stacks, bit):
    return stacks + [(flip(rows, "dp", bit), [m | (1 << bit) for m in masks]) for rows, masks in stacks]


def joined_step(stacks, bit):
    rows = jnp.concatenate([s[0] for s in stacks], 0)
    return stacks + [(flip(rows, "dp", bit), [m | (1 << bit) for s in stacks for m in s[1]])]


def gather_plan(stacks, block, bits):
    plan = []
    for which, (_, masks) in enumerate(stacks):
        for i, m in enumerate(masks):
            plan.append((which, i * block, reversed_bits(m, bits) * block, block))
    return [s[0] for s in stacks], tuple(plan)


def core_copies(stacks):
    return [(flip(rows, "dp", 0), [m | 1 for m in masks]) for rows, masks in stacks]


def route_order(last):
    return [b for b in range(bits_of(lax.axis_size("dp")) - 1, -1, -1) if b != last]


def route_first(block, last):
    return jnp.stack([block, flip(block, "dp", route_order(last)[0])], 0)


def route_more(stack, last):
    order = route_order(last)[1:]
    for bit in order[:-1]:
        stack = jnp.concatenate([stack, flip(stack, "dp", bit)], 0)
    return (stack, flip(stack, "dp", order[-1]))


def route_picks(halves, wanted, index, last):
    order = route_order(last)
    count = halves[0].shape[0]

    def pick(want):
        mask = index ^ want
        at = sum(((mask >> bit) & 1) << k for k, bit in enumerate(order))
        found = [lax.dynamic_index_in_dim(h, at % count, 0, keepdims=False) for h in halves]
        return found[0] if len(found) == 1 else jnp.where(at < count, found[0], found[1])

    return pick(wanted[index ^ (1 << last)]), pick(wanted[index])


def route_end(given, held, wanted, index, last):
    arrived = flip(given, "dp", last)
    return jnp.where(((index ^ wanted[index]) >> last) & 1 == 1, arrived, held)


def gather_small(stack, axis_name):
    for bit in range(bits_of(lax.axis_size(axis_name))):
        stack = jnp.concatenate([stack, flip(stack, axis_name, bit)], 0)
    return stack


def scatter_along(stack, axis_name):
    bits = bits_of(lax.axis_size(axis_name))
    stack = stack.reshape((2,) * bits + stack.shape[1:])
    stack = stack.transpose(tuple(range(bits - 1, -1, -1)) + tuple(range(bits, stack.ndim)))
    for bit in range(bits):
        stack = stack[0] + flip(stack[1], axis_name, bit)
    return stack


def after(values, *others):
    held = lax.optimization_barrier((tuple(values), tuple(others)))
    return held[0]


def shards(
    hidden_in,
    cotangent,
    lengths,
    slot_of_seq,
    seq_of_slot,
    qkv_weight,
    out_weight,
    fc1_weight,
    fc2_weight,
    ln_gain,
    ln_bias,
    qkv_bias,
    out_bias,
    fc1_bias,
    fc2_bias,
):
    rows_here = hidden_in.shape[1]
    width = hidden_in.shape[2]
    tensor_count = lax.axis_size("tensor")
    data_count = lax.axis_size("dp")
    tensor_index = lax.axis_index("tensor")
    data_index = lax.axis_index("dp")
    seq_len = rows_here * tensor_count
    heads_local = qkv_weight.shape[2]
    hidden_local = fc1_weight.shape[1]
    block = width // data_count
    length = lengths[seq_of_slot[data_index]]
    bits = bits_of(data_count)
    x_first = list(range(1, bits))
    y_first = x_first[::-1]
    tile_f = min(512, hidden_local)

    lasts = (bits - 1, bits - 2)
    wave_rows = rows_here // 2
    at = jnp.stack([tensor_index, data_index, length]).astype(jnp.int32)

    def send(parts):
        return [route_first(h, last) for h, last in zip(parts, lasts)]

    def picks_of(stacks, wanted):
        return [route_picks(f, wanted, data_index, last) for f, last in zip(stacks, lasts)]

    def route_ends(picks, wanted):
        return jnp.concatenate(
            [route_end(g, k, wanted, data_index, last) for (g, k), last in zip(picks, lasts)], 0
        )

    def receive(firsts, wanted):
        stacks = [route_more(f, last) for f, last in zip(firsts, lasts)]
        stacks = [(jnp.concatenate(halves, 0),) for halves in stacks]
        return route_ends(picks_of(stacks, wanted), wanted)

    firsts = send((hidden_in[0, :wave_rows], hidden_in[0, wave_rows:]))
    vectors = [ln_gain, ln_bias, out_bias, fc2_bias, qkv_bias, fc1_bias]
    s = ln_gain.shape[0]
    vectors = after(vectors, *firsts)
    small = jnp.concatenate([v.reshape(-1, s) for v in vectors], 0)
    stack = gather_small(small[None], "tensor")
    routed = receive(firsts, seq_of_slot)
    routed, stack = after((routed, stack))
    extra_rows = 16
    full = lax.all_gather(routed, "tensor", axis=0, tiled=True)

    stack = swap_blocks(stack, tensor_index, 0, tensor_count).reshape(-1)
    extra = jnp.pad(stack, (0, extra_rows * 2 * heads_local - stack.shape[0]))
    qk_shard = jnp.concatenate(
        [qkv_weight[:, :2].reshape(block, 2 * heads_local), extra.reshape(extra_rows, 2 * heads_local)], 0
    )
    vo_shard = jnp.concatenate([qkv_weight[:, 2], out_weight], 1)
    qk_shard, vo_shard = after((qk_shard, vo_shard), routed)
    qk_stacks = gather_step([(qk_shard, [0])], x_first[0])
    vo_stacks = gather_step([(vo_shard, [0])], y_first[0])
    first_qk, first_vo, fc1_shard, fc2_shard = after(
        (qk_stacks[1][0], vo_stacks[1][0], fc1_weight, fc2_weight)
    )
    qk_stacks[1], vo_stacks[1] = (first_qk, qk_stacks[1][1]), (first_vo, vo_stacks[1][1])
    for step in range(1, len(x_first)):
        qk_stacks = gather_step(qk_stacks, x_first[step])
        vo_stacks = gather_step(vo_stacks, y_first[step])

    def held_back(groups, *values):
        flat = [rows for stacks in groups for rows, _ in stacks]
        out = list(after(tuple(flat) + values))
        fresh = [[(out.pop(0), masks) for _, masks in stacks] for stacks in groups]
        return fresh, out

    row_ids, = after((jnp.arange(seq_len, dtype=jnp.int32),), qk_shard)
    tables = rotary_tables(row_ids, PAIR)
    (qk_stacks, vo_stacks), tables = held_back((qk_stacks, vo_stacks), *tables)
    qk_stacks = qk_stacks + core_copies(qk_stacks)
    qk = gather_plan(qk_stacks, block, bits)
    by_mask = sorted(qk_stacks, key=lambda st: st[1][0])
    gathered = jnp.stack([rows[block:].reshape(-1)[: stack.shape[0]] for rows, _ in by_mask], 0)
    gathered = swap_blocks(gathered, data_index, 0, data_count)
    gathered = gathered.reshape(data_count, tensor_count, -1)
    vo = gather_plan(vo_stacks + core_copies(vo_stacks), block, bits)
    fc1_stacks = gather_step([(fc1_shard, [0])], x_first[0])
    fc2_stacks = gather_step([(fc2_shard, [0])], y_first[0])

    positions = tensor_index * rows_here + jnp.arange(rows_here, dtype=jnp.int32)
    valid = (positions < length)[:, None]
    cot_rows = cotangent[0]
    low_plain = jnp.where(valid, cot_rows, jnp.zeros_like(cot_rows))
    low, = after((low_plain,), routed)
    low = xor_columns(low, data_index, data_count)
    grads = lax.all_gather(low, "tensor", axis=0, tiled=True)

    gain, shift, bias_a, bias_b = [
        gathered[:, :, i * s : (i + 1) * s].reshape(1, width).astype(f32) for i in range(4)
    ]
    q = qkv_bias.shape[0]
    bias_qkv = lax.dynamic_slice_in_dim(
        gathered[:, :, 4 * s : 4 * s + q].reshape(3, width), tensor_index * heads_local, heads_local, 1
    ).astype(f32)
    bias_fc1 = lax.dynamic_slice_in_dim(
        gathered[:, :, 4 * s + q :].reshape(1, hidden_local * tensor_count),
        tensor_index * hidden_local,
        hidden_local,
        1,
    ).astype(f32)

    row_tables = [v.reshape(tensor_count, 1, rows_here, PAIR) for v in tables]
    size = length.reshape(1)
    (fc1_stacks, fc2_stacks), (gain, shift) = held_back((fc1_stacks, fc2_stacks), gain, shift)
    fc1_far, fc2_far = core_copies(fc1_stacks), core_copies(fc2_stacks)
    for step in range(1, len(x_first)):
        fc1_stacks = joined_step(fc1_stacks, x_first[step])
        fc2_stacks = joined_step(fc2_stacks, y_first[step])
    ln = norm(full, tensor_count, at, gain, shift, data_count)
    (fc1_far, fc2_far), (ln,) = held_back((fc1_far, fc2_far), ln)
    qkv, weights = project(ln, qk, vo, bias_qkv, row_tables)
    ln, qkv = ln.reshape(seq_len, width), qkv.reshape(3, seq_len, heads_local)
    mixed, totals = attend(qkv, size)
    (fc1_stacks, fc2_stacks), (mixed,) = held_back((fc1_stacks, fc2_stacks), mixed)
    fc1_far = fc1_far + core_copies(fc1_stacks[2:])
    fc2_far = fc2_far + core_copies(fc2_stacks[2:])
    w1 = gather_plan(fc1_stacks + fc1_far, block, bits)
    w2 = gather_plan(fc2_stacks + fc2_far, block, bits)
    branch, hidden, slope, full1, full2 = feed(ln, mixed, weights, w1, w2, bias_fc1, tile_f)
    branch, grads = after((branch, grads))
    branch = lax.psum_scatter(branch, "tensor", scatter_dimension=0, tiled=True)

    count = data_count // 2
    steps = len(x_first)
    feed_sum, grad_pre, grad_mixed, grad_fc1_b = back(grads, full1, full2, slope, weights, tile_f)
    hidden, = after((hidden,), grad_pre)
    k2, s2 = feed_weight(grads, hidden, tile_f)
    c2 = flip(s2, "dp", 0)
    grad_pre, = after((grad_pre,), s2)
    k1, s1 = feed_weight(ln, grad_pre, tile_f)
    c1 = flip(s1, "dp", 0)

    pair = ((0, 2), (1, 2))
    both = (x_first, y_first)

    def gives_of(full, sums):
        return give([(full, s, low, p) for s, low, p in zip(sums, (False, True), pair)], count)

    def send_on(gives, step):
        return [flip(g, "dp", order[step]) for g, order in zip(gives, both)]

    k2, c2 = after((k2, c2), s1)
    gives2 = gives_of([k2, c2], ([], []))
    sums2 = [[f] for f in send_on(gives2, 0)]
    k1, c1 = after((k1, c1), *gives2)
    gives1 = gives_of([k1, c1], ([], []))
    sums1 = [[f] for f in send_on(gives1, 0)]
    grad_mixed, = after((grad_mixed,), *gives1)
    grad_qkv = attend_back(qkv, grad_mixed, totals, size, tables)
    kqk, kvo, sqk, svo, grad_qkv_b = weight_grad(ln, grads, grad_qkv, mixed)
    cq, cv = flip(sqk, "dp", 0), flip(svo, "dp", 0)
    grad_qkv, branch, sums2, sums1 = after((grad_qkv, branch, sums2, sums1), sqk)
    ln_part = ln_grad(grad_qkv, weights, feed_sum)
    total = lax.psum_scatter(ln_part, "tensor", scatter_dimension=0, tiled=True)
    kqk, kvo, cq, cv = after((kqk, kvo, cq, cv), ln_part)
    giveq, givev = give(
        [([kqk, cq], [], False, (0, 1)), ([kvo, cv], [], True, (0, 1))], count
    )
    sumsq, sumsv = [flip(giveq, "dp", x_first[0])], [flip(givev, "dp", y_first[0])]
    k2, = after((k2,), giveq, givev)
    for step in range(1, steps):
        gives2 = gives_of([k2, c2], sums2)
        sums2 = [s + [f] for s, f in zip(sums2, send_on(gives2, step))]
    k1, = after((k1,), *gives2)
    for step in range(1, steps):
        gives1 = gives_of([k1, c1], sums1)
        sums1 = [s + [f] for s, f in zip(sums1, send_on(gives1, step))]
    branch, = after((branch,), *gives1)
    block_out = finish(branch, routed, bias_a, bias_b, at, data_count)[None]
    grad_bias = jnp.sum(low_plain.astype(f32), axis=0)
    devices = data_count * tensor_count
    full_qkv_b = lax.dynamic_update_slice_in_dim(
        jnp.zeros((3, width), f32), grad_qkv_b[:, 0], tensor_index * heads_local, 1
    )
    full_fc1_b = lax.dynamic_update_slice_in_dim(
        jnp.zeros((hidden_local * tensor_count,), f32), grad_fc1_b[0], tensor_index * hidden_local, 0
    )
    known = jnp.concatenate(
        [grad_bias.reshape(devices, s), full_qkv_b.reshape(devices, q), full_fc1_b.reshape(devices, -1)],
        1,
    )
    kqk, kvo, sumsq, sumsv = after((kqk, kvo, sumsq, sumsv), block_out)
    for step in range(1, steps):
        giveq, givev = give(
            [([kqk, cq], sumsq, False, (0, 1)), ([kvo, cv], sumsv, True, (0, 1))], count
        )
        sumsq = sumsq + [flip(giveq, "dp", x_first[step])]
        sumsv = sumsv + [flip(givev, "dp", y_first[step])]
    k2, k1, sums2, sums1 = after((k2, k1, sums2, sums1), giveq, givev)
    grad_fc2_w, grad_fc1_w = final([k2, c2], sums2, block), final([k1, c1], sums1, block)
    sumsq, sumsv = after((sumsq, sumsv), grad_fc2_w, grad_fc1_w)
    grad_qkv_w, grad_out_w = final_attention([kqk, cq] + sumsq, [kvo, cv] + sumsv, block)
    grad_qkv_w = grad_qkv_w.swapaxes(0, 1)
    total, known = after((total, known), grad_out_w)
    *slot, vector_sums = norm_back(total, routed, cotangent[0], gain, at, data_count)
    firsts = send(slot)
    vector_sums = vector_sums.reshape(2, devices, s)
    sums = jnp.concatenate([vector_sums[0], vector_sums[1], known], 1)
    sums = swap_blocks(sums, data_index * tensor_count + tensor_index, 0, devices)
    sums = sums.reshape(data_count, tensor_count, -1).swapaxes(0, 1)
    sums = scatter_along(sums, "tensor")
    firsts, sums = after((firsts, sums))
    stacks = [route_more(f, last) for f, last in zip(firsts, lasts)]
    picks = picks_of(stacks, slot_of_seq)
    picks, sums = after((picks, sums))
    grad_input = route_ends(picks, slot_of_seq)[None]
    total = scatter_along(sums, "dp")
    return (
        block_out,
        grad_input,
        grad_qkv_w,
        grad_out_w,
        grad_fc1_w,
        grad_fc2_w,
        total[:s],
        total[s : 2 * s],
        total[3 * s : 3 * s + q],
        total[2 * s : 3 * s],
        total[3 * s + q :],
        total[2 * s : 3 * s],
    )


def solution(mesh):
    in_specs = (
        P("dp", "tensor", None),
        P("dp", "tensor", None),
        P(),
        P(),
        P(),
        P("dp", None, "tensor"),
        P("dp", "tensor"),
        P("dp", "tensor"),
        P("dp", "tensor"),
        P(("dp", "tensor")),
        P(("dp", "tensor")),
        P(("dp", "tensor")),
        P(("dp", "tensor")),
        P(("dp", "tensor")),
        P(("dp", "tensor")),
    )
    out_specs = (
        P("dp", "tensor", None),
        P("dp", "tensor", None),
        P("dp", None, "tensor"),
        P("dp", "tensor"),
        P("dp", "tensor"),
        P("dp", "tensor"),
        P(("dp", "tensor")),
        P(("dp", "tensor")),
        P(("dp", "tensor")),
        P(("dp", "tensor")),
        P(("dp", "tensor")),
        P(("dp", "tensor")),
    )
    return jax.shard_map(shards, mesh=mesh, in_specs=in_specs, out_specs=out_specs, check_vma=False)
```

```python
import functools
import math

import jax
import jax.numpy as jnp
from jax import lax
from jax.experimental import pallas as pl
from jax.experimental.pallas import tpu as pltpu
from jax.sharding import PartitionSpec as P

HEAD_DIM = 64
ROT = 32
PAIR = 2 * HEAD_DIM
VMEM = 63 * 1024 * 1024
SHARE = 0.4


eps = 1e-05
masked_score = -1e30
f32 = jnp.float32
bf16 = jnp.bfloat16
NN = (((1,), (0,)), ((), ()))
NT = (((1,), (1,)), ((), ()))
TN = (((0,), (0,)), ((), ()))
once = pl.Buffered(1)


def dot(a, b, dims):
    return lax.dot_general(a, b, dims, preferred_element_type=f32)


def params(mib):
    return pltpu.CompilerParams(vmem_limit_bytes=VMEM)


def cost(flops, nbytes, exps=0):
    return pl.CostEstimate(
        flops=int(flops * SHARE), bytes_accessed=int(nbytes * SHARE), transcendentals=int(exps * SHARE)
    )


def shape(dims, dtype):
    return jax.ShapeDtypeStruct(dims, dtype)


def turned(field, tables):
    cosine, ahead, behind = tables
    half = ROT // 2
    wide = field.shape[1]
    return (
        field * cosine
        + pltpu.roll(field, wide - half, 1) * ahead
        + pltpu.roll(field, half, 1) * behind
    )


def turned_back(grad, tables):
    cosine, ahead, behind = tables
    half = ROT // 2
    wide = grad.shape[1]
    return (
        grad * cosine
        + pltpu.roll(grad * ahead, half, 1)
        + pltpu.roll(grad * behind, wide - half, 1)
    )


def norm_kernel(blocks, at_ref, x_ref, gain_ref, shift_ref, *rest):
    out_ref, plain = rest[-2:]
    rows = x_ref[...].astype(f32)
    centred = rows - jnp.mean(rows, -1, keepdims=True)
    scale = lax.rsqrt(jnp.mean(centred * centred, -1, keepdims=True) + eps)
    plain[...] = (centred * scale * gain_ref[...] + shift_ref[...]).astype(bf16)
    wide = plain.shape[1] // blocks
    bits = blocks.bit_length() - 1
    for p in range(blocks):
        place = (at_ref[1] ^ reversed_bits(p, bits)) * wide
        out_ref[0, 0, :, p * wide : (p + 1) * wide] = plain[:, pl.ds(pl.multiple_of(place, wide), wide)]


def norm(rows_in, count, at, gain, shift, blocks):
    rows, width = rows_in.shape[0] // count, rows_in.shape[1]
    vector = pl.BlockSpec((1, width), lambda j, n: (0, 0))
    return pl.pallas_call(
        functools.partial(norm_kernel, blocks),
        grid_spec=pltpu.PrefetchScalarGridSpec(
            num_scalar_prefetch=1,
            grid=(2 * count,),
            in_specs=[pl.BlockSpec((rows // 2, width), lambda j, n: (j, 0)), vector, vector],
            out_specs=pl.BlockSpec((1, 1, rows // 2, width), lambda j, n: (j // 2, 0, j % 2, 0)),
            scratch_shapes=[pltpu.VMEM((rows // 2, width), bf16)],
        ),
        out_shape=shape((count, 1, rows, width), bf16),
        compiler_params=params(32),
        cost_estimate=cost(10 * count * rows * width, 4 * count * rows * width),
        name="norm",
    )(at, rows_in, gain, shift)


def project_rows(kind, ln_ref, weight, bias_ref, tables, out_ref):
    rows = ln_ref.shape[0] * ln_ref.shape[2]
    many, size = ln_ref.shape[0], ln_ref.shape[2]
    raw = dot(ln_ref[...].reshape(rows, ln_ref.shape[3]), weight, NN) + bias_ref[0]

    @pl.when(kind < 2)
    def _():
        here = [t[...].reshape(rows, PAIR) for t in tables]
        for pair in range(raw.shape[1] // PAIR):
            cols = slice(pair * PAIR, (pair + 1) * PAIR)
            out_ref[0, :, 0, :, cols] = (
                turned(raw[:, cols], here).astype(bf16).reshape(many, size, PAIR)
            )

    @pl.when(kind == 2)
    def _():
        out_ref[0, :, 0] = raw.astype(bf16).reshape(many, size, raw.shape[1])


def assemble_start(refs, plan, column, size, buffer, sems):
    for j, (which, row, place, count) in enumerate(plan):
        pltpu.make_async_copy(
            refs[which].at[pl.ds(row, count), pl.ds(column, size)],
            buffer.at[pl.ds(place, count), :],
            sems.at[j],
        ).start()


def assemble_wait(refs, plan, column, size, buffer, sems):
    for j, (which, row, place, count) in enumerate(plan):
        pltpu.make_async_copy(
            refs[which].at[pl.ds(row, count), pl.ds(column, size)],
            buffer.at[pl.ds(place, count), :],
            sems.at[j],
        ).wait()


def project_kernel(qk_plan, vo_plan, ln_ref, bias_ref, c_ref, a_ref, b_ref, *rest):
    n = len({p[0] for p in qk_plan})
    qk_refs, vo_refs = rest[:n], rest[n : 2 * n]
    out_ref, w_ref, buffer, sems, out_sems = rest[2 * n :]
    kind = pl.program_id(0)
    heads = buffer.shape[2]
    sources = (
        (qk_refs, qk_plan, 0),
        (qk_refs, qk_plan, heads),
        (vo_refs, vo_plan, 0),
        (vo_refs, vo_plan, heads),
    )

    def drain(k):
        pltpu.make_async_copy(buffer.at[k % 2], w_ref.at[k], out_sems.at[k % 2]).wait()

    for k in range(4):
        refs, plan, column = sources[k]
        slot = k % 2

        @pl.when(kind == k)
        def _():
            if k == 0:
                assemble_start(refs, plan, column, heads, buffer.at[slot], sems.at[slot])
            assemble_wait(refs, plan, column, heads, buffer.at[slot], sems.at[slot])
            pltpu.make_async_copy(buffer.at[slot], w_ref.at[k], out_sems.at[slot]).start()
            if k >= 1:
                drain(k - 1)
            if k < 3:
                nrefs, nplan, ncolumn = sources[k + 1]
                assemble_start(
                    nrefs, nplan, ncolumn, heads, buffer.at[1 - slot], sems.at[1 - slot]
                )
            else:
                drain(k)

    @pl.when(kind < 3)
    def _():
        project_rows(kind, ln_ref, buffer[kind % 2], bias_ref, (c_ref, a_ref, b_ref), out_ref)


def project(ln, qk, vo, bias, tables):
    many, _, size, width = ln.shape
    heads = bias.shape[1]
    table = pl.BlockSpec((many, 1, size, PAIR), lambda i: (0, 0, 0, 0), pipeline_mode=once)
    hbm = pl.BlockSpec(memory_space=pl.ANY)
    last = lambda i: jnp.minimum(i, 2)
    return pl.pallas_call(
        functools.partial(project_kernel, qk[1], vo[1]),
        grid=(4,),
        in_specs=[
            pl.BlockSpec((many, 1, size, width), lambda i: (0, 0, 0, 0), pipeline_mode=once),
            pl.BlockSpec((1, 1, heads), lambda i: (last(i), 0, 0)),
            table,
            table,
            table,
        ]
        + [hbm] * (len(qk[0]) + len(vo[0])),
        out_specs=[
            pl.BlockSpec((1, many, 1, size, heads), lambda i: (last(i), 0, 0, 0, 0)),
            hbm,
        ],
        out_shape=[shape((3, many, 1, size, heads), bf16), shape((4, width, heads), bf16)],
        scratch_shapes=[
            pltpu.VMEM((2, width, heads), bf16),
            pltpu.SemaphoreType.DMA((2, len(qk[1]))),
            pltpu.SemaphoreType.DMA((2,)),
        ],
        compiler_params=params(48),
        cost_estimate=cost(6 * many * size * width * heads, 22 << 20),
        name="project",
    )(ln, bias[:, None, :], *tables, *qk[0], *vo[0])


def side_lanes(side):
    lane = lax.broadcasted_iota(jnp.int32, (1, PAIR), 1)
    return (lane // HEAD_DIM) == side


def masked_scores(keys, queries, first, length):
    scores = dot(keys, queries, NT)
    key = lax.broadcasted_iota(jnp.int32, scores.shape, 0)
    row = first + lax.broadcasted_iota(jnp.int32, (1, scores.shape[1]), 1)
    return jnp.where(key <= jnp.minimum(row, length - 1), scores, masked_score)


def attend_kernel(block, len_ref, q_ref, k_ref, v_ref, out_ref, total_ref, q_mine, v_turned):
    rows = q_ref.shape[1]
    zero = jnp.zeros((rows, PAIR), bf16)
    scale = jnp.asarray(1.0 / math.sqrt(HEAD_DIM), bf16)
    length = len_ref[0]
    for side in range(2):
        lanes = side_lanes(side)
        q_mine[side] = jnp.where(lanes, q_ref[0] * scale, zero)
    v_turned[...] = v_ref[0].T
    for first in range(0, rows, block):
        n = first + block
        r = slice(first, n)
        mixed = []
        for side in range(2):
            scores = masked_scores(k_ref[0, :n, :], q_mine[side, r, :], first, length)
            top = jnp.max(scores, 0, keepdims=True)
            exped = jnp.exp(scores - top)
            total = jnp.sum(exped, 0, keepdims=True)
            part = v_turned[side*HEAD_DIM:(side+1)*HEAD_DIM, :n]
            mixed.append(dot(part, exped.astype(bf16), NN) * (1.0 / total))
            total_ref[0, side:side+1, r] = top + jnp.log(total)
        out_ref[r, :] = jnp.concatenate(mixed, 0).T.astype(bf16)


def attend(qkv, length, block=512):
    _, rows, width = qkv.shape
    pairs = width // PAIR
    kind = lambda c: pl.BlockSpec((1, rows, PAIR), lambda h, n: (c, 0, h))
    return pl.pallas_call(functools.partial(attend_kernel, min(block, rows)),
        grid_spec=pltpu.PrefetchScalarGridSpec(num_scalar_prefetch=1, grid=(pairs,),
            in_specs=[kind(0), kind(1), kind(2)],
            out_specs=[pl.BlockSpec((rows, PAIR), lambda h, n: (0, h)), pl.BlockSpec((1, 2, rows), lambda h, n: (h, 0, 0))],
            scratch_shapes=[pltpu.VMEM((2, rows, PAIR), bf16), pltpu.VMEM((PAIR, rows), bf16)]),
        out_shape=[shape((rows, width), bf16), shape((pairs, 2, rows), f32)],
        compiler_params=params(48),
        cost_estimate=cost(16 * rows * rows * width, 4 << 20, rows * rows * 2 * pairs),
        name="attend")(length, qkv, qkv, qkv)


def attend_back_kernel(block, len_ref, q_ref, k_ref, v_ref, do_ref, total_ref, c_ref, a_ref, b_ref, grad_ref, q_mine, do_mine, k_turned, key_sum, value_sum):
    rows = q_ref.shape[1]
    zero = jnp.zeros((rows, PAIR), bf16)
    scale = 1.0 / math.sqrt(HEAD_DIM)
    for side in range(2):
        lanes = side_lanes(side)
        q_mine[side] = jnp.where(lanes, q_ref[0] * jnp.asarray(scale, bf16), zero)
        do_mine[side] = jnp.where(lanes, do_ref[...], zero)
    k_turned[...] = k_ref[0].T
    length = len_ref[0]
    tables_of = lambda r: (c_ref[r, :], a_ref[r, :], b_ref[r, :])
    for first in range(rows - block, -1, -block):
        n = first + block
        r = slice(first, n)
        gk = gv = None
        gq = []
        for side in range(2):
            scores = masked_scores(k_ref[0, :n, :], q_mine[side, r, :], first, length)
            probs = jnp.exp(scores - total_ref[0, side:side+1, r])
            grad_probs = dot(v_ref[0, :n, :], do_mine[side, r, :], NT)
            product = probs * grad_probs
            delta = jnp.sum(product, 0, keepdims=True)
            grad_scores = (product - probs * delta).astype(bf16)
            a = dot(grad_scores, q_mine[side, r, :], NN)
            b = dot(probs.astype(bf16), do_mine[side, r, :], NN)
            gk = a if gk is None else gk + a
            gv = b if gv is None else gv + b
            gq.append(dot(k_turned[side*HEAD_DIM:(side+1)*HEAD_DIM, :n], grad_scores, NN))
        if n == rows:
            key_sum[...] = gk
            value_sum[...] = gv
        else:
            key_sum[:n, :] += gk
            value_sum[:n, :] += gv
        grad_query = jnp.concatenate(gq, 0).T * scale
        grad_ref[0, r, :] = turned_back(grad_query, tables_of(r)).astype(bf16)
    for first in range(0, rows, block):
        r = slice(first, first + block)
        grad_ref[1, r, :] = turned_back(key_sum[r, :], tables_of(r)).astype(bf16)
        grad_ref[2, r, :] = value_sum[r, :].astype(bf16)


def attend_back(qkv, grad_mixed, totals, length, tables, block=512):
    _, rows, width = qkv.shape
    pairs = width // PAIR
    kind = lambda c: pl.BlockSpec((1, rows, PAIR), lambda h, n: (c, 0, h))
    table = pl.BlockSpec((rows, PAIR), lambda h, n: (0, 0))
    return pl.pallas_call(functools.partial(attend_back_kernel, min(block, rows)),
        grid_spec=pltpu.PrefetchScalarGridSpec(num_scalar_prefetch=1, grid=(pairs,),
            in_specs=[kind(0), kind(1), kind(2), pl.BlockSpec((rows, PAIR), lambda h, n: (0, h)), pl.BlockSpec((1, 2, rows), lambda h, n: (h, 0, 0)), table, table, table],
            out_specs=pl.BlockSpec((3, rows, PAIR), lambda h, n: (0, 0, h)),
            scratch_shapes=[pltpu.VMEM((2, rows, PAIR), bf16)]*2+[pltpu.VMEM((PAIR, rows), bf16)]+[pltpu.VMEM((rows, PAIR), f32)]*2),
        out_shape=shape((3, rows, width), bf16),
        compiler_params=params(48),
        cost_estimate=cost(40 * rows * rows * width, 8 << 20, rows * rows * 2 * pairs),
        name="attend_back")(length, qkv, qkv, qkv, grad_mixed, totals, *tables)


def feed_kernel(steps, late_steps, plan1, plan2, ln_ref, mixed_ref, wo_ref, bias_ref, *rest):
    n1 = len({p[0] for p in plan1})
    w1_refs, w2_refs = rest[:n1], rest[n1 : 2 * n1]
    (branch_ref, hidden_ref, slope_ref, full1_ref, full2_ref, held, buf1, buf2, sems1, sems2,
     out_sems) = rest[2 * n1 :]
    step = pl.program_id(0)
    slot = lax.rem(step, 2)
    tile_f = buf1.shape[2]
    tile_d = buf2.shape[1]
    c0 = math.sqrt(2.0 / math.pi)
    c1 = 0.044715
    plan2 = sorted(plan2, key=lambda p: p[2])
    per_tile = len(plan2) // late_steps

    def columns(s):
        return pl.ds(pl.multiple_of(s * tile_f, tile_f), tile_f)

    def start1(s):
        at = lax.rem(s, 2)
        column = pl.multiple_of(s * tile_f, tile_f)
        assemble_start(w1_refs, plan1, column, tile_f, buf1.at[at], sems1.at[at])

    def pieces2(tile):
        at = tile % 2
        for j, (which, row, place, count) in enumerate(plan2[tile * per_tile : (tile + 1) * per_tile]):
            yield pltpu.make_async_copy(
                w2_refs[which].at[pl.ds(row, count), :],
                buf2.at[at, pl.ds(place - tile * tile_d, count), :],
                sems2.at[at, j],
            )

    def out1(s, at):
        return pltpu.make_async_copy(buf1.at[at], full1_ref.at[:, columns(s)], out_sems.at[at])

    def out2(tile):
        return pltpu.make_async_copy(
            buf2.at[tile % 2], full2_ref.at[pl.ds(tile * tile_d, tile_d), :], out_sems.at[2 + tile % 2]
        )

    @pl.when(step == 0)
    def _():
        start1(0)
        for copy in pieces2(0):
            copy.start()

    @pl.when(step < steps)
    def _():
        column = pl.multiple_of(step * tile_f, tile_f)
        assemble_wait(w1_refs, plan1, column, tile_f, buf1.at[slot], sems1.at[slot])
        out1(step, slot).start()

        @pl.when(step > 0)
        def _():
            out1(step - 1, 1 - slot).wait()

        @pl.when(step < steps - 1)
        def _():
            start1(step + 1)

        pre = dot(ln_ref[...], buf1[slot], NN) + bias_ref[...]
        square = pre * pre
        bent = jnp.tanh(c0 * (pre + c1 * (square * pre)))
        half_pre = 0.5 * pre
        hidden = (half_pre * (1.0 + bent)).astype(bf16)
        hidden_ref[...] = hidden
        held[:, columns(step)] = hidden
        slope_ref[...] = 0.5 * (1.0 + bent) + half_pre * (1.0 - bent * bent) * (
            c0 * (1.0 + (3.0 * c1) * square)
        )

        @pl.when(step == steps - 1)
        def _():
            out1(step, slot).wait()

    for tile in range(late_steps):
        @pl.when(step == steps + tile)
        def _():
            for copy in pieces2(tile):
                copy.wait()
            out2(tile).start()
            if tile > 0:
                out2(tile - 1).wait()
            if tile < late_steps - 1:
                for copy in pieces2(tile + 1):
                    copy.start()
            total = dot(held[...], buf2[tile % 2], NT) + dot(mixed_ref[...], wo_ref[0], NT)
            branch_ref[...] = total.astype(bf16)
            if tile == late_steps - 1:
                out2(tile).wait()


def feed(ln, mixed, weights, w1, w2, bias, tile_f):
    rows, width = ln.shape
    hidden = bias.shape[1]
    heads = mixed.shape[1]
    steps = hidden // tile_f
    tile_d = 512
    late_steps = width // tile_d
    whole = lambda dims: pl.BlockSpec(dims, lambda i: (0, 0), pipeline_mode=once)
    early = lambda i: jnp.minimum(i, steps - 1)
    late = lambda i: jnp.maximum(i - steps, 0)
    by_row = pl.BlockSpec((rows, tile_f), lambda i: (0, early(i)))
    hbm = pl.BlockSpec(memory_space=pl.ANY)
    return pl.pallas_call(
        functools.partial(feed_kernel, steps, late_steps, w1[1], w2[1]),
        grid=(steps + late_steps,),
        in_specs=[
            whole((rows, width)),
            whole((rows, heads)),
            pl.BlockSpec((1, tile_d, heads), lambda i: (3, late(i), 0)),
            pl.BlockSpec((1, tile_f), lambda i: (0, early(i))),
        ]
        + [hbm] * (len(w1[0]) + len(w2[0])),
        out_specs=[
            pl.BlockSpec((rows, tile_d), lambda i: (0, late(i))), by_row, by_row, hbm, hbm
        ],
        out_shape=[
            shape((rows, width), bf16),
            shape((rows, hidden), bf16),
            shape((rows, hidden), f32),
            shape((width, hidden), bf16),
            shape((width, hidden), bf16),
        ],
        scratch_shapes=[
            pltpu.VMEM((rows, hidden), bf16),
            pltpu.VMEM((2, width, tile_f), bf16),
            pltpu.VMEM((2, tile_d, hidden), bf16),
            pltpu.SemaphoreType.DMA((2, len(w1[1]))),
            pltpu.SemaphoreType.DMA((2, len(w2[1]) // late_steps)),
            pltpu.SemaphoreType.DMA((4,)),
        ],
        compiler_params=params(58),
        cost_estimate=cost(4 * rows * width * hidden, 56 << 20, rows * hidden),
        name="feed",
    )(ln, mixed, weights, bias, *w1[0], *w2[0])


def back_kernel(steps, g_ref, w1_ref, w2_ref, slope_ref, wo_ref, sum_ref, pre_ref, mixed_ref, bias_ref, held):
    step = pl.program_id(0)
    tile = pre_ref.shape[1]

    @pl.when(step == 0)
    def _():
        mixed_ref[...] = dot(g_ref[...], wo_ref[0], NN).astype(bf16)

    @pl.when(step < steps)
    def _():
        grad = (dot(g_ref[...], w2_ref[...], NN) * slope_ref[...]).astype(bf16)
        pre_ref[...] = grad
        held[:, pl.ds(pl.multiple_of(step * tile, tile), tile)] = grad
        bias_ref[...] = jnp.sum(grad.astype(f32), axis=0, keepdims=True)

    @pl.when(step >= steps)
    def _():
        sum_ref[...] = dot(held[...], w1_ref[...], NT)


def back(grads, w1, w2, slope, weights, tile_f):
    rows, width = grads.shape
    units = slope.shape[1]
    heads = weights.shape[2]
    steps = units // tile_f
    tile_d = 512
    whole = lambda dims: pl.BlockSpec(dims, lambda i: (0, 0), pipeline_mode=once)
    early = lambda i: jnp.minimum(i, steps - 1)
    late = lambda i: jnp.maximum(i - steps, 0)
    by_row = pl.BlockSpec((rows, tile_f), lambda i: (0, early(i)))
    return pl.pallas_call(
        functools.partial(back_kernel, steps),
        grid=(steps + width // tile_d,),
        in_specs=[
            whole((rows, width)),
            pl.BlockSpec((tile_d, units), lambda i: (late(i), 0)),
            pl.BlockSpec((width, tile_f), lambda i: (0, early(i))),
            by_row,
            pl.BlockSpec((1, width, heads), lambda i: (3, 0, 0), pipeline_mode=once),
        ],
        out_specs=[
            pl.BlockSpec((rows, tile_d), lambda i: (0, late(i))),
            by_row,
            whole((rows, heads)),
            pl.BlockSpec((1, tile_f), lambda i: (0, early(i))),
        ],
        out_shape=[
            shape((rows, width), f32),
            shape((rows, units), bf16),
            shape((rows, heads), bf16),
            shape((1, units), f32),
        ],
        scratch_shapes=[pltpu.VMEM((rows, units), bf16)],
        compiler_params=params(58),
        cost_estimate=cost(4 * rows * width * units, 40 << 20),
        name="back",
    )(grads, w1, w2, slope, weights)


def feed_weight_kernel(left_ref, right_ref, near_ref, far_ref):
    half = left_ref.shape[1] // 2
    far_ref[...] = dot(left_ref[:, half:], right_ref[...], TN).astype(bf16)
    near_ref[...] = dot(left_ref[:, :half], right_ref[...], TN).astype(bf16)


def feed_weight(left, right, tile_f):
    rows, width = left.shape
    units = right.shape[1]
    half = pl.BlockSpec((width // 2, tile_f), lambda i: (0, i))
    return pl.pallas_call(
        feed_weight_kernel,
        grid=(units // tile_f,),
        in_specs=[
            pl.BlockSpec((rows, width), lambda i: (0, 0), pipeline_mode=once),
            pl.BlockSpec((rows, tile_f), lambda i: (0, i)),
        ],
        out_specs=[half, half],
        out_shape=[shape((width // 2, units), bf16)] * 2,
        compiler_params=params(48),
        cost_estimate=cost(2 * rows * width * units, 16 << 20),
        name="feed_weight",
    )(left, right)


def ln_grad_kernel(grad_ref, w_ref, sum_ref, out_ref):
    total = sum_ref[...]
    for kind in range(3):
        total += dot(grad_ref[kind], w_ref[kind], NT)
    out_ref[...] = total.astype(bf16)


def ln_grad(grad_qkv, weights, partial_sum):
    _, rows, heads = grad_qkv.shape
    width = partial_sum.shape[1]
    tile = 512
    return pl.pallas_call(
        ln_grad_kernel,
        grid=(width // tile,),
        in_specs=[
            pl.BlockSpec((3, rows, heads), lambda i: (0, 0, 0), pipeline_mode=once),
            pl.BlockSpec((3, tile, heads), lambda i: (0, i, 0)),
            pl.BlockSpec((rows, tile), lambda i: (0, i)),
        ],
        out_specs=pl.BlockSpec((rows, tile), lambda i: (0, i)),
        out_shape=shape((rows, width), bf16),
        compiler_params=params(48),
        cost_estimate=cost(6 * rows * width * heads, 22 << 20),
        name="ln_grad",
    )(grad_qkv, weights, partial_sum)


def weight_grad_kernel(ln_ref, g_ref, grad_ref, mixed_ref, kqk_ref, kvo_ref, sqk_ref, svo_ref, bias_ref):
    heads = mixed_ref.shape[1]
    step = pl.program_id(0)
    steps = pl.num_programs(0)
    for kind in range(3):
        @pl.when(step == 0)
        def _():
            bias_ref[kind] = jnp.sum(grad_ref[kind].astype(f32), axis=0, keepdims=True)

    for qk_ref, vo_ref, here in ((kqk_ref, kvo_ref, step < steps // 2), (sqk_ref, svo_ref, step >= steps // 2)):
        @pl.when(here)
        def _():
            qk_ref[:, :heads] = dot(ln_ref[...], grad_ref[0], TN).astype(bf16)
            qk_ref[:, heads:] = dot(ln_ref[...], grad_ref[1], TN).astype(bf16)
            vo_ref[:, :heads] = dot(ln_ref[...], grad_ref[2], TN).astype(bf16)
            vo_ref[:, heads:] = dot(g_ref[...], mixed_ref[...], TN).astype(bf16)


def weight_grad(ln, grads, grad_qkv, mixed):
    rows, width = ln.shape
    heads = mixed.shape[1]
    half = width // 2
    tile = min(512, half)
    near = half // tile
    column = pl.BlockSpec((rows, tile), lambda i: (0, i))
    kept = pl.BlockSpec((tile, 2 * heads), lambda i: (jnp.minimum(i, near - 1), 0))
    sent = pl.BlockSpec((tile, 2 * heads), lambda i: (jnp.maximum(i - near, 0), 0))
    return pl.pallas_call(
        weight_grad_kernel,
        grid=(2 * near,),
        in_specs=[
            column,
            column,
            pl.BlockSpec((3, rows, heads), lambda i: (0, 0, 0), pipeline_mode=once),
            pl.BlockSpec((rows, heads), lambda i: (0, 0), pipeline_mode=once),
        ],
        out_specs=[kept, kept, sent, sent, pl.BlockSpec((3, 1, heads), lambda i: (0, 0, 0))],
        out_shape=[shape((half, 2 * heads), bf16)] * 4 + [shape((3, 1, heads), f32)],
        compiler_params=params(48),
        cost_estimate=cost(8 * rows * width * heads, 20 << 20),
        name="weight_grad",
    )(ln, grads, grad_qkv, mixed)


def give_kernel(counts, *refs):
    outs = refs[sum(counts) :]
    start = 0
    for number, out_ref in zip(counts, outs):
        total = refs[start][...].astype(f32)
        for ref in refs[start + 1 : start + number]:
            total += ref[...].astype(f32)
        out_ref[...] = total.astype(bf16)
        start += number


def give(items, count):
    specs, operands, numbers, outs = [], [], [], []
    for full, arrivals, low, part in items:
        rows, width = full[0].shape[0], full[0].shape[1] // part[1]
        block = rows // count
        level = len(arrivals) + 1
        out_count = count >> level
        place = (lambda i: (2 * i + 1) << (level - 1)) if low else (lambda i: out_count + i)
        for k in range(level):
            for array in full if k == 0 else [arrivals[k - 1]]:
                off = part[0] if k == 0 else 0
                specs.append(
                    pl.BlockSpec(
                        (block, width),
                        lambda i, k=k, off=off, low=low, place=place: (
                            place(i) >> k if low else place(i),
                            off,
                        ),
                    )
                )
                operands.append(array)
        numbers.append(len(full) + level - 1)
        outs.append(shape((out_count * block, width), bf16))
    moved = sum(o.shape[0] * o.shape[1] for o in outs)
    return pl.pallas_call(
        functools.partial(give_kernel, tuple(numbers)),
        grid=(out_count,),
        in_specs=specs,
        out_specs=[pl.BlockSpec((block, o.shape[1]), lambda i: (i, 0)) for o in outs],
        out_shape=outs,
        compiler_params=params(32),
        cost_estimate=cost(moved * 2, 6 * moved),
        name="give",
    )(*operands)


def norm_back_kernel(
    blocks, at_ref, sum_ref, rows_ref, cot_ref, gain_ref, first_ref, second_ref, vector_ref, held
):
    wide = rows_ref.shape[1] // blocks
    bits = blocks.bit_length() - 1
    for q in range(blocks):
        place = pl.multiple_of(reversed_bits(at_ref[1] ^ q, bits) * wide, wide)
        held[:, q * wide : (q + 1) * wide] = sum_ref[:, pl.ds(place, wide)]
    grad_ln = held[...].astype(f32)
    rows = rows_ref[...].astype(f32)
    centred = rows - jnp.mean(rows, -1, keepdims=True)
    inv_scale = lax.rsqrt(jnp.mean(centred * centred, -1, keepdims=True) + eps)
    normed = centred * inv_scale
    grad_norm = grad_ln * gain_ref[...]
    back = inv_scale * (
        grad_norm
        - jnp.mean(grad_norm, -1, keepdims=True)
        - normed * jnp.mean(grad_norm * normed, -1, keepdims=True)
    )
    slot = (cot_ref[...].astype(f32) + back).astype(bf16)
    gain_sum = jnp.sum(grad_ln * normed, 0, keepdims=True)
    shift_sum = jnp.sum(grad_ln, 0, keepdims=True)

    @pl.when(pl.program_id(0) == 0)
    def _():
        first_ref[...] = slot
        vector_ref[0:1] = gain_sum
        vector_ref[1:2] = shift_sum

    @pl.when(pl.program_id(0) == 1)
    def _():
        second_ref[...] = slot
        vector_ref[0:1] += gain_sum
        vector_ref[1:2] += shift_sum


def norm_back(total, rows_in, cot, gain, at, blocks):
    rows, width = rows_in.shape
    whole = pl.BlockSpec((rows // 2, width), lambda i, n: (i, 0))
    vector = pl.BlockSpec((1, width), lambda i, n: (0, 0))
    return pl.pallas_call(
        functools.partial(norm_back_kernel, blocks),
        grid_spec=pltpu.PrefetchScalarGridSpec(
            num_scalar_prefetch=1,
            grid=(2,),
            in_specs=[whole, whole, whole, vector],
            out_specs=[pl.BlockSpec((rows // 2, width), lambda i, n: (0, 0))] * 2
            + [pl.BlockSpec((2, width), lambda i, n: (0, 0))],
            scratch_shapes=[pltpu.VMEM((rows // 2, width), bf16)],
        ),
        out_shape=[shape((rows // 2, width), bf16)] * 2 + [shape((2, width), f32)],
        compiler_params=params(32),
        cost_estimate=cost(20 * rows * width, 8 * rows * width),
        name="norm_back",
    )(at, total, rows_in, cot, gain)


def final_kernel(parts, levels, *refs):
    full, rest, out_ref = refs[:2], refs[2:-1], refs[-1]
    base = full[0][...].astype(f32) + full[1][...].astype(f32)
    for part in range(parts):
        @pl.when(pl.program_id(0) == part)
        def _():
            total = base
            for ref in rest[part * levels : (part + 1) * levels]:
                total += ref[...].astype(f32)
            out_ref[...] = total


def final(full, sums, block):
    parts, levels = len(sums), len(sums[0])
    width = full[0].shape[1]
    wide = width // parts
    piece = pl.BlockSpec((block, wide), lambda i: (0, i))
    held = pl.BlockSpec((block, wide), lambda i: (0, 0))
    return pl.pallas_call(
        functools.partial(final_kernel, parts, levels),
        grid=(parts,),
        in_specs=[piece, piece] + [held] * (parts * levels),
        out_specs=piece,
        out_shape=shape((block, width), f32),
        compiler_params=params(32),
        cost_estimate=cost(4 * block * width, 12 * block * width),
        name="final",
    )(*full, *[f for s in sums for f in s])


def finish_kernel(blocks, at_ref, sum_ref, rows_ref, bias_a_ref, bias_b_ref, out_ref, held):
    rows, width = rows_ref.shape
    wide = width // blocks
    bits = blocks.bit_length() - 1
    for q in range(blocks):
        place = pl.multiple_of(reversed_bits(at_ref[1] ^ q, bits) * wide, wide)
        held[:, q * wide : (q + 1) * wide] = sum_ref[:, pl.ds(place, wide)]
    branch = held[...].astype(f32) + bias_a_ref[...] + bias_b_ref[...]
    position = at_ref[0] * rows + lax.broadcasted_iota(jnp.int32, (rows, 1), 0)
    branch = jnp.where(position < at_ref[2], branch, 0.0)
    out_ref[...] = (rows_ref[...].astype(f32) + branch).astype(bf16)


def finish(branch_sum, rows_in, bias_a, bias_b, at, blocks):
    rows, width = rows_in.shape
    whole = pl.BlockSpec((rows, width), lambda i, n: (0, 0))
    vector = pl.BlockSpec((1, width), lambda i, n: (0, 0))
    return pl.pallas_call(
        functools.partial(finish_kernel, blocks),
        grid_spec=pltpu.PrefetchScalarGridSpec(
            num_scalar_prefetch=1,
            grid=(1,),
            in_specs=[whole, whole, vector, vector],
            out_specs=whole,
            scratch_shapes=[pltpu.VMEM((rows, width), bf16)],
        ),
        out_shape=shape((rows, width), bf16),
        compiler_params=params(32),
        cost_estimate=cost(8 * rows * width, 6 * rows * width),
        name="finish",
    )(at, branch_sum, rows_in, bias_a, bias_b)


def final_attention_kernel(levels, *refs):
    heads = refs[0].shape[1] // 2
    grad_ref, out_ref = refs[-2:]
    totals = []
    for start in (0, levels + 2):
        total = refs[start][...].astype(f32)
        for ref in refs[start + 1 : start + levels + 2]:
            total += ref[...].astype(f32)
        totals.append(total)
    grad_ref[0] = totals[0][:, :heads]
    grad_ref[1] = totals[0][:, heads:]
    grad_ref[2] = totals[1][:, :heads]
    out_ref[...] = totals[1][:, heads:]


def final_attention(qk, vo, block):
    levels = len(qk) - 2
    width = qk[0].shape[1]
    piece = pl.BlockSpec((block, width), lambda i: (0, 0))
    return pl.pallas_call(
        functools.partial(final_attention_kernel, levels),
        grid=(1,),
        in_specs=[piece] * (2 * levels + 4),
        out_specs=[
            pl.BlockSpec((3, block, width // 2), lambda i: (0, 0, 0)),
            pl.BlockSpec((block, width // 2), lambda i: (0, 0)),
        ],
        out_shape=[shape((3, block, width // 2), f32), shape((block, width // 2), f32)],
        compiler_params=params(32),
        cost_estimate=cost(8 * block * width, 24 * block * width),
        name="final_attention",
    )(*qk, *vo)


def rotary_tables(rows, col_count):
    half_rot = ROT // 2
    column = jnp.arange(col_count) % HEAD_DIM
    exponent = (2 * (column % half_rot)).astype(jnp.float32) / ROT
    frequency = jnp.exp(-math.log(10000.0) * exponent)
    angles = rows.astype(jnp.float32)[:, None] * frequency[None, :]
    inside = column < ROT
    cosine = jnp.where(inside, jnp.cos(angles), 1.0)
    sine_part = jnp.sin(angles)
    ahead_sin = jnp.where(column < half_rot, -sine_part, 0.0)
    behind_sin = jnp.where(inside & (column >= half_rot), sine_part, 0.0)
    return (cosine, ahead_sin, behind_sin)


def flip(array, axis_name, bit):
    size = lax.axis_size(axis_name)
    return lax.ppermute(array, axis_name, [(i, i ^ (1 << bit)) for i in range(size)])


def bits_of(size):
    return size.bit_length() - 1


def swap_blocks(array, index, axis, blocks):
    for bit in range(bits_of(blocks)):
        dims = array.shape
        parts = dims[:axis] + (blocks >> (bit + 1), 2, 1 << bit, dims[axis] // blocks)
        view = array.reshape(parts + dims[axis + 1 :])
        other = jnp.flip(view, axis=axis + 1)
        array = jnp.where((index >> bit) & 1 == 1, other, view).reshape(dims)
    return array


def reversed_bits(value, bits):
    return sum(((value >> k) & 1) << (bits - 1 - k) for k in range(bits))


def xor_columns(array, index, blocks):
    width = array.shape[-1] // blocks
    bits = bits_of(blocks)
    pieces = [
        lax.dynamic_slice_in_dim(
            array, (index ^ reversed_bits(p, bits)) * width, width, array.ndim - 1
        )
        for p in range(blocks)
    ]
    return jnp.concatenate(pieces, -1)


def plain_columns(array, index, blocks):
    width = array.shape[-1] // blocks
    bits = bits_of(blocks)
    pieces = []
    for q in range(blocks):
        place = reversed_bits(index ^ q, bits)
        pieces.append(lax.dynamic_slice_in_dim(array, place * width, width, array.ndim - 1))
    return jnp.concatenate(pieces, -1)


def gather_step(stacks, bit):
    return stacks + [(flip(rows, "dp", bit), [m | (1 << bit) for m in masks]) for rows, masks in stacks]


def joined_step(stacks, bit):
    rows = jnp.concatenate([s[0] for s in stacks], 0)
    return stacks + [(flip(rows, "dp", bit), [m | (1 << bit) for s in stacks for m in s[1]])]


def gather_plan(stacks, block, bits):
    plan = []
    for which, (_, masks) in enumerate(stacks):
        for i, m in enumerate(masks):
            plan.append((which, i * block, reversed_bits(m, bits) * block, block))
    return [s[0] for s in stacks], tuple(plan)


def core_copies(stacks):
    return [(flip(rows, "dp", 0), [m | 1 for m in masks]) for rows, masks in stacks]


def route_order(last):
    return [b for b in range(bits_of(lax.axis_size("dp")) - 1, -1, -1) if b != last]


def route_first(block, last):
    return jnp.stack([block, flip(block, "dp", route_order(last)[0])], 0)


def route_more(stack, last):
    order = route_order(last)[1:]
    for bit in order[:-1]:
        stack = jnp.concatenate([stack, flip(stack, "dp", bit)], 0)
    return (stack, flip(stack, "dp", order[-1]))


def route_picks(halves, wanted, index, last):
    order = route_order(last)
    count = halves[0].shape[0]

    def pick(want):
        mask = index ^ want
        at = sum(((mask >> bit) & 1) << k for k, bit in enumerate(order))
        found = [lax.dynamic_index_in_dim(h, at % count, 0, keepdims=False) for h in halves]
        return found[0] if len(found) == 1 else jnp.where(at < count, found[0], found[1])

    return pick(wanted[index ^ (1 << last)]), pick(wanted[index])


def route_end(given, held, wanted, index, last):
    arrived = flip(given, "dp", last)
    return jnp.where(((index ^ wanted[index]) >> last) & 1 == 1, arrived, held)


def gather_small(stack, axis_name):
    for bit in range(bits_of(lax.axis_size(axis_name))):
        stack = jnp.concatenate([stack, flip(stack, axis_name, bit)], 0)
    return stack


def scatter_along(stack, axis_name):
    bits = bits_of(lax.axis_size(axis_name))
    stack = stack.reshape((2,) * bits + stack.shape[1:])
    stack = stack.transpose(tuple(range(bits - 1, -1, -1)) + tuple(range(bits, stack.ndim)))
    for bit in range(bits):
        stack = stack[0] + flip(stack[1], axis_name, bit)
    return stack


def after(values, *others):
    held = lax.optimization_barrier((tuple(values), tuple(others)))
    return held[0]


def shards(
    hidden_in,
    cotangent,
    lengths,
    slot_of_seq,
    seq_of_slot,
    qkv_weight,
    out_weight,
    fc1_weight,
    fc2_weight,
    ln_gain,
    ln_bias,
    qkv_bias,
    out_bias,
    fc1_bias,
    fc2_bias,
):
    rows_here = hidden_in.shape[1]
    width = hidden_in.shape[2]
    tensor_count = lax.axis_size("tensor")
    data_count = lax.axis_size("dp")
    tensor_index = lax.axis_index("tensor")
    data_index = lax.axis_index("dp")
    seq_len = rows_here * tensor_count
    heads_local = qkv_weight.shape[2]
    hidden_local = fc1_weight.shape[1]
    block = width // data_count
    length = lengths[seq_of_slot[data_index]]
    bits = bits_of(data_count)
    x_first = list(range(1, bits))
    y_first = x_first[::-1]
    tile_f = min(512, hidden_local)

    lasts = (bits - 1, bits - 2)
    wave_rows = rows_here // 2
    at = jnp.stack([tensor_index, data_index, length]).astype(jnp.int32)

    def send(parts):
        return [route_first(h, last) for h, last in zip(parts, lasts)]

    def picks_of(stacks, wanted):
        return [route_picks(f, wanted, data_index, last) for f, last in zip(stacks, lasts)]

    def route_ends(picks, wanted):
        return jnp.concatenate(
            [route_end(g, k, wanted, data_index, last) for (g, k), last in zip(picks, lasts)], 0
        )

    def receive(firsts, wanted):
        stacks = [route_more(f, last) for f, last in zip(firsts, lasts)]
        stacks = [(jnp.concatenate(halves, 0),) for halves in stacks]
        return route_ends(picks_of(stacks, wanted), wanted)

    firsts = send((hidden_in[0, :wave_rows], hidden_in[0, wave_rows:]))
    vectors = [ln_gain, ln_bias, out_bias, fc2_bias, qkv_bias, fc1_bias]
    s = ln_gain.shape[0]
    vectors = after(vectors, *firsts)
    small = jnp.concatenate([v.reshape(-1, s) for v in vectors], 0)
    stack = gather_small(small[None], "tensor")
    routed = receive(firsts, seq_of_slot)
    routed, stack = after((routed, stack))
    extra_rows = 16
    full = lax.all_gather(routed, "tensor", axis=0, tiled=True)

    stack = swap_blocks(stack, tensor_index, 0, tensor_count).reshape(-1)
    extra = jnp.pad(stack, (0, extra_rows * 2 * heads_local - stack.shape[0]))
    qk_shard = jnp.concatenate(
        [qkv_weight[:, :2].reshape(block, 2 * heads_local), extra.reshape(extra_rows, 2 * heads_local)], 0
    )
    vo_shard = jnp.concatenate([qkv_weight[:, 2], out_weight], 1)
    qk_shard, vo_shard = after((qk_shard, vo_shard), routed)
    qk_stacks = gather_step([(qk_shard, [0])], x_first[0])
    vo_stacks = gather_step([(vo_shard, [0])], y_first[0])
    first_qk, first_vo, fc1_shard, fc2_shard = after(
        (qk_stacks[1][0], vo_stacks[1][0], fc1_weight, fc2_weight)
    )
    qk_stacks[1], vo_stacks[1] = (first_qk, qk_stacks[1][1]), (first_vo, vo_stacks[1][1])
    for step in range(1, len(x_first)):
        qk_stacks = gather_step(qk_stacks, x_first[step])
        vo_stacks = gather_step(vo_stacks, y_first[step])

    def held_back(groups, *values):
        flat = [rows for stacks in groups for rows, _ in stacks]
        out = list(after(tuple(flat) + values))
        fresh = [[(out.pop(0), masks) for _, masks in stacks] for stacks in groups]
        return fresh, out

    row_ids, = after((jnp.arange(seq_len, dtype=jnp.int32),), qk_shard)
    tables = rotary_tables(row_ids, PAIR)
    (qk_stacks, vo_stacks), tables = held_back((qk_stacks, vo_stacks), *tables)
    qk_stacks = qk_stacks + core_copies(qk_stacks)
    qk = gather_plan(qk_stacks, block, bits)
    by_mask = sorted(qk_stacks, key=lambda st: st[1][0])
    gathered = jnp.stack([rows[block:].reshape(-1)[: stack.shape[0]] for rows, _ in by_mask], 0)
    gathered = swap_blocks(gathered, data_index, 0, data_count)
    gathered = gathered.reshape(data_count, tensor_count, -1)
    vo = gather_plan(vo_stacks + core_copies(vo_stacks), block, bits)
    fc1_stacks = gather_step([(fc1_shard, [0])], x_first[0])
    fc2_stacks = gather_step([(fc2_shard, [0])], y_first[0])

    positions = tensor_index * rows_here + jnp.arange(rows_here, dtype=jnp.int32)
    valid = (positions < length)[:, None]
    cot_rows = cotangent[0]
    low_plain = jnp.where(valid, cot_rows, jnp.zeros_like(cot_rows))
    low, = after((low_plain,), routed)
    low = xor_columns(low, data_index, data_count)
    grads = lax.all_gather(low, "tensor", axis=0, tiled=True)

    gain, shift, bias_a, bias_b = [
        gathered[:, :, i * s : (i + 1) * s].reshape(1, width).astype(f32) for i in range(4)
    ]
    q = qkv_bias.shape[0]
    bias_qkv = lax.dynamic_slice_in_dim(
        gathered[:, :, 4 * s : 4 * s + q].reshape(3, width), tensor_index * heads_local, heads_local, 1
    ).astype(f32)
    bias_fc1 = lax.dynamic_slice_in_dim(
        gathered[:, :, 4 * s + q :].reshape(1, hidden_local * tensor_count),
        tensor_index * hidden_local,
        hidden_local,
        1,
    ).astype(f32)

    row_tables = [v.reshape(tensor_count, 1, rows_here, PAIR) for v in tables]
    size = length.reshape(1)
    (fc1_stacks, fc2_stacks), (gain, shift) = held_back((fc1_stacks, fc2_stacks), gain, shift)
    fc1_far, fc2_far = core_copies(fc1_stacks), core_copies(fc2_stacks)
    for step in range(1, len(x_first)):
        fc1_stacks = joined_step(fc1_stacks, x_first[step])
        fc2_stacks = joined_step(fc2_stacks, y_first[step])
    ln = norm(full, tensor_count, at, gain, shift, data_count)
    (fc1_far, fc2_far), (ln,) = held_back((fc1_far, fc2_far), ln)
    qkv, weights = project(ln, qk, vo, bias_qkv, row_tables)
    ln, qkv = ln.reshape(seq_len, width), qkv.reshape(3, seq_len, heads_local)
    mixed, totals = attend(qkv, size)
    (fc1_stacks, fc2_stacks), (mixed,) = held_back((fc1_stacks, fc2_stacks), mixed)
    fc1_far = fc1_far + core_copies(fc1_stacks[2:])
    fc2_far = fc2_far + core_copies(fc2_stacks[2:])
    w1 = gather_plan(fc1_stacks + fc1_far, block, bits)
    w2 = gather_plan(fc2_stacks + fc2_far, block, bits)
    branch, hidden, slope, full1, full2 = feed(ln, mixed, weights, w1, w2, bias_fc1, tile_f)
    branch, grads = after((branch, grads))
    branch = lax.psum_scatter(branch, "tensor", scatter_dimension=0, tiled=True)

    count = data_count // 2
    steps = len(x_first)
    feed_sum, grad_pre, grad_mixed, grad_fc1_b = back(grads, full1, full2, slope, weights, tile_f)
    hidden, = after((hidden,), grad_pre)
    k2, s2 = feed_weight(grads, hidden, tile_f)
    c2 = flip(s2, "dp", 0)
    grad_pre, = after((grad_pre,), s2)
    k1, s1 = feed_weight(ln, grad_pre, tile_f)
    c1 = flip(s1, "dp", 0)

    pair = ((0, 2), (1, 2))
    both = (x_first, y_first)

    def gives_of(full, sums):
        return give([(full, s, low, p) for s, low, p in zip(sums, (False, True), pair)], count)

    def send_on(gives, step):
        return [flip(g, "dp", order[step]) for g, order in zip(gives, both)]

    k2, c2 = after((k2, c2), s1)
    gives2 = gives_of([k2, c2], ([], []))
    sums2 = [[f] for f in send_on(gives2, 0)]
    k1, c1 = after((k1, c1), *gives2)
    gives1 = gives_of([k1, c1], ([], []))
    sums1 = [[f] for f in send_on(gives1, 0)]
    grad_mixed, = after((grad_mixed,), *gives1)
    grad_qkv = attend_back(qkv, grad_mixed, totals, size, tables)
    kqk, kvo, sqk, svo, grad_qkv_b = weight_grad(ln, grads, grad_qkv, mixed)
    cq, cv = flip(sqk, "dp", 0), flip(svo, "dp", 0)
    grad_qkv, branch, sums2, sums1 = after((grad_qkv, branch, sums2, sums1), sqk)
    ln_part = ln_grad(grad_qkv, weights, feed_sum)
    total = lax.psum_scatter(ln_part, "tensor", scatter_dimension=0, tiled=True)
    kqk, kvo, cq, cv = after((kqk, kvo, cq, cv), ln_part)
    giveq, givev = give(
        [([kqk, cq], [], False, (0, 1)), ([kvo, cv], [], True, (0, 1))], count
    )
    sumsq, sumsv = [flip(giveq, "dp", x_first[0])], [flip(givev, "dp", y_first[0])]
    k2, = after((k2,), giveq, givev)
    for step in range(1, steps):
        gives2 = gives_of([k2, c2], sums2)
        sums2 = [s + [f] for s, f in zip(sums2, send_on(gives2, step))]
    k1, = after((k1,), *gives2)
    for step in range(1, steps):
        gives1 = gives_of([k1, c1], sums1)
        sums1 = [s + [f] for s, f in zip(sums1, send_on(gives1, step))]
    branch, = after((branch,), *gives1)
    block_out = finish(branch, routed, bias_a, bias_b, at, data_count)[None]
    grad_bias = jnp.sum(low_plain.astype(f32), axis=0)
    devices = data_count * tensor_count
    full_qkv_b = lax.dynamic_update_slice_in_dim(
        jnp.zeros((3, width), f32), grad_qkv_b[:, 0], tensor_index * heads_local, 1
    )
    full_fc1_b = lax.dynamic_update_slice_in_dim(
        jnp.zeros((hidden_local * tensor_count,), f32), grad_fc1_b[0], tensor_index * hidden_local, 0
    )
    known = jnp.concatenate(
        [grad_bias.reshape(devices, s), full_qkv_b.reshape(devices, q), full_fc1_b.reshape(devices, -1)],
        1,
    )
    kqk, kvo, sumsq, sumsv = after((kqk, kvo, sumsq, sumsv), block_out)
    for step in range(1, steps):
        giveq, givev = give(
            [([kqk, cq], sumsq, False, (0, 1)), ([kvo, cv], sumsv, True, (0, 1))], count
        )
        sumsq = sumsq + [flip(giveq, "dp", x_first[step])]
        sumsv = sumsv + [flip(givev, "dp", y_first[step])]
    k2, k1, sums2, sums1 = after((k2, k1, sums2, sums1), giveq, givev)
    grad_fc2_w, grad_fc1_w = final([k2, c2], sums2, block), final([k1, c1], sums1, block)
    sumsq, sumsv = after((sumsq, sumsv), grad_fc2_w, grad_fc1_w)
    grad_qkv_w, grad_out_w = final_attention([kqk, cq] + sumsq, [kvo, cv] + sumsv, block)
    grad_qkv_w = grad_qkv_w.swapaxes(0, 1)
    total, known = after((total, known), grad_out_w)
    *slot, vector_sums = norm_back(total, routed, cotangent[0], gain, at, data_count)
    firsts = send(slot)
    vector_sums = vector_sums.reshape(2, devices, s)
    sums = jnp.concatenate([vector_sums[0], vector_sums[1], known], 1)
    sums = swap_blocks(sums, data_index * tensor_count + tensor_index, 0, devices)
    sums = sums.reshape(data_count, tensor_count, -1).swapaxes(0, 1)
    sums = scatter_along(sums, "tensor")
    firsts, sums = after((firsts, sums))
    stacks = [route_more(f, last) for f, last in zip(firsts, lasts)]
    picks = picks_of(stacks, slot_of_seq)
    picks, sums = after((picks, sums))
    grad_input = route_ends(picks, slot_of_seq)[None]
    total = scatter_along(sums, "dp")
    return (
        block_out,
        grad_input,
        grad_qkv_w,
        grad_out_w,
        grad_fc1_w,
        grad_fc2_w,
        total[:s],
        total[s : 2 * s],
        total[3 * s : 3 * s + q],
        total[2 * s : 3 * s],
        total[3 * s + q :],
        total[2 * s : 3 * s],
    )


def solution(mesh):
    in_specs = (
        P("dp", "tensor", None),
        P("dp", "tensor", None),
        P(),
        P(),
        P(),
        P("dp", None, "tensor"),
        P("dp", "tensor"),
        P("dp", "tensor"),
        P("dp", "tensor"),
        P(("dp", "tensor")),
        P(("dp", "tensor")),
        P(("dp", "tensor")),
        P(("dp", "tensor")),
        P(("dp", "tensor")),
        P(("dp", "tensor")),
    )
    out_specs = (
        P("dp", "tensor", None),
        P("dp", "tensor", None),
        P("dp", None, "tensor"),
        P("dp", "tensor"),
        P("dp", "tensor"),
        P("dp", "tensor"),
        P(("dp", "tensor")),
        P(("dp", "tensor")),
        P(("dp", "tensor")),
        P(("dp", "tensor")),
        P(("dp", "tensor")),
        P(("dp", "tensor")),
    )
    return jax.shard_map(shards, mesh=mesh, in_specs=in_specs, out_specs=out_specs, check_vma=False)
```
